32 devices in a mesh: seq: 16 (over z, x, core), shard: 2 (over y).
Axes of the slice: x: 2, y: 2, z: 4, core: 2. Of those that a mesh axis runs over, the one named last changes fastest.
Arguments:
- x_embed: bfloat16 [2, 8192, 768], P('shard', 'seq'), may hold values from -9 to 9
- doc_ids: int32 [2, 8192], P('shard', 'seq'), may hold values from 0 to 3, never falling along the last dimension, each value on 1 to 4096 neighbouring positions
- owners: int32 [2, 8192, 2], P('shard', 'seq'), may hold values from 0 to 31, all different within a row; in each aligned block of 512 rows (0 to 511, 512 to 1023, ..., all dimensions but the last counted through in order) at most 64 rows name the same one
- row_ids: int32 [2, 8192, 2], P('shard', 'seq'), may hold values from 0 to 24999
- table: bfloat16 [800000, 192], P(('seq', 'shard')), may hold values from -6 to 6
- ngram_weight: bfloat16 [384, 768], P('shard'), may hold values from -0.3125 to 0.3125
- stream_gain: bfloat16 [768], P('shard'), may hold values from 0.5 to 1.5
- query_weight: bfloat16 [768, 768], P('shard'), may hold values from -0.21875 to 0.21875
- key_weight: bfloat16 [768, 768], P('shard'), may hold values from -0.21875 to 0.21875
- value_weight: bfloat16 [768, 768], P('shard'), may hold values from -0.21875 to 0.21875
- out_weight: bfloat16 [768, 768], P('shard'), may hold values from -1.75 to 1.75
- mixer_gain: bfloat16 [768], P('shard'), may hold values from 0.5 to 1.5
- gate_weight: bfloat16 [768, 2048], P('shard'), may hold values from -0.21875 to 0.21875
- up_weight: bfloat16 [768, 2048], P('shard'), may hold values from -0.21875 to 0.21875
- down_weight: bfloat16 [2048, 768], P('shard'), may hold values from -0.25 to 0.25
- feed_gain: bfloat16 [768], P('shard'), may hold values from 0.5 to 1.5
- cotangent: bfloat16 [2, 8192, 768], P('shard', 'seq'), may hold values from -6 to 6
Outputs:
- mixed: bfloat16 [2, 8192, 768], P('shard', 'seq')
- grad_input: float32 [2, 8192, 768], P('shard', 'seq')
- stream_rms: float32 [], replicated
- mixer_rms: float32 [], replicated
- feed_rms: float32 [], replicated
- grad_table: float32 [800000, 192], P(('seq', 'shard'))
- grad_ngram: float32 [384, 768], P('shard')
- grad_stream_gain: float32 [768], P('shard')
- grad_query: float32 [768, 768], P('shard')
- grad_key: float32 [768, 768], P('shard')
- grad_value: float32 [768, 768], P('shard')
- grad_out: float32 [768, 768], P('shard')
- grad_mixer_gain: float32 [768], P('shard')
- grad_gate: float32 [768, 2048], P('shard')
- grad_up: float32 [768, 2048], P('shard')
- grad_down: float32 [2048, 768], P('shard')
- grad_feed_gain: float32 [768], P('shard')
The draws below stay inside these ranges and needn't reach their ends.
Inputs may be any that keep to these rules, and one draw needn't show every extreme that they name: `owners`: the two shards named by one token differ; among the ids of one device's tokens no shard is named more than 64 times. `doc_ids`: along a sequence the document numbers never fall; each document covers 1 to 4096 tokens, and one covers exactly 4096.
All inputs are finite; a program needn't handle non-finite values.
Results may differ from the reference program's by a relative error of at most 0.019.
Values may be sent and summed in bfloat16 or wider, within the bound.
A program may use at most 192 MiB of HBM per device.

```python
import math
import jax
import jax.numpy as jnp
import numpy as np
from jax import lax

D = 768
HEADS = 12
HEAD_DIM = 64
FF = 2048
ROW_WIDTH = 192
ROWS_DEV = 25000
TOK_DEV = 512
SEQS = 2
LEN = 8192
DOCLEN = 4096
DOCS = 4
CAP = 64
TABLE_ROWS = 800000
DEVICES = 32


def draw_x_embed(key, part):
    places = jnp.arange(LEN, dtype=jnp.float32) / LEN
    base = jnp.clip(jax.random.normal(key, (SEQS, LEN, D), jnp.float32), -6.0, 6.0)
    scale_row = 0.5 + places
    return (base * scale_row[None, :, None]).astype(jnp.bfloat16)


def with_ends(drawn, own_key, smallest, top_value):
    spot = [jax.random.randint(jax.random.fold_in(own_key, axis), (), 0, length) for axis, length in enumerate(drawn.shape)]
    widest = drawn.shape.index(max(drawn.shape))
    neighbour = spot[:widest] + [(spot[widest] + 1) % drawn.shape[widest]] + spot[widest + 1:]
    return drawn.at[tuple(spot)].set(smallest).at[tuple(neighbour)].set(top_value)


def block_levels(rng, dims, cuts, low, high):
    gain, own = 1.0, jax.random.fold_in(rng, 6)
    for axis_at, parts in cuts:
        heights = jnp.exp(jax.random.uniform(jax.random.fold_in(own, axis_at), (parts,), jnp.float32, low / len(cuts), high / len(cuts)))
        gain = gain * jnp.repeat(heights, dims[axis_at] // parts).reshape([-1 if axis == axis_at else 1 for axis in range(len(dims))])
    return gain


def length_profile(number_of, total, reach, lean):
    portions = [(1 << 20) // math.isqrt(rank ** lean) + 1 for rank in range(2, number_of + 1)]
    surplus, holding = total - reach - (number_of - 1), [1] * (number_of - 1)
    while surplus > 0:
        candidates = [i for i in range(number_of - 1) if holding[i] < reach]
        mass, remaining = sum([portions[i] for i in candidates]), surplus
        for i in candidates:
            addition = min(reach - holding[i], max(1, remaining * portions[i] // mass), surplus)
            holding[i] = holding[i] + addition
            surplus = surplus - addition
    return np.array([reach] + holding)


def ragged_sizes(rng, count, total, most, slope):
    if count == 2:
        one = jax.random.randint(rng, (), max(1, total - most), min(most, total - 1) + 1)
        return jnp.stack([one, total - one])
    lengths = jnp.asarray(length_profile(count, total, most, slope), jnp.int32)
    couples = (count - 1) // 2
    giver, taker = lengths[1:1 + 2 * couples:2], lengths[2:2 + 2 * couples:2]
    room = jnp.minimum(giver - 1, most - taker)
    shifted = jax.random.randint(jax.random.fold_in(rng, 1), (couples,), 0, 1 << 20) % (room + 1)
    lengths = lengths.at[1:1 + 2 * couples:2].set(giver - shifted).at[2:2 + 2 * couples:2].set(taker + shifted)
    return lengths[jax.random.permutation(jax.random.fold_in(rng, 2), count)]


def assign_block(rng, own, number, rows, count, top, reach, lean):
    order = jax.random.permutation(rng, count)
    heavy_load, ordinary = portions_of(count, rows * top, reach, lean, True), portions_of(count, rows * top, reach, lean, False)
    places = jnp.arange(count)

    def named(lengths, rotation):
        used = int((lengths > 0).sum())
        fixed = max(1, used // 4)
        shifted = fixed + (places - fixed + rotation * (used - fixed)) % max(1, count - fixed)
        return jnp.zeros((count,), jnp.int32).at[order[jnp.where(places < fixed, places, shifted)]].set(jnp.asarray(lengths, jnp.int32))

    lengths = jnp.where(number % 4 == 0, named(heavy_load, number // 4), named(ordinary, number - number // 4 - 1))
    mixed = jax.random.permutation(jax.random.fold_in(own, 3), count)
    donor, sink = mixed[0:count // 2 * 2:2], mixed[1:count // 2 * 2:2]
    room = jnp.minimum(lengths[donor] - 1, reach - lengths[sink]) // 2
    room = jnp.where((donor == order[0]) | (sink == order[0]) | (lengths[sink] == 0), 0, jnp.maximum(room, 0))
    shifted = jax.random.randint(jax.random.fold_in(own, 4), (count // 2,), 0, 1 << 20) % (room + 1)
    lengths = lengths.at[donor].add(-shifted).at[sink].add(shifted)
    members = jnp.searchsorted(jnp.cumsum(lengths), jnp.arange(rows * top), side="right").astype(jnp.int32)
    listing = members.reshape(top, rows).T
    listing = listing[jax.random.permutation(jax.random.fold_in(own, 1), rows)]
    rotation = jax.random.randint(jax.random.fold_in(own, 2), (rows, 1), 0, top)
    return jnp.take_along_axis(listing, (jnp.arange(top)[None, :] + rotation) % top, axis=1)


def portions_of(amount, total, reach, skew, full):
    weights = [(1 << 20) // math.isqrt(grade ** skew) + 1 for grade in range(1, amount + 1)]
    largest = reach if full else min(reach, max(-(-total // amount), total * weights[0] // sum(weights)))
    least = 1 if total - largest >= amount - 1 else 0
    given, surplus = [largest] + [least] * (amount - 1), total - largest - least * (amount - 1)
    while surplus > 0:
        movable = [i for i in range(1, amount) if given[i] < largest] or [i for i in range(1, amount) if given[i] < reach]
        mass, left = sum([weights[i] for i in movable]), surplus
        for i in movable:
            more = min(reach - given[i], max(1, left * weights[i] // mass), surplus)
            given[i] = given[i] + more
            surplus = surplus - more
    return np.array(given)


def bell_draw(own_key, extent, deviation, limit, cuts=(), held_as=jnp.bfloat16):
    drawn = deviation * jax.random.normal(own_key, extent, jnp.float32)
    if cuts:
        drawn = drawn * block_levels(own_key, extent, cuts, -0.22, 0.18)
    return jnp.clip(drawn, -limit, limit).astype(held_as)


def setup_inputs(seed: int = 0) -> dict:
    streams_of = jax.random.split(jax.random.key(seed), 18)
    x_embed = draw_x_embed(jax.random.fold_in(streams_of[17], 71), 0)
    doc_ids = jax.vmap(lambda own: jnp.searchsorted(jnp.cumsum(ragged_sizes(own, DOCS, LEN, DOCLEN, 2)), jnp.arange(LEN), side="right"))(jax.random.split(streams_of[1], SEQS)).reshape((SEQS, LEN)).astype(jnp.int32)
    owners_keys = jax.random.split(jax.random.fold_in(streams_of[2], 1), SEQS * LEN // TOK_DEV)
    owners_turns = jax.random.permutation(jax.random.fold_in(streams_of[2], 3), SEQS * LEN // TOK_DEV)
    owners = jax.vmap(lambda own, number: assign_block(jax.random.fold_in(streams_of[2], 2), own, number, TOK_DEV, DEVICES, 2, CAP, 1))(owners_keys, owners_turns).reshape((SEQS, LEN, 2))
    row_ids = with_ends(jax.random.randint(streams_of[3], (SEQS, LEN, 2), 0, ROWS_DEV), jax.random.fold_in(streams_of[3], 1), 0, ROWS_DEV - 1).astype(jnp.int32)
    table = bell_draw(streams_of[4], (TABLE_ROWS, ROW_WIDTH), 1.0, 6.0, ((0, 32),))
    ngram_weight = bell_draw(streams_of[5], (2 * ROW_WIDTH, D), (2 * ROW_WIDTH) ** -0.5, 0.3125, ((0, 2),))
    stream_gain = jnp.clip(1.0 + 0.1 * jax.random.normal(streams_of[6], (D,), jnp.float32), 0.5, 1.5).astype(jnp.bfloat16)
    query_weight = bell_draw(streams_of[7], (D, D), D ** -0.5, 0.21875, ((0, 2),))
    key_weight = bell_draw(streams_of[8], (D, D), D ** -0.5, 0.21875, ((0, 2),))
    value_weight = bell_draw(streams_of[9], (D, D), D ** -0.5, 0.21875, ((0, 2),))
    out_weight = bell_draw(streams_of[10], (D, D), (max(1, D // 64)) ** -0.5, 1.75, ((0, 2),))
    mixer_gain = jnp.clip(1.0 + 0.1 * jax.random.normal(streams_of[11], (D,), jnp.float32), 0.5, 1.5).astype(jnp.bfloat16)
    gate_weight = bell_draw(streams_of[12], (D, FF), D ** -0.5, 0.21875, ((0, 2),))
    up_weight = bell_draw(streams_of[13], (D, FF), D ** -0.5, 0.21875, ((0, 2),))
    down_weight = bell_draw(streams_of[14], (FF, D), (FF // 4) ** -0.5, 0.25, ((0, 2),))
    feed_gain = jnp.clip(1.0 + 0.1 * jax.random.normal(streams_of[15], (D,), jnp.float32), 0.5, 1.5).astype(jnp.bfloat16)
    cotangent = bell_draw(streams_of[16], (SEQS, LEN, D), 1.0, 6.0, ((0, 2), (1, 16)))
    return {"x_embed": x_embed, "doc_ids": doc_ids, "owners": owners, "row_ids": row_ids, "table": table, "ngram_weight": ngram_weight, "stream_gain": stream_gain, "query_weight": query_weight, "key_weight": key_weight, "value_weight": value_weight, "out_weight": out_weight, "mixer_gain": mixer_gain, "gate_weight": gate_weight, "up_weight": up_weight, "down_weight": down_weight, "feed_gain": feed_gain, "cotangent": cotangent}


EPSILON = 1e-06
ROPE_BASE = 500000.0
MASKED_SCORE = -1e+30

@jax.custom_vjp
def low(v):
    return lax.optimization_barrier(v.astype(jnp.bfloat16)).astype(jnp.float32)

@jax.custom_vjp
def low_back(v):
    return v

def low_keep(v):
    return (low(v), None)

def low_pass(kept, grad):
    return (grad,)

def back_keep(v):
    return (v, None)

def back_low(kept, grad):
    return (low(grad),)
low.defvjp(low_keep, low_pass)
low_back.defvjp(back_keep, back_low)

def rms_norm(field, gain_row):
    return field * lax.rsqrt(lax.optimization_barrier(jnp.mean(field * field, axis=-1, keepdims=True)) + EPSILON) * gain_row

def project(activations, weight):
    return jnp.einsum('sti,io->sto', activations, weight, precision=lax.Precision.HIGHEST)

def rotary(field, places):
    half_dim = HEAD_DIM // 2
    frequency = ROPE_BASE ** (-2.0 * jnp.arange(half_dim, dtype=jnp.float32) / HEAD_DIM)
    angles = places.astype(jnp.float32)[:, None] * frequency[None, :]
    cosine = jnp.cos(angles)[:, None, :]
    sine_part = jnp.sin(angles)[:, None, :]
    first_half = field[..., :half_dim]
    second_half = field[..., half_dim:]
    return jnp.concatenate([first_half * cosine - second_half * sine_part, second_half * cosine + first_half * sine_part], axis=-1)

def attend(query_rot, key_rot, value_low, documents, places):
    block_count = LEN // 512
    scale_factor = HEAD_DIM ** (-0.5)

    def one_block(block_item):
        query_block, query_places, query_docs = block_item
        raw_scores = jnp.einsum('qhd,khd->hqk', query_block, key_rot, precision=lax.Precision.HIGHEST)
        allowed = (query_places[:, None] >= places[None, :]) & (query_docs[:, None] == documents[None, :])
        scores = low_back(jnp.where(allowed[None], raw_scores * scale_factor, MASKED_SCORE))
        row_max = lax.optimization_barrier(jnp.max(scores, axis=-1, keepdims=True))
        lifted = jnp.exp(scores - row_max)
        probability = low(lifted / lax.optimization_barrier(jnp.sum(lifted, axis=-1, keepdims=True)))
        return jnp.einsum('hqk,khd->qhd', probability, value_low, precision=lax.Precision.HIGHEST)
    blocks = lax.map(jax.checkpoint(one_block), (query_rot.reshape(block_count, 512, HEADS, HEAD_DIM), places.reshape(block_count, 512), documents.reshape(block_count, 512)))
    return blocks.reshape(LEN, HEADS, HEAD_DIM)

def forward(x_embed, table, ngram_weight, stream_gain, query_weight, key_weight, value_weight, out_weight, mixer_gain, gate_weight, up_weight, down_weight, feed_gain, owners, row_ids, doc_ids):
    table_ids = owners * ROWS_DEV + row_ids
    picked = low_back(jnp.take(table, table_ids, axis=0)).reshape(SEQS, LEN, 2 * ROW_WIDTH)
    embedded = low_back(project(picked, ngram_weight))
    stream = x_embed + embedded
    residual = rms_norm(stream, stream_gain)
    mixer_in = low(rms_norm(residual, mixer_gain))
    query_rows = low_back(project(mixer_in, query_weight))
    key_rows = low_back(project(mixer_in, key_weight))
    value_rows = low_back(project(mixer_in, value_weight))
    places = jnp.arange(LEN, dtype=jnp.int32)
    heads_out = []
    for sequence in range(SEQS):
        query_rot = low(rotary(query_rows[sequence].reshape(LEN, HEADS, HEAD_DIM), places))
        key_rot = low(rotary(key_rows[sequence].reshape(LEN, HEADS, HEAD_DIM), places))
        value_low = low(value_rows[sequence].reshape(LEN, HEADS, HEAD_DIM))
        heads_out.append(attend(query_rot, key_rot, value_low, doc_ids[sequence], places).reshape(LEN, D))
    heads_low = low(low_back(jnp.stack(heads_out)))
    mixer_out = project(heads_low, out_weight)
    middle = residual + low_back(mixer_out)
    feed_in = low(rms_norm(middle, feed_gain))
    gate_rows = low_back(project(feed_in, gate_weight))
    up_rows = low_back(project(feed_in, up_weight))
    hidden = low(jax.nn.silu(gate_rows) * up_rows)
    feed_out = project(hidden, down_weight)
    result = middle + low_back(feed_out)
    return (result, (stream, mixer_out, feed_out))

def reference(x_embed, doc_ids, owners, row_ids, table, ngram_weight, stream_gain, query_weight, key_weight, value_weight, out_weight, mixer_gain, gate_weight, up_weight, down_weight, feed_gain, cotangent):
    floats = (x_embed, table, ngram_weight, stream_gain, query_weight, key_weight, value_weight, out_weight, mixer_gain, gate_weight, up_weight, down_weight, feed_gain)
    floats = jax.tree.map(lambda array_in: array_in.astype(jnp.float32), floats)

    def wrapped(*values_in):
        return forward(*values_in, owners, row_ids, doc_ids)
    mixed, pullback, extras = jax.vjp(wrapped, *floats, has_aux=True)
    stream, mixer_out, feed_out = extras
    gradients = pullback(cotangent.astype(jnp.float32))
    stream_rms = jnp.sqrt(jnp.mean(stream * stream))
    mixer_rms = jnp.sqrt(jnp.mean(mixer_out * mixer_out))
    feed_rms = jnp.sqrt(jnp.mean(feed_out * feed_out))
    return (mixed.astype(jnp.bfloat16), gradients[0], stream_rms, mixer_rms, feed_rms, gradients[1], gradients[2], gradients[3], gradients[4], gradients[5], gradients[6], gradients[7], gradients[8], gradients[9], gradients[10], gradients[11], gradients[12])
```

```python
import functools

import jax
import jax.numpy as jnp
import numpy as np
from jax import lax
from jax.experimental import pallas as pl
from jax.experimental.pallas import tpu as pltpu
from jax.sharding import PartitionSpec as P

HEADS = 12
HEAD_DIM = 64
DOC_MAX = 4096
DOC_FEATURES = 16

EPSILON = 1e-06
ROPE_BASE = 500000.0
LOG2E = 1.4426950408889634
LN2 = 0.6931471805599453
FAR = 1073741824.0

GROUP = 3
GROUPS = HEADS // GROUP
HALF = HEAD_DIM // 2
VROWS = 80
SLOTS = 12
DOC_LANE = 96
LSE_LANE = 112
DELTA_LANE = 192

F32 = jnp.float32
BF16 = jnp.bfloat16
VMEM_BIG = 64000000


def nt(a, b):
    return lax.dot_general(a, b, (((1,), (1,)), ((), ())), preferred_element_type=F32)


def nn(a, b):
    return jnp.dot(a, b, preferred_element_type=F32)


def tn(a, b):
    return lax.dot_general(a, b, (((0,), (0,)), ((), ())), preferred_element_type=F32)


def norm_parts(field, gain_row):
    inverse = lax.rsqrt(jnp.mean(field * field, axis=-1, keepdims=True) + EPSILON)
    unit_rows = field * inverse
    return (unit_rows * gain_row, unit_rows, inverse)


def norm_back(gradient, unit_rows, inverse, gain_row):
    scaled = gradient * gain_row
    back_rows = inverse * (
        scaled - unit_rows * jnp.mean(scaled * unit_rows, axis=-1, keepdims=True)
    )
    return (back_rows, jnp.sum(gradient * unit_rows, axis=0))


CHUNKS = 2


def remote(src, dst, sems, kind, chunk, target):
    return pltpu.make_async_remote_copy(
        src_ref=src,
        dst_ref=dst,
        send_sem=sems[0].at[kind, chunk],
        recv_sem=sems[1].at[kind, chunk],
        device_id={"seq": target},
        device_id_type=pl.DeviceIdType.MESH,
    )


def greet(me, group_count):
    barrier = pltpu.get_barrier_semaphore()
    group = me // 4
    mine = me % 4
    peers = (group * 4 + (mine + 2) % 4, group * 4 + mine + 1 - 2 * (mine % 2))
    for peer in peers:
        pl.semaphore_signal(
            barrier, inc=1, device_id={"seq": peer}, device_id_type=pl.DeviceIdType.MESH
        )
    up = group + 1 < group_count
    down = group > 0

    @pl.when(up)
    def _():
        pl.semaphore_signal(
            barrier, inc=1, device_id={"seq": me + 4}, device_id_type=pl.DeviceIdType.MESH
        )

    @pl.when(down)
    def _():
        pl.semaphore_signal(
            barrier, inc=1, device_id={"seq": me - 4}, device_id_type=pl.DeviceIdType.MESH
        )

    pl.semaphore_wait(barrier, 2 + up.astype(jnp.int32) + down.astype(jnp.int32))


def gather_kernel(group_count, own_ref, out_ref, send_sem, recv_sem, local_sem):
    me = lax.axis_index("seq")
    group = me // 4
    mine = me % 4
    core = mine % 2
    far = mine // 2
    over = (mine + 2) % 4
    partner = mine + 1 - 2 * core
    over_id = group * 4 + over
    partner_id = group * 4 + partner
    rows = own_ref.shape[0] // CHUNKS
    sems = (send_sem, recv_sem)
    has_one = group >= 1
    has_two = group >= 2
    up = group + 1 < group_count
    greet(me, group_count)

    def part(ref, chunk):
        return ref.at[pl.ds(chunk * rows, rows)]

    def slot(level, pos, chunk):
        return out_ref.at[level * 4 + pos, pl.ds(chunk * rows, rows)]

    def own_send(kind, level, target, chunk):
        return remote(part(own_ref, chunk), slot(level, mine, chunk), sems, kind, chunk, target)

    def relay(kind, level, pos, to_level, target, chunk):
        return remote(slot(level, pos, chunk), slot(to_level, pos, chunk), sems, kind, chunk, target)

    moves = {
        "z1": lambda c: own_send(0, 1, me + 4, c),
        "x0": lambda c: own_send(1, 0, over_id, c),
        "c0": lambda c: own_send(2, 0, partner_id, c),
        "c0b": lambda c: relay(3, 0, over, 0, partner_id, c),
        "z2": lambda c: relay(4, 1, mine, 2, me + 4, c),
        "x1": lambda c: relay(5, 1, mine, 1, over_id, c),
        "c1a": lambda c: relay(6, 1, mine, 1, partner_id, c),
        "c1b": lambda c: relay(7, 1, over, 1, partner_id, c),
        "x2": lambda c: relay(8, 2, mine, 2, over_id, c),
        "c2a": lambda c: relay(9, 2, mine, 2, partner_id, c),
        "c2b": lambda c: relay(10, 2, over, 2, partner_id, c),
    }
    sends = {
        "z1": up,
        "x0": far == 0,
        "c0": core == 0,
        "c0b": far == 1,
        "z2": has_one & up,
        "x1": has_one,
        "c1a": has_one,
        "c1b": has_one,
        "x2": has_two & (far == 1),
        "c2a": has_two & (core == 1),
        "c2b": has_two & (far == 0),
    }
    receives = {
        "z1": has_one,
        "x0": far == 1,
        "c0": core == 1,
        "c0b": far == 1,
        "z2": has_two,
        "x1": has_one,
        "c1a": has_one,
        "c1b": has_one,
        "x2": has_two & (far == 0),
        "c2a": has_two & (core == 0),
        "c2b": has_two & (far == 0),
    }

    def start(name, chunk):
        @pl.when(sends[name])
        def _():
            moves[name](chunk).start()

    def take(name, chunk):
        @pl.when(receives[name])
        def _():
            moves[name](chunk).wait_recv()

    def finish(name, chunk):
        @pl.when(sends[name])
        def _():
            moves[name](chunk).wait_send()

    every = range(CHUNKS)
    for chunk in every:
        for name in ("z1", "x0", "c0"):
            start(name, chunk)
    local = pltpu.make_async_copy(own_ref, out_ref.at[mine], local_sem)
    local.start()
    for chunk in every:
        take("z1", chunk)
        for name in ("z2", "x1", "c1a"):
            start(name, chunk)
        take("x0", chunk)
        start("c0b", chunk)
    for chunk in every:
        take("x1", chunk)
        start("c1b", chunk)
        take("z2", chunk)
        start("x2", chunk)
        start("c2a", chunk)
    for chunk in every:
        take("x2", chunk)
        start("c2b", chunk)
    for chunk in every:
        for name in ("c0", "c0b", "c1a", "c1b", "c2a", "c2b"):
            take(name, chunk)
    local.wait()
    for chunk in every:
        for name in moves:
            finish(name, chunk)


def halo_gather(own, group_count):
    tokens, width = own.shape
    return pl.pallas_call(
        functools.partial(gather_kernel, group_count),
        out_shape=jax.ShapeDtypeStruct((SLOTS + 1, tokens, width), own.dtype),
        in_specs=[pl.BlockSpec(memory_space=pltpu.VMEM)],
        out_specs=pl.BlockSpec(memory_space=pl.ANY),
        scratch_shapes=[
            pltpu.SemaphoreType.DMA((11, CHUNKS)),
            pltpu.SemaphoreType.DMA((11, CHUNKS)),
            pltpu.SemaphoreType.DMA,
        ],
        compiler_params=pltpu.CompilerParams(collective_id=1, has_side_effects=True),
        name="halo_gather",
    )(own)


def reduce_kernel(
    group_count, part_ref, out_ref, work_ref, got_ref, send_sem, recv_sem, local_sem
):
    me = lax.axis_index("seq")
    group = me // 4
    mine = me % 4
    core = mine % 2
    far = mine // 2
    over = (mine + 2) % 4
    partner = mine + 1 - 2 * core
    partner_over = (partner + 2) % 4
    over_id = group * 4 + over
    partner_id = group * 4 + partner
    rows = out_ref.shape[0] // CHUNKS
    sems = (send_sem, recv_sem)
    has_one = group >= 1
    has_two = group >= 2
    up = group + 1 < group_count

    def load(level):
        four = pl.ds(level * 4, 4)
        return pltpu.make_async_copy(part_ref.at[four], work_ref.at[four], local_sem.at[level])

    for level in (2, 1, 0):
        load(level).start()
    greet(me, group_count)

    def span(chunk):
        return pl.ds(chunk * rows, rows)

    def send(kind, level, pos, target, chunk):
        return remote(
            work_ref.at[level * 4 + pos, span(chunk)],
            got_ref.at[kind, span(chunk)],
            sems,
            kind,
            chunk,
            target,
        )

    moves = {
        "c2o": lambda c: send(0, 2, partner_over, partner_id, c),
        "c2": lambda c: send(1, 2, partner, partner_id, c),
        "c1o": lambda c: send(2, 1, partner_over, partner_id, c),
        "c1": lambda c: send(3, 1, partner, partner_id, c),
        "c0o": lambda c: send(4, 0, partner_over, partner_id, c),
        "c0": lambda c: send(5, 0, partner, partner_id, c),
        "x2": lambda c: send(6, 2, over, over_id, c),
        "x1": lambda c: send(7, 1, over, over_id, c),
        "x0": lambda c: send(8, 0, over, over_id, c),
        "z2": lambda c: send(9, 2, mine, me - 4, c),
        "z1": lambda c: send(10, 1, mine, me - 4, c),
    }
    kinds = {name: kind for kind, name in enumerate(moves)}
    sends = {
        "c2o": has_two & (far == 0),
        "c2": has_two & (core == 0),
        "c1o": has_one,
        "c1": has_one,
        "c0o": far == 1,
        "c0": core == 1,
        "x2": has_two & (far == 0),
        "x1": has_one,
        "x0": far == 1,
        "z2": has_two,
        "z1": has_one,
    }
    receives = {
        "c2o": has_two & (far == 0),
        "c2": has_two & (core == 1),
        "c1o": has_one,
        "c1": has_one,
        "c0o": far == 1,
        "c0": core == 0,
        "x2": has_two & (far == 1),
        "x1": has_one,
        "x0": far == 0,
        "z2": has_one & up,
        "z1": up,
    }
    lands = {
        "c2o": (2, over),
        "c2": (2, mine),
        "c1o": (1, over),
        "c1": (1, mine),
        "c0o": (0, over),
        "c0": (0, mine),
        "x2": (2, mine),
        "x1": (1, mine),
        "x0": (0, mine),
        "z2": (1, mine),
        "z1": (0, mine),
    }

    def start(name, chunk):
        @pl.when(sends[name])
        def _():
            moves[name](chunk).start()

    def absorb(name, chunk):
        @pl.when(receives[name])
        def _():
            moves[name](chunk).wait_recv()
            level, pos = lands[name]
            at = level * 4 + pos
            total = work_ref[at, span(chunk), :].astype(F32) + got_ref[
                kinds[name], span(chunk), :
            ].astype(F32)
            work_ref[at, span(chunk), :] = total.astype(BF16)

    every = range(CHUNKS)
    for level in (2, 1, 0):
        load(level).wait()
        for name in (f"c{level}o", f"c{level}"):
            for chunk in every:
                start(name, chunk)
    for level in (2, 1, 0):
        for chunk in every:
            absorb(f"c{level}o", chunk)
            start(f"x{level}", chunk)
    for chunk in every:
        absorb("c2", chunk)
        absorb("x2", chunk)
        start("z2", chunk)
    for chunk in every:
        absorb("c1", chunk)
        absorb("x1", chunk)
        absorb("z2", chunk)
        start("z1", chunk)
    for chunk in every:
        absorb("c0", chunk)
        absorb("x0", chunk)
        absorb("z1", chunk)
        out_ref[span(chunk), :] = work_ref[mine, span(chunk), :].astype(F32)
    for name in moves:
        for chunk in every:

            @pl.when(sends[name])
            def _():
                moves[name](chunk).wait_send()


def halo_reduce(parts, group_count):
    slots, tokens, width = parts.shape
    return pl.pallas_call(
        functools.partial(reduce_kernel, group_count),
        out_shape=jax.ShapeDtypeStruct((tokens, width), F32),
        in_specs=[pl.BlockSpec(memory_space=pl.ANY)],
        out_specs=pl.BlockSpec(memory_space=pltpu.VMEM),
        scratch_shapes=[
            pltpu.VMEM((SLOTS, tokens, width), BF16),
            pltpu.VMEM((11, tokens, width), BF16),
            pltpu.SemaphoreType.DMA((11, CHUNKS)),
            pltpu.SemaphoreType.DMA((11, CHUNKS)),
            pltpu.SemaphoreType.DMA((3,)),
        ],
        compiler_params=pltpu.CompilerParams(
            collective_id=2, has_side_effects=True, vmem_limit_bytes=VMEM_BIG
        ),
        name="halo_reduce",
    )(parts)


def lane_tables(tokens):
    theta = ROPE_BASE ** (-2.0 * jnp.arange(HALF, dtype=F32) / HEAD_DIM)
    lanes = jnp.concatenate([theta] * GROUP + [jnp.zeros((128 - GROUP * HALF,), F32)])
    angle = jnp.arange(tokens, dtype=F32)[:, None] * lanes[None, :]
    return theta, lanes, jnp.cos(angle), jnp.sin(angle)


def rotate(pair, cosine, sine):
    first, second = pair[:, :128], pair[:, 128:]
    return first * cosine - second * sine, second * cosine + first * sine


def block_angles(step, cos_row, sin_row, cos_block, sin_block):
    c_row, s_row = cos_row[...], sin_row[...]
    c_blk, s_blk = cos_block[pl.ds(step, 1), :], sin_block[pl.ds(step, 1), :]
    return c_row * c_blk - s_row * s_blk, s_row * c_blk + c_row * s_blk


def head_lanes(shape, start, width):
    lane = lax.broadcasted_iota(jnp.int32, shape, 1)
    return (lane >= start) & (lane < start + width)


def forward_kernel(
    slot_ref, valid_ref, own_ref, x_ref, wq_ref, wk_ref, wv_ref, cr_ref, sr_ref, cb_ref, sb_ref,
    kf_ref, qf_ref, out_ref, lse_ref, qm_ref, kb_ref, vt_ref, acc_ref, top_ref,
):
    step = pl.program_id(0)
    tokens = own_ref.shape[0]

    @pl.when(step == 0)
    def _():
        cosine, sine = block_angles(0, cr_ref, sr_ref, cb_ref, sb_ref)
        features = qf_ref[...].astype(F32)

        def one_group(g, carry):
            first, second = rotate(nn(own_ref[...], wq_ref[g]), cosine, sine)
            for hh in range(GROUP):
                mask = head_lanes((tokens, 128), hh * HALF, HALF)
                scale = LOG2E * HEAD_DIM**-0.5
                qm_ref[g * GROUP + hh, :, :128] = (
                    jnp.where(mask, first * scale, features).astype(BF16)
                )
                qm_ref[g * GROUP + hh, :, 128:] = (
                    jnp.where(mask, second * scale, 0.0).astype(BF16)
                )
            return carry

        lax.fori_loop(0, GROUPS, one_group, 0)
        top_ref[...] = jnp.full_like(top_ref, -FAR * FAR)
        acc_ref[...] = jnp.zeros_like(acc_ref)

    @pl.when(valid_ref[step] > 0)
    def _():
        x = x_ref[0]
        cosine, sine = block_angles(step, cr_ref, sr_ref, cb_ref, sb_ref)
        features = kf_ref[0].astype(F32)

        def keys(g, carry):
            first, second = rotate(nn(x_ref[0], wk_ref[g]), cosine, sine)
            kb_ref[g, :, :128] = (first + features).astype(BF16)
            kb_ref[g, :, 128:] = second.astype(BF16)
            values = nt(wv_ref[g], x_ref[0])
            row = lax.broadcasted_iota(jnp.int32, values.shape, 0) % VROWS
            values = jnp.where(row == HEAD_DIM, 1.0, values).astype(BF16)
            for hh in range(GROUP):
                vt_ref[g * GROUP + hh] = values[hh * VROWS : (hh + 1) * VROWS]
            return carry

        lax.fori_loop(0, GROUPS, keys, 0)

        def attend(causal):
            def one_group(g, carry):
                for hh in range(GROUP):
                    h = g * GROUP + hh
                    scores = nt(kb_ref[g], qm_ref[h])
                    if causal:
                        key = lax.broadcasted_iota(jnp.int32, scores.shape, 0)
                        query = lax.broadcasted_iota(jnp.int32, scores.shape, 1)
                        scores = jnp.where(key <= query, scores, -FAR)
                    old = top_ref[h]
                    new = jnp.maximum(old, jnp.max(scores, axis=0, keepdims=True))
                    prob = jnp.exp2(scores - new).astype(BF16)
                    fade = jnp.exp2(old - new)
                    acc_ref[h] = acc_ref[h] * fade + nn(vt_ref[h], prob)
                    top_ref[h] = new
                return carry

            lax.fori_loop(0, GROUPS, one_group, 0)

        @pl.when(step == 0)
        def _():
            attend(True)

        @pl.when(step > 0)
        def _():
            attend(False)

    @pl.when(step == pl.num_programs(0) - 1)
    def _():
        lses = []
        for g in range(GROUPS):
            parts = []
            for h in range(g * GROUP, (g + 1) * GROUP):
                total = acc_ref[h, HEAD_DIM : HEAD_DIM + 1, :]
                parts.append(acc_ref[h, :HEAD_DIM, :] / total)
                lses.append(top_ref[h] + jnp.log2(total))
            parts.append(jnp.zeros((256 - GROUP * HEAD_DIM, tokens), F32))
            out_ref[:, g * 256 : (g + 1) * 256] = jnp.concatenate(parts, axis=0).T
        lses.append(jnp.zeros((128 - HEADS, tokens), F32))
        lse_ref[...] = jnp.concatenate(lses, axis=0).T


def whole(*shape):
    return pl.BlockSpec(shape, lambda *_: (0,) * len(shape), pipeline_mode=pl.Buffered(1))


def attention_forward(own, blocks, slots, valid, weights, tables, features):
    tokens, width = own.shape
    steps = slots.shape[0]
    key_features, query_features = features
    wq, wk, wv = weights
    return pl.pallas_call(
        forward_kernel,
        out_shape=(
            jax.ShapeDtypeStruct((tokens, GROUPS * 256), F32),
            jax.ShapeDtypeStruct((tokens, 128), F32),
        ),
        grid_spec=pltpu.PrefetchScalarGridSpec(
            num_scalar_prefetch=2,
            grid=(steps,),
            in_specs=[
                whole(tokens, width),
                pl.BlockSpec((1, tokens, width), lambda t, slot, valid: (slot[t], 0, 0)),
                whole(*wq.shape),
                whole(*wk.shape),
                whole(*wv.shape),
                whole(tokens, 128),
                whole(tokens, 128),
                whole(*tables[2].shape),
                whole(*tables[3].shape),
                pl.BlockSpec((1, tokens, 128), lambda t, slot, valid: (t, 0, 0)),
                whole(tokens, 128),
            ],
            out_specs=[whole(tokens, GROUPS * 256), whole(tokens, 128)],
            scratch_shapes=[
                pltpu.VMEM((HEADS, tokens, 256), BF16),
                pltpu.VMEM((GROUPS, tokens, 256), BF16),
                pltpu.VMEM((HEADS, VROWS, tokens), BF16),
                pltpu.VMEM((HEADS, VROWS, tokens), F32),
                pltpu.VMEM((HEADS, 1, tokens), F32),
            ],
        ),
        compiler_params=pltpu.CompilerParams(
            dimension_semantics=("arbitrary",), vmem_limit_bytes=VMEM_BIG
        ),
        name="attention_forward",
    )(slots, valid, own, blocks, wq, wk, wv, *tables, key_features, query_features)


def split_bf16(column):
    high = column.astype(BF16).astype(F32)
    return high, column - high


def backward_kernel(
    slot_ref, valid_ref, own_ref, x_ref, wq_ref, wk_ref, wkt_ref, wv_ref, cr_ref, sr_ref, cb_ref,
    sb_ref, ct_ref, st_ref, kf_ref, qf_ref, go_ref, heads_ref, lse_ref, gx_ref, dq_ref, dwk_ref,
    dwv_ref, qb_ref, gm_ref, kb_ref, kt_ref, vb_ref, dqt_ref, dk_ref, dv_ref, gxa_ref, wka_ref,
    wva_ref,
):
    step = pl.program_id(0)
    tokens = own_ref.shape[0]

    @pl.when(step == 0)
    def _():
        cosine, sine = block_angles(0, cr_ref, sr_ref, cb_ref, sb_ref)
        features = qf_ref[...].astype(F32)

        def one_group(g, carry):
            first, second = rotate(nn(own_ref[...], wq_ref[g]), cosine, sine)
            lane = lax.broadcasted_iota(jnp.int32, (tokens, 128), 1)
            wide = lax.broadcasted_iota(jnp.int32, (tokens, 256), 1)
            lanes = pl.ds(pl.multiple_of(g * 256, 256), 256)
            grads = go_ref[:, lanes].astype(F32)
            products = grads * heads_ref[:, lanes]
            for hh in range(GROUP):
                h = g * GROUP + hh
                lse = jnp.sum(jnp.where(lane == h, lse_ref[...], 0.0), axis=1, keepdims=True)
                own = head_lanes((tokens, 256), hh * HEAD_DIM, HEAD_DIM)
                delta = jnp.sum(jnp.where(own, products, 0.0), axis=1, keepdims=True)
                lse_one, rest = split_bf16(lse)
                lse_two, lse_three = split_bf16(rest)
                mask = head_lanes((tokens, 128), hh * HALF, HALF)
                scale = LOG2E * HEAD_DIM**-0.5
                tile = jnp.where(mask, first * scale, features)
                tile = jnp.where(lane == LSE_LANE, -lse_one, tile)
                tile = jnp.where(lane == LSE_LANE + 1, -lse_two, tile)
                tile = jnp.where(lane == LSE_LANE + 2, -lse_three, tile)
                qb_ref[h, :, :128] = tile.astype(BF16)
                qb_ref[h, :, 128:] = jnp.where(mask, second * scale, 0.0).astype(BF16)
                delta_one, delta_two = split_bf16(delta)
                tile = jnp.where(own, grads, 0.0)
                tile = jnp.where(wide == DELTA_LANE, -delta_one, tile)
                tile = jnp.where(wide == DELTA_LANE + 1, -delta_two, tile)
                gm_ref[h] = tile.astype(BF16)
            return carry

        lax.fori_loop(0, GROUPS, one_group, 0)
        dqt_ref[...] = jnp.zeros_like(dqt_ref)
        wka_ref[...] = jnp.zeros_like(wka_ref)
        wva_ref[...] = jnp.zeros_like(wva_ref)

    @pl.when(valid_ref[step] > 0)
    def _():
        cosine, sine = block_angles(step, cr_ref, sr_ref, cb_ref, sb_ref)
        features = kf_ref[0].astype(F32)

        def keys(g, carry):
            first, second = rotate(nn(x_ref[0], wk_ref[g]), cosine, sine)
            kb_ref[g, :, :128] = (first + features).astype(BF16)
            kb_ref[g, :, 128:] = second.astype(BF16)
            values = nn(x_ref[0], wv_ref[g])
            wide = lax.broadcasted_iota(jnp.int32, values.shape, 1)
            ones = (wide == DELTA_LANE) | (wide == DELTA_LANE + 1)
            vb_ref[g] = jnp.where(ones, 1.0, values).astype(BF16)
            turned = nt(wkt_ref[g], x_ref[0])
            for hh in range(GROUP):
                upper = turned[hh * HEAD_DIM : hh * HEAD_DIM + HALF]
                lower = turned[hh * HEAD_DIM + HALF : (hh + 1) * HEAD_DIM]
                c_row, s_row = ct_ref[step], st_ref[step]
                kt_ref[g * GROUP + hh, :HALF] = (upper * c_row - lower * s_row).astype(BF16)
                kt_ref[g * GROUP + hh, HALF:] = (lower * c_row + upper * s_row).astype(BF16)
            return carry

        lax.fori_loop(0, GROUPS, keys, 0)

        def grads(causal):
            def one_group(g, carry):
                for hh in range(GROUP):
                    h = g * GROUP + hh
                    prob = jnp.exp2(nt(kb_ref[g], qb_ref[h]))
                    if causal:
                        key = lax.broadcasted_iota(jnp.int32, prob.shape, 0)
                        query = lax.broadcasted_iota(jnp.int32, prob.shape, 1)
                        prob = jnp.where(key <= query, prob, 0.0)
                    grad = (prob * nt(vb_ref[g], gm_ref[h])).astype(BF16)
                    prob = prob.astype(BF16)
                    value_part = nn(prob, gm_ref[h])
                    key_part = nn(grad, qb_ref[h])
                    if hh == 0:
                        dv_ref[...] = value_part
                        dk_ref[...] = key_part
                    else:
                        dv_ref[...] += value_part
                        dk_ref[...] += key_part
                    dqt_ref[h] += nn(kt_ref[h], grad)
                first, second = rotate(dk_ref[...] * LN2, cosine, -sine)
                pad = head_lanes((tokens, 128), 0, GROUP * HALF)
                key_rows = jnp.concatenate(
                    [jnp.where(pad, first, 0.0), jnp.where(pad, second, 0.0)], axis=1
                ).astype(BF16)
                keep = head_lanes((tokens, 256), 0, GROUP * HEAD_DIM)
                value_rows = jnp.where(keep, dv_ref[...], 0.0).astype(BF16)
                wka_ref[g] += tn(x_ref[0], key_rows)
                wva_ref[g] += tn(x_ref[0], value_rows)
                gxa_ref[...] += nt(key_rows, wk_ref[g]) + nt(value_rows, wv_ref[g])
                return carry

            gxa_ref[...] = jnp.zeros_like(gxa_ref)
            lax.fori_loop(0, GROUPS, one_group, 0)
            gx_ref[0] = gxa_ref[...].astype(BF16)

        @pl.when(step == 0)
        def _():
            grads(True)

        @pl.when(step > 0)
        def _():
            grads(False)

    @pl.when(step == pl.num_programs(0) - 1)
    def _():
        for h in range(HEADS):
            upper = dqt_ref[h, :HALF, :] * HEAD_DIM**-0.5
            lower = dqt_ref[h, HALF:, :] * HEAD_DIM**-0.5
            c_row, s_row = ct_ref[0], st_ref[0]
            dq_ref[h * HEAD_DIM : h * HEAD_DIM + HALF, :] = (
                upper * c_row + lower * s_row
            ).astype(BF16)
            dq_ref[h * HEAD_DIM + HALF : (h + 1) * HEAD_DIM, :] = (
                lower * c_row - upper * s_row
            ).astype(BF16)
        dwk_ref[...] = wka_ref[...].astype(BF16)
        dwv_ref[...] = wva_ref[...].astype(BF16)


def attention_backward(
    own, blocks, slots, valid, weights, tables, turned, features, grad_heads, heads, lse
):
    tokens, width = own.shape
    steps = slots.shape[0]
    key_features, query_features = features
    wq, wk, wkt, wv = weights
    ct, st = turned
    return pl.pallas_call(
        backward_kernel,
        out_shape=(
            jax.ShapeDtypeStruct((SLOTS + 1, tokens, width), BF16),
            jax.ShapeDtypeStruct((width, tokens), BF16),
            jax.ShapeDtypeStruct(wk.shape, BF16),
            jax.ShapeDtypeStruct(wv.shape, BF16),
        ),
        grid_spec=pltpu.PrefetchScalarGridSpec(
            num_scalar_prefetch=2,
            grid=(steps,),
            in_specs=[
                whole(tokens, width),
                pl.BlockSpec((1, tokens, width), lambda t, slot, valid: (slot[t], 0, 0)),
                whole(*wq.shape),
                whole(*wk.shape),
                whole(*wkt.shape),
                whole(*wv.shape),
                whole(tokens, 128),
                whole(tokens, 128),
                whole(*tables[2].shape),
                whole(*tables[3].shape),
                whole(*ct.shape),
                whole(*st.shape),
                pl.BlockSpec((1, tokens, 128), lambda t, slot, valid: (t, 0, 0)),
                whole(tokens, 128),
                whole(tokens, GROUPS * 256),
                whole(tokens, GROUPS * 256),
                whole(tokens, 128),
            ],
            out_specs=[
                pl.BlockSpec((1, tokens, width), lambda t, slot, valid: (slot[t], 0, 0)),
                whole(width, tokens),
                whole(*wk.shape),
                whole(*wv.shape),
            ],
            scratch_shapes=[
                pltpu.VMEM((HEADS, tokens, 256), BF16),
                pltpu.VMEM((HEADS, tokens, 256), BF16),
                pltpu.VMEM((GROUPS, tokens, 256), BF16),
                pltpu.VMEM((HEADS, HEAD_DIM, tokens), BF16),
                pltpu.VMEM((GROUPS, tokens, 256), BF16),
                pltpu.VMEM((HEADS, HEAD_DIM, tokens), F32),
                pltpu.VMEM((tokens, 256), F32),
                pltpu.VMEM((tokens, 256), F32),
                pltpu.VMEM((tokens, width), F32),
                pltpu.VMEM(wk.shape, F32),
                pltpu.VMEM(wv.shape, F32),
            ],
        ),
        compiler_params=pltpu.CompilerParams(
            dimension_semantics=("arbitrary",), vmem_limit_bytes=VMEM_BIG
        ),
        name="attention_backward",
    )(
        slots, valid, own, blocks, wq, wk, wkt, wv, *tables, ct, st, key_features,
        query_features, grad_heads, heads, lse,
    )


def rotary_groups(weight):
    rows = weight.shape[0]
    split = weight.reshape(rows, GROUPS, GROUP, 2, HALF).transpose(1, 0, 3, 2, 4)
    split = split.reshape(GROUPS, rows, 2, GROUP * HALF)
    split = jnp.pad(split, ((0, 0), (0, 0), (0, 0), (0, 128 - GROUP * HALF)))
    return split.reshape(GROUPS, rows, 256)


def from_rotary_groups(grouped):
    rows = grouped.shape[1]
    split = grouped.reshape(GROUPS, rows, 2, 128)[..., : GROUP * HALF]
    split = split.reshape(GROUPS, rows, 2, GROUP, HALF).transpose(1, 0, 3, 2, 4)
    return split.reshape(rows, HEADS * HEAD_DIM)


def value_groups(weight):
    rows = weight.shape[0]
    split = weight.reshape(rows, GROUPS, GROUP * HEAD_DIM).transpose(1, 0, 2)
    return jnp.pad(split, ((0, 0), (0, 0), (0, 256 - GROUP * HEAD_DIM)))


def from_value_groups(grouped):
    rows = grouped.shape[1]
    return grouped[..., : GROUP * HEAD_DIM].transpose(1, 0, 2).reshape(rows, HEADS * HEAD_DIM)


def padded_rows(weight):
    split = weight.reshape(GROUPS, GROUP * HEAD_DIM, weight.shape[1])
    split = jnp.pad(split, ((0, 0), (0, 256 - GROUP * HEAD_DIM), (0, 0)))
    return split.reshape(GROUPS * 256, weight.shape[1])


def from_padded_rows(grouped):
    split = grouped.reshape(GROUPS, 256, grouped.shape[1])[:, : GROUP * HEAD_DIM]
    return split.reshape(HEADS * HEAD_DIM, grouped.shape[1])


def shards(
    x_embed,
    doc_ids,
    owners,
    row_ids,
    table,
    ngram_weight,
    stream_gain,
    query_weight,
    key_weight,
    value_weight,
    out_weight,
    mixer_gain,
    gate_weight,
    up_weight,
    down_weight,
    feed_gain,
    cotangent,
):
    tokens = x_embed.shape[1]
    seq_count = lax.axis_size("seq")
    shard_count = lax.axis_size("shard")
    owner_count = seq_count * shard_count
    capacity = max(2, 4 * tokens // owner_count)
    score_scale = HEAD_DIM ** (-0.5)
    gathered = (
        lax.all_gather(ngram_weight, "shard", axis=0, tiled=True),
        lax.all_gather(stream_gain, "shard", axis=0, tiled=True),
        lax.all_gather(query_weight, "shard", axis=0, tiled=True),
        lax.all_gather(key_weight, "shard", axis=0, tiled=True),
        lax.all_gather(value_weight, "shard", axis=0, tiled=True),
        lax.all_gather(out_weight, "shard", axis=0, tiled=True),
        lax.all_gather(mixer_gain, "shard", axis=0, tiled=True),
        lax.all_gather(gate_weight, "shard", axis=0, tiled=True),
        lax.all_gather(up_weight, "shard", axis=0, tiled=True),
        lax.all_gather(down_weight, "shard", axis=0, tiled=True),
        lax.all_gather(feed_gain, "shard", axis=0, tiled=True),
    )
    (
        full_ngram,
        full_stream_gain,
        full_query,
        full_key,
        full_value,
        full_out,
        full_mixer_gain,
        full_gate,
        full_up,
        full_down,
        full_feed_gain,
    ) = gathered
    gain_stream = full_stream_gain.astype(jnp.float32)
    gain_mixer = full_mixer_gain.astype(jnp.float32)
    gain_feed = full_feed_gain.astype(jnp.float32)
    flat_owner = owners.reshape(-1)
    flat_row = row_ids.reshape(-1)
    request_count = flat_owner.shape[0]
    one_hot = (flat_owner[:, None] == jnp.arange(owner_count, dtype=jnp.int32)[None, :]).astype(
        jnp.bfloat16
    )
    earlier = (jnp.arange(request_count)[:, None] > jnp.arange(request_count)[None, :]).astype(
        jnp.bfloat16
    )
    before = jnp.dot(earlier, one_hot, preferred_element_type=jnp.float32)
    rank_index = jnp.sum(before * one_hot, axis=1).astype(jnp.int32)
    slot_index = flat_owner * capacity + rank_index
    request = jnp.full((owner_count * capacity,), -1, jnp.int32).at[slot_index].set(flat_row)
    asked_rows = lax.all_to_all(
        lax.all_to_all(
            request.reshape(seq_count, shard_count, capacity),
            "seq",
            split_axis=0,
            concat_axis=0,
            tiled=True,
        ),
        "shard",
        split_axis=1,
        concat_axis=1,
        tiled=True,
    )
    present = asked_rows >= 0
    found_rows = jnp.take(table, jnp.maximum(asked_rows, 0).reshape(-1), axis=0)
    found_rows = jnp.where(present.reshape(-1)[:, None], found_rows, jnp.zeros_like(found_rows))
    answer = lax.all_to_all(
        lax.all_to_all(
            found_rows.reshape(seq_count, shard_count, capacity, -1),
            "seq",
            split_axis=0,
            concat_axis=0,
            tiled=True,
        ),
        "shard",
        split_axis=1,
        concat_axis=1,
        tiled=True,
    )
    picked = jnp.take(answer.reshape(owner_count * capacity, -1), slot_index, axis=0).reshape(
        tokens, -1
    )
    inputs = x_embed[0].astype(jnp.float32)
    embedded = jnp.dot(picked, full_ngram, preferred_element_type=jnp.float32)
    stream = inputs + embedded
    residual, unit_zero, inverse_zero = norm_parts(stream, gain_stream)
    normed_one, unit_one, inverse_one = norm_parts(residual, gain_mixer)
    mixer_in = normed_one.astype(jnp.bfloat16)
    my_index = lax.axis_index("seq")
    reach_count = min((min(DOC_MAX, tokens * seq_count) + tokens - 2) // tokens, seq_count - 1)
    steps = reach_count + 1
    sources = my_index - jnp.arange(steps, dtype=jnp.int32)
    valid = (sources >= 0).astype(jnp.int32)
    levels = my_index // 4 - sources // 4
    slots = jnp.where(sources >= 0, levels * 4 + sources % 4, SLOTS)
    all_docs = lax.all_gather(doc_ids[0], "seq", axis=0)
    step_docs = jnp.take(all_docs, jnp.maximum(sources, 0), axis=0)
    lane = jnp.arange(128, dtype=jnp.int32)
    doc_lane = (lane >= DOC_LANE) & (lane < DOC_LANE + DOC_FEATURES)
    lse_lane = (lane >= LSE_LANE) & (lane < LSE_LANE + 3)
    same = step_docs[:, :, None] == (lane - DOC_LANE)[None, None, :]
    key_features = ((same & doc_lane) | lse_lane).astype(BF16)
    same_own = doc_ids[0][:, None] == (lane - DOC_LANE)[None, :]
    query_features = jnp.where(doc_lane & ~same_own, -FAR, 0.0).astype(BF16)
    theta, lane_theta, cos_row, sin_row = lane_tables(tokens)
    starts = (sources * tokens).astype(F32)
    block_rows = jnp.pad(starts, (0, 16 - steps))[:, None] * lane_theta[None, :]
    tables = (cos_row, sin_row, jnp.cos(block_rows), jnp.sin(block_rows))
    turned_block = starts[:, None, None] * theta[None, :, None]
    cos_block, sin_block = jnp.cos(turned_block), jnp.sin(turned_block)
    turned_row = theta[:, None] * jnp.arange(tokens, dtype=F32)[None, :]
    cos_turn, sin_turn = jnp.cos(turned_row)[None], jnp.sin(turned_row)[None]
    turned = (
        cos_block * cos_turn - sin_block * sin_turn,
        sin_block * cos_turn + cos_block * sin_turn,
    )
    features = (key_features, query_features)
    query_groups = rotary_groups(full_query)
    key_groups = rotary_groups(full_key)
    value_turned = jnp.pad(
        full_value.T.reshape(HEADS, HEAD_DIM, -1), ((0, 0), (0, VROWS - HEAD_DIM), (0, 0))
    ).reshape(GROUPS, GROUP * VROWS, -1)
    key_turned = full_key.T.reshape(GROUPS, GROUP * HEAD_DIM, -1)
    value_grouped = value_groups(full_value)
    out_rows = padded_rows(full_out)
    blocks = halo_gather(mixer_in, seq_count // 4)
    mixed_full, log_sum = attention_forward(
        mixer_in, blocks, slots, valid, (query_groups, key_groups, value_turned), tables, features
    )
    heads_low = mixed_full.astype(BF16)
    mixer_out = jnp.dot(heads_low, out_rows, preferred_element_type=jnp.float32)
    middle = residual + mixer_out
    normed_two, unit_two, inverse_two = norm_parts(middle, gain_feed)
    feed_in = normed_two.astype(jnp.bfloat16)
    gate_rows = jnp.dot(feed_in, full_gate, preferred_element_type=jnp.float32)
    up_rows = jnp.dot(feed_in, full_up, preferred_element_type=jnp.float32)
    sigmoid = jax.nn.sigmoid(gate_rows)
    hidden = (gate_rows * sigmoid * up_rows).astype(jnp.bfloat16)
    feed_out = jnp.dot(hidden, full_down, preferred_element_type=jnp.float32)
    result = middle + feed_out
    mixed = result.astype(jnp.bfloat16)[None]
    energies = lax.psum(
        (jnp.sum(stream * stream), jnp.sum(mixer_out * mixer_out), jnp.sum(feed_out * feed_out)),
        ("seq", "shard"),
    )
    entry_count = owner_count * tokens * stream.shape[1]
    stream_rms = jnp.sqrt(energies[0] / entry_count)
    mixer_rms = jnp.sqrt(energies[1] / entry_count)
    feed_rms = jnp.sqrt(energies[2] / entry_count)
    grad_result = cotangent[0].astype(jnp.float32)
    grad_feed = cotangent[0]
    grad_down = jnp.einsum("tf,td->fd", hidden, grad_feed, preferred_element_type=jnp.float32)
    grad_hidden = jnp.einsum("td,fd->tf", grad_feed, full_down, preferred_element_type=jnp.float32)
    grad_gate_rows = (grad_hidden * up_rows * sigmoid * (1.0 + gate_rows * (1.0 - sigmoid))).astype(
        jnp.bfloat16
    )
    grad_up_rows = (grad_hidden * gate_rows * sigmoid).astype(jnp.bfloat16)
    grad_gate = jnp.einsum("td,tf->df", feed_in, grad_gate_rows, preferred_element_type=jnp.float32)
    grad_up = jnp.einsum("td,tf->df", feed_in, grad_up_rows, preferred_element_type=jnp.float32)
    grad_feed_in = jnp.einsum(
        "tf,df->td", grad_gate_rows, full_gate, preferred_element_type=jnp.float32
    ) + jnp.einsum("tf,df->td", grad_up_rows, full_up, preferred_element_type=jnp.float32)
    back_two, grad_feed_gain = norm_back(grad_feed_in, unit_two, inverse_two, gain_feed)
    grad_middle = grad_result + back_two
    grad_mixer = grad_middle.astype(jnp.bfloat16)
    grad_out = from_padded_rows(
        jnp.einsum("te,td->ed", heads_low, grad_mixer, preferred_element_type=jnp.float32)
    )
    grad_heads = jnp.einsum(
        "td,ed->te", grad_mixer, out_rows, preferred_element_type=jnp.float32
    ).astype(jnp.bfloat16)
    parts, grad_query_turned, grad_key_groups, grad_value_groups = attention_backward(
        mixer_in,
        blocks,
        slots,
        valid,
        (query_groups, key_groups, key_turned, value_grouped),
        tables,
        turned,
        features,
        grad_heads,
        mixed_full,
        log_sum,
    )
    grad_key = from_rotary_groups(grad_key_groups)
    grad_value = from_value_groups(grad_value_groups)
    grad_mixer_in = halo_reduce(parts, seq_count // 4) + jnp.einsum(
        "et,de->td", grad_query_turned, full_query, preferred_element_type=jnp.float32
    )
    grad_query = jnp.einsum(
        "td,et->de", mixer_in, grad_query_turned, preferred_element_type=jnp.float32
    )
    back_one, grad_mixer_gain = norm_back(grad_mixer_in, unit_one, inverse_one, gain_mixer)
    grad_residual = grad_middle + back_one
    back_zero, grad_stream_gain = norm_back(grad_residual, unit_zero, inverse_zero, gain_stream)
    grad_input = back_zero[None]
    grad_embed = back_zero.astype(jnp.bfloat16)
    grad_ngram = jnp.einsum("ti,to->io", picked, grad_embed, preferred_element_type=jnp.float32)
    grad_picked = (
        jnp.einsum("to,io->ti", grad_embed, full_ngram, preferred_element_type=jnp.float32)
        .astype(jnp.bfloat16)
        .reshape(request_count, -1)
    )
    outgoing = (
        jnp.zeros((owner_count * capacity, grad_picked.shape[1]), jnp.bfloat16)
        .at[slot_index]
        .set(grad_picked)
    )
    incoming = lax.all_to_all(
        lax.all_to_all(
            outgoing.reshape(seq_count, shard_count, capacity, -1),
            "seq",
            split_axis=0,
            concat_axis=0,
            tiled=True,
        ),
        "shard",
        split_axis=1,
        concat_axis=1,
        tiled=True,
    )
    incoming = (
        jnp.where(present[..., None], incoming, jnp.zeros_like(incoming))
        .reshape(owner_count * capacity, -1)
        .astype(jnp.float32)
    )
    grad_table = (
        jnp.zeros(table.shape, jnp.float32).at[jnp.maximum(asked_rows, 0).reshape(-1)].add(incoming)
    )
    shares = (
        lax.psum_scatter(
            grad_ngram.astype(jnp.bfloat16), "shard", scatter_dimension=0, tiled=True
        ).astype(jnp.float32),
        lax.psum_scatter(
            grad_stream_gain.astype(jnp.bfloat16), "shard", scatter_dimension=0, tiled=True
        ).astype(jnp.float32),
        lax.psum_scatter(
            grad_query.astype(jnp.bfloat16), "shard", scatter_dimension=0, tiled=True
        ).astype(jnp.float32),
        lax.psum_scatter(
            grad_key.astype(jnp.bfloat16), "shard", scatter_dimension=0, tiled=True
        ).astype(jnp.float32),
        lax.psum_scatter(
            grad_value.astype(jnp.bfloat16), "shard", scatter_dimension=0, tiled=True
        ).astype(jnp.float32),
        lax.psum_scatter(
            grad_out.astype(jnp.bfloat16), "shard", scatter_dimension=0, tiled=True
        ).astype(jnp.float32),
        lax.psum_scatter(
            grad_mixer_gain.astype(jnp.bfloat16), "shard", scatter_dimension=0, tiled=True
        ).astype(jnp.float32),
        lax.psum_scatter(
            grad_gate.astype(jnp.bfloat16), "shard", scatter_dimension=0, tiled=True
        ).astype(jnp.float32),
        lax.psum_scatter(
            grad_up.astype(jnp.bfloat16), "shard", scatter_dimension=0, tiled=True
        ).astype(jnp.float32),
        lax.psum_scatter(
            grad_down.astype(jnp.bfloat16), "shard", scatter_dimension=0, tiled=True
        ).astype(jnp.float32),
        lax.psum_scatter(
            grad_feed_gain.astype(jnp.bfloat16), "shard", scatter_dimension=0, tiled=True
        ).astype(jnp.float32),
    )
    totals = lax.psum(
        (
            shares[0],
            shares[1],
            shares[2],
            shares[3],
            shares[4],
            shares[5],
            shares[6],
            shares[7],
            shares[8],
            shares[9],
            shares[10],
        ),
        "seq",
    )
    return (
        mixed,
        grad_input,
        stream_rms,
        mixer_rms,
        feed_rms,
        grad_table,
        totals[0],
        totals[1],
        totals[2],
        totals[3],
        totals[4],
        totals[5],
        totals[6],
        totals[7],
        totals[8],
        totals[9],
        totals[10],
    )


def solution(mesh):
    return jax.shard_map(
        shards,
        mesh=mesh,
        in_specs=(
            P("shard", "seq", None),
            P("shard", "seq"),
            P("shard", "seq", None),
            P("shard", "seq", None),
            P(("seq", "shard"), None),
            P("shard", None),
            P("shard"),
            P("shard", None),
            P("shard", None),
            P("shard", None),
            P("shard", None),
            P("shard"),
            P("shard", None),
            P("shard", None),
            P("shard", None),
            P("shard"),
            P("shard", "seq", None),
        ),
        out_specs=(
            P("shard", "seq", None),
            P("shard", "seq", None),
            P(),
            P(),
            P(),
            P(("seq", "shard"), None),
            P("shard", None),
            P("shard"),
            P("shard", None),
            P("shard", None),
            P("shard", None),
            P("shard", None),
            P("shard"),
            P("shard", None),
            P("shard", None),
            P("shard", None),
            P("shard"),
        ),
        check_vma=False,
    )
```

```python
import functools

import jax
import jax.numpy as jnp
import numpy as np
from jax import lax
from jax.experimental import pallas as pl
from jax.experimental.pallas import tpu as pltpu
from jax.sharding import PartitionSpec as P

HEADS = 12
HEAD_DIM = 64
DOC_MAX = 4096
DOC_FEATURES = 16

EPSILON = 1e-06
ROPE_BASE = 500000.0
LOG2E = 1.4426950408889634
LN2 = 0.6931471805599453
FAR = 1073741824.0

GROUP = 3
GROUPS = HEADS // GROUP
HALF = HEAD_DIM // 2
VROWS = 80
SLOTS = 12
DOC_LANE = 96
LSE_LANE = 112
DELTA_LANE = 192

F32 = jnp.float32
BF16 = jnp.bfloat16
VMEM_BIG = 64000000


def nt(a, b):
    return lax.dot_general(a, b, (((1,), (1,)), ((), ())), preferred_element_type=F32)


def nn(a, b):
    return jnp.dot(a, b, preferred_element_type=F32)


def tn(a, b):
    return lax.dot_general(a, b, (((0,), (0,)), ((), ())), preferred_element_type=F32)


def norm_parts(field, gain_row):
    inverse = lax.rsqrt(jnp.mean(field * field, axis=-1, keepdims=True) + EPSILON)
    unit_rows = field * inverse
    return (unit_rows * gain_row, unit_rows, inverse)


def norm_back(gradient, unit_rows, inverse, gain_row):
    scaled = gradient * gain_row
    back_rows = inverse * (
        scaled - unit_rows * jnp.mean(scaled * unit_rows, axis=-1, keepdims=True)
    )
    return (back_rows, jnp.sum(gradient * unit_rows, axis=0))


def exchange_kernel(seq_count, shard_count, shared, *refs):
    count = len(shared)
    srcs, dsts = refs[:count], refs[count : 2 * count]
    send_sem, recv_sem, local_sem = refs[2 * count :]
    total = seq_count * shard_count
    me = lax.axis_index("seq") * shard_count + lax.axis_index("shard")
    barrier = pltpu.get_barrier_semaphore()

    def place(target):
        return {"seq": target // shard_count, "shard": target % shard_count}

    def greet(step, carry):
        pl.semaphore_signal(
            barrier,
            inc=1,
            device_id=place(lax.rem(me + step, total)),
            device_id_type=pl.DeviceIdType.MESH,
        )
        return carry

    lax.fori_loop(1, total, greet, 0)
    local = []
    for p in range(count):
        own = srcs[p] if shared[p] else srcs[p].at[me]
        local.append(pltpu.make_async_copy(own, dsts[p].at[me], local_sem.at[p]))
        local[p].start()
    pl.semaphore_wait(barrier, total - 1)

    def send(step, carry):
        target = lax.rem(me + step, total)
        for p in range(count):
            pltpu.make_async_remote_copy(
                src_ref=srcs[p] if shared[p] else srcs[p].at[target],
                dst_ref=dsts[p].at[me],
                send_sem=send_sem.at[p],
                recv_sem=recv_sem.at[p],
                device_id=place(target),
                device_id_type=pl.DeviceIdType.MESH,
            ).start()
        return carry

    lax.fori_loop(1, total, send, 0)
    for p in range(count):
        local[p].wait()
        others = dsts[p].at[pl.ds(0, total - 1)]
        every = pltpu.make_async_remote_copy(
            src_ref=others,
            dst_ref=others,
            send_sem=send_sem.at[p],
            recv_sem=recv_sem.at[p],
            device_id=place(lax.rem(me + 1, total)),
            device_id_type=pl.DeviceIdType.MESH,
        )
        every.wait_recv()
        every.wait_send()


def exchange(payloads, shared, collective_id, name):
    seq_count = lax.axis_size("seq")
    shard_count = lax.axis_size("shard")
    total = seq_count * shard_count
    shapes = [
        jax.ShapeDtypeStruct((total,) + (p.shape if whole_one else p.shape[1:]), p.dtype)
        for p, whole_one in zip(payloads, shared)
    ]
    return pl.pallas_call(
        functools.partial(exchange_kernel, seq_count, shard_count, shared),
        out_shape=shapes,
        in_specs=[pl.BlockSpec(memory_space=pltpu.VMEM)] * len(payloads),
        out_specs=[pl.BlockSpec(memory_space=pltpu.VMEM)] * len(payloads),
        scratch_shapes=[pltpu.SemaphoreType.DMA((len(payloads),))] * 3,
        compiler_params=pltpu.CompilerParams(collective_id=collective_id, has_side_effects=True),
        name=name,
    )(*payloads)


CHUNKS = 2


def remote(src, dst, sems, kind, chunk, target):
    return pltpu.make_async_remote_copy(
        src_ref=src,
        dst_ref=dst,
        send_sem=sems[0].at[kind, chunk],
        recv_sem=sems[1].at[kind, chunk],
        device_id={"seq": target},
        device_id_type=pl.DeviceIdType.MESH,
    )


def greet(me, group_count):
    barrier = pltpu.get_barrier_semaphore()
    group = me // 4
    mine = me % 4
    peers = (group * 4 + (mine + 2) % 4, group * 4 + mine + 1 - 2 * (mine % 2))
    for peer in peers:
        pl.semaphore_signal(
            barrier, inc=1, device_id={"seq": peer}, device_id_type=pl.DeviceIdType.MESH
        )
    up = group + 1 < group_count
    down = group > 0

    @pl.when(up)
    def _():
        pl.semaphore_signal(
            barrier, inc=1, device_id={"seq": me + 4}, device_id_type=pl.DeviceIdType.MESH
        )

    @pl.when(down)
    def _():
        pl.semaphore_signal(
            barrier, inc=1, device_id={"seq": me - 4}, device_id_type=pl.DeviceIdType.MESH
        )

    pl.semaphore_wait(barrier, 2 + up.astype(jnp.int32) + down.astype(jnp.int32))


def gather_kernel(group_count, own_ref, out_ref, send_sem, recv_sem, local_sem):
    me = lax.axis_index("seq")
    group = me // 4
    mine = me % 4
    core = mine % 2
    far = mine // 2
    over = (mine + 2) % 4
    partner = mine + 1 - 2 * core
    over_id = group * 4 + over
    partner_id = group * 4 + partner
    rows = own_ref.shape[0] // CHUNKS
    sems = (send_sem, recv_sem)
    has_one = group >= 1
    has_two = group >= 2
    up = group + 1 < group_count
    greet(me, group_count)

    def part(ref, chunk):
        return ref.at[pl.ds(chunk * rows, rows)]

    def slot(level, pos, chunk):
        return out_ref.at[level * 4 + pos, pl.ds(chunk * rows, rows)]

    def own_send(kind, level, target, chunk):
        return remote(part(own_ref, chunk), slot(level, mine, chunk), sems, kind, chunk, target)

    def relay(kind, level, pos, to_level, target, chunk):
        return remote(slot(level, pos, chunk), slot(to_level, pos, chunk), sems, kind, chunk, target)

    moves = {
        "z1": lambda c: own_send(0, 1, me + 4, c),
        "x0": lambda c: own_send(1, 0, over_id, c),
        "c0": lambda c: own_send(2, 0, partner_id, c),
        "c0b": lambda c: relay(3, 0, over, 0, partner_id, c),
        "z2": lambda c: relay(4, 1, mine, 2, me + 4, c),
        "x1": lambda c: relay(5, 1, mine, 1, over_id, c),
        "c1a": lambda c: relay(6, 1, mine, 1, partner_id, c),
        "c1b": lambda c: relay(7, 1, over, 1, partner_id, c),
        "x2": lambda c: relay(8, 2, mine, 2, over_id, c),
        "c2a": lambda c: relay(9, 2, mine, 2, partner_id, c),
        "c2b": lambda c: relay(10, 2, over, 2, partner_id, c),
    }
    sends = {
        "z1": up,
        "x0": far == 0,
        "c0": core == 0,
        "c0b": far == 1,
        "z2": has_one & up,
        "x1": has_one,
        "c1a": has_one,
        "c1b": has_one,
        "x2": has_two & (far == 1),
        "c2a": has_two & (core == 1),
        "c2b": has_two & (far == 0),
    }
    receives = {
        "z1": has_one,
        "x0": far == 1,
        "c0": core == 1,
        "c0b": far == 1,
        "z2": has_two,
        "x1": has_one,
        "c1a": has_one,
        "c1b": has_one,
        "x2": has_two & (far == 0),
        "c2a": has_two & (core == 0),
        "c2b": has_two & (far == 0),
    }

    def start(name, chunk):
        @pl.when(sends[name])
        def _():
            moves[name](chunk).start()

    def take(name, chunk):
        @pl.when(receives[name])
        def _():
            moves[name](chunk).wait_recv()

    def finish(name, chunk):
        @pl.when(sends[name])
        def _():
            moves[name](chunk).wait_send()

    every = range(CHUNKS)
    for chunk in every:
        for name in ("z1", "x0", "c0"):
            start(name, chunk)
    local = pltpu.make_async_copy(own_ref, out_ref.at[mine], local_sem)
    local.start()
    for chunk in every:
        take("z1", chunk)
        for name in ("z2", "x1", "c1a"):
            start(name, chunk)
        take("x0", chunk)
        start("c0b", chunk)
    for chunk in every:
        take("x1", chunk)
        start("c1b", chunk)
        take("z2", chunk)
        start("x2", chunk)
        start("c2a", chunk)
    for chunk in every:
        take("x2", chunk)
        start("c2b", chunk)
    for chunk in every:
        for name in ("c0", "c0b", "c1a", "c1b", "c2a", "c2b"):
            take(name, chunk)
    local.wait()
    for chunk in every:
        for name in moves:
            finish(name, chunk)


def halo_gather(own, group_count):
    tokens, width = own.shape
    return pl.pallas_call(
        functools.partial(gather_kernel, group_count),
        out_shape=jax.ShapeDtypeStruct((SLOTS + 1, tokens, width), own.dtype),
        in_specs=[pl.BlockSpec(memory_space=pltpu.VMEM)],
        out_specs=pl.BlockSpec(memory_space=pl.ANY),
        scratch_shapes=[
            pltpu.SemaphoreType.DMA((11, CHUNKS)),
            pltpu.SemaphoreType.DMA((11, CHUNKS)),
            pltpu.SemaphoreType.DMA,
        ],
        compiler_params=pltpu.CompilerParams(collective_id=1, has_side_effects=True),
        name="halo_gather",
    )(own)


def reduce_kernel(
    group_count, part_ref, out_ref, work_ref, got_ref, send_sem, recv_sem, local_sem
):
    me = lax.axis_index("seq")
    group = me // 4
    mine = me % 4
    core = mine % 2
    far = mine // 2
    over = (mine + 2) % 4
    partner = mine + 1 - 2 * core
    partner_over = (partner + 2) % 4
    over_id = group * 4 + over
    partner_id = group * 4 + partner
    rows = out_ref.shape[0] // CHUNKS
    sems = (send_sem, recv_sem)
    has_one = group >= 1
    has_two = group >= 2
    up = group + 1 < group_count

    def load(level):
        four = pl.ds(level * 4, 4)
        return pltpu.make_async_copy(part_ref.at[four], work_ref.at[four], local_sem.at[level])

    for level in (2, 1, 0):
        load(level).start()
    greet(me, group_count)

    def span(chunk):
        return pl.ds(chunk * rows, rows)

    def send(kind, level, pos, target, chunk):
        return remote(
            work_ref.at[level * 4 + pos, span(chunk)],
            got_ref.at[kind, span(chunk)],
            sems,
            kind,
            chunk,
            target,
        )

    moves = {
        "c2o": lambda c: send(0, 2, partner_over, partner_id, c),
        "c2": lambda c: send(1, 2, partner, partner_id, c),
        "c1o": lambda c: send(2, 1, partner_over, partner_id, c),
        "c1": lambda c: send(3, 1, partner, partner_id, c),
        "c0o": lambda c: send(4, 0, partner_over, partner_id, c),
        "c0": lambda c: send(5, 0, partner, partner_id, c),
        "x2": lambda c: send(6, 2, over, over_id, c),
        "x1": lambda c: send(7, 1, over, over_id, c),
        "x0": lambda c: send(8, 0, over, over_id, c),
        "z2": lambda c: send(9, 2, mine, me - 4, c),
        "z1": lambda c: send(10, 1, mine, me - 4, c),
    }
    kinds = {name: kind for kind, name in enumerate(moves)}
    sends = {
        "c2o": has_two & (far == 0),
        "c2": has_two & (core == 0),
        "c1o": has_one,
        "c1": has_one,
        "c0o": far == 1,
        "c0": core == 1,
        "x2": has_two & (far == 0),
        "x1": has_one,
        "x0": far == 1,
        "z2": has_two,
        "z1": has_one,
    }
    receives = {
        "c2o": has_two & (far == 0),
        "c2": has_two & (core == 1),
        "c1o": has_one,
        "c1": has_one,
        "c0o": far == 1,
        "c0": core == 0,
        "x2": has_two & (far == 1),
        "x1": has_one,
        "x0": far == 0,
        "z2": has_one & up,
        "z1": up,
    }
    lands = {
        "c2o": (2, over),
        "c2": (2, mine),
        "c1o": (1, over),
        "c1": (1, mine),
        "c0o": (0, over),
        "c0": (0, mine),
        "x2": (2, mine),
        "x1": (1, mine),
        "x0": (0, mine),
        "z2": (1, mine),
        "z1": (0, mine),
    }

    def start(name, chunk):
        @pl.when(sends[name])
        def _():
            moves[name](chunk).start()

    def absorb(name, chunk):
        @pl.when(receives[name])
        def _():
            moves[name](chunk).wait_recv()
            level, pos = lands[name]
            at = level * 4 + pos
            total = work_ref[at, span(chunk), :].astype(F32) + got_ref[
                kinds[name], span(chunk), :
            ].astype(F32)
            work_ref[at, span(chunk), :] = total.astype(BF16)

    every = range(CHUNKS)
    for level in (2, 1, 0):
        load(level).wait()
        for name in (f"c{level}o", f"c{level}"):
            for chunk in every:
                start(name, chunk)
    for level in (2, 1, 0):
        for chunk in every:
            absorb(f"c{level}o", chunk)
            start(f"x{level}", chunk)
    for chunk in every:
        absorb("c2", chunk)
        absorb("x2", chunk)
        start("z2", chunk)
    for chunk in every:
        absorb("c1", chunk)
        absorb("x1", chunk)
        absorb("z2", chunk)
        start("z1", chunk)
    for chunk in every:
        absorb("c0", chunk)
        absorb("x0", chunk)
        absorb("z1", chunk)
        out_ref[span(chunk), :] = work_ref[mine, span(chunk), :].astype(F32)
    for name in moves:
        for chunk in every:

            @pl.when(sends[name])
            def _():
                moves[name](chunk).wait_send()


def halo_reduce(parts, group_count):
    slots, tokens, width = parts.shape
    return pl.pallas_call(
        functools.partial(reduce_kernel, group_count),
        out_shape=jax.ShapeDtypeStruct((tokens, width), F32),
        in_specs=[pl.BlockSpec(memory_space=pl.ANY)],
        out_specs=pl.BlockSpec(memory_space=pltpu.VMEM),
        scratch_shapes=[
            pltpu.VMEM((SLOTS, tokens, width), BF16),
            pltpu.VMEM((11, tokens, width), BF16),
            pltpu.SemaphoreType.DMA((11, CHUNKS)),
            pltpu.SemaphoreType.DMA((11, CHUNKS)),
            pltpu.SemaphoreType.DMA((3,)),
        ],
        compiler_params=pltpu.CompilerParams(
            collective_id=2, has_side_effects=True, vmem_limit_bytes=VMEM_BIG
        ),
        name="halo_reduce",
    )(parts)


def lane_tables(tokens):
    theta = ROPE_BASE ** (-2.0 * jnp.arange(HALF, dtype=F32) / HEAD_DIM)
    lanes = jnp.concatenate([theta] * GROUP + [jnp.zeros((128 - GROUP * HALF,), F32)])
    angle = jnp.arange(tokens, dtype=F32)[:, None] * lanes[None, :]
    return theta, lanes, jnp.cos(angle), jnp.sin(angle)


def rotate(pair, cosine, sine):
    first, second = pair[:, :128], pair[:, 128:]
    return first * cosine - second * sine, second * cosine + first * sine


def block_angles(step, cos_row, sin_row, cos_block, sin_block):
    c_row, s_row = cos_row[...], sin_row[...]
    c_blk, s_blk = cos_block[pl.ds(step, 1), :], sin_block[pl.ds(step, 1), :]
    return c_row * c_blk - s_row * s_blk, s_row * c_blk + c_row * s_blk


def head_lanes(shape, start, width):
    lane = lax.broadcasted_iota(jnp.int32, shape, 1)
    return (lane >= start) & (lane < start + width)


def forward_kernel(
    slot_ref, valid_ref, own_ref, x_ref, wq_ref, wk_ref, wv_ref, cr_ref, sr_ref, cb_ref, sb_ref,
    kf_ref, qf_ref, out_ref, lse_ref, qm_ref, kb_ref, vt_ref, acc_ref, top_ref,
):
    step = pl.program_id(0)
    tokens = own_ref.shape[0]

    @pl.when(step == 0)
    def _():
        cosine, sine = block_angles(0, cr_ref, sr_ref, cb_ref, sb_ref)
        features = qf_ref[...].astype(F32)

        def one_group(g, carry):
            first, second = rotate(nn(own_ref[...], wq_ref[g]), cosine, sine)
            for hh in range(GROUP):
                mask = head_lanes((tokens, 128), hh * HALF, HALF)
                scale = LOG2E * HEAD_DIM**-0.5
                qm_ref[g * GROUP + hh, :, :128] = (
                    jnp.where(mask, first * scale, features).astype(BF16)
                )
                qm_ref[g * GROUP + hh, :, 128:] = (
                    jnp.where(mask, second * scale, 0.0).astype(BF16)
                )
            return carry

        lax.fori_loop(0, GROUPS, one_group, 0)
        top_ref[...] = jnp.full_like(top_ref, -FAR * FAR)
        acc_ref[...] = jnp.zeros_like(acc_ref)

    @pl.when(valid_ref[step] > 0)
    def _():
        x = x_ref[0]
        cosine, sine = block_angles(step, cr_ref, sr_ref, cb_ref, sb_ref)
        features = kf_ref[0].astype(F32)

        def keys(g, carry):
            first, second = rotate(nn(x_ref[0], wk_ref[g]), cosine, sine)
            kb_ref[g, :, :128] = (first + features).astype(BF16)
            kb_ref[g, :, 128:] = second.astype(BF16)
            values = nt(wv_ref[g], x_ref[0])
            row = lax.broadcasted_iota(jnp.int32, values.shape, 0) % VROWS
            values = jnp.where(row == HEAD_DIM, 1.0, values).astype(BF16)
            for hh in range(GROUP):
                vt_ref[g * GROUP + hh] = values[hh * VROWS : (hh + 1) * VROWS]
            return carry

        lax.fori_loop(0, GROUPS, keys, 0)

        def attend(causal):
            def one_group(g, carry):
                for hh in range(GROUP):
                    h = g * GROUP + hh
                    scores = nt(kb_ref[g], qm_ref[h])
                    if causal:
                        key = lax.broadcasted_iota(jnp.int32, scores.shape, 0)
                        query = lax.broadcasted_iota(jnp.int32, scores.shape, 1)
                        scores = jnp.where(key <= query, scores, -FAR)
                    old = top_ref[h]
                    new = jnp.maximum(old, jnp.max(scores, axis=0, keepdims=True))
                    prob = jnp.exp2(scores - new).astype(BF16)
                    fade = jnp.exp2(old - new)
                    acc_ref[h] = acc_ref[h] * fade + nn(vt_ref[h], prob)
                    top_ref[h] = new
                return carry

            lax.fori_loop(0, GROUPS, one_group, 0)

        @pl.when(step == 0)
        def _():
            attend(True)

        @pl.when(step > 0)
        def _():
            attend(False)

    @pl.when(step == pl.num_programs(0) - 1)
    def _():
        lses = []
        for g in range(GROUPS):
            parts = []
            for h in range(g * GROUP, (g + 1) * GROUP):
                total = acc_ref[h, HEAD_DIM : HEAD_DIM + 1, :]
                parts.append(acc_ref[h, :HEAD_DIM, :] / total)
                lses.append(top_ref[h] + jnp.log2(total))
            parts.append(jnp.zeros((256 - GROUP * HEAD_DIM, tokens), F32))
            out_ref[:, g * 256 : (g + 1) * 256] = jnp.concatenate(parts, axis=0).T
        lses.append(jnp.zeros((128 - HEADS, tokens), F32))
        lse_ref[...] = jnp.concatenate(lses, axis=0).T


def whole(*shape):
    return pl.BlockSpec(shape, lambda *_: (0,) * len(shape), pipeline_mode=pl.Buffered(1))


def attention_forward(own, blocks, slots, valid, weights, tables, features):
    tokens, width = own.shape
    steps = slots.shape[0]
    key_features, query_features = features
    wq, wk, wv = weights
    return pl.pallas_call(
        forward_kernel,
        out_shape=(
            jax.ShapeDtypeStruct((tokens, GROUPS * 256), F32),
            jax.ShapeDtypeStruct((tokens, 128), F32),
        ),
        grid_spec=pltpu.PrefetchScalarGridSpec(
            num_scalar_prefetch=2,
            grid=(steps,),
            in_specs=[
                whole(tokens, width),
                pl.BlockSpec((1, tokens, width), lambda t, slot, valid: (slot[t], 0, 0)),
                whole(*wq.shape),
                whole(*wk.shape),
                whole(*wv.shape),
                whole(tokens, 128),
                whole(tokens, 128),
                whole(*tables[2].shape),
                whole(*tables[3].shape),
                pl.BlockSpec((1, tokens, 128), lambda t, slot, valid: (t, 0, 0)),
                whole(tokens, 128),
            ],
            out_specs=[whole(tokens, GROUPS * 256), whole(tokens, 128)],
            scratch_shapes=[
                pltpu.VMEM((HEADS, tokens, 256), BF16),
                pltpu.VMEM((GROUPS, tokens, 256), BF16),
                pltpu.VMEM((HEADS, VROWS, tokens), BF16),
                pltpu.VMEM((HEADS, VROWS, tokens), F32),
                pltpu.VMEM((HEADS, 1, tokens), F32),
            ],
        ),
        compiler_params=pltpu.CompilerParams(
            dimension_semantics=("arbitrary",), vmem_limit_bytes=VMEM_BIG
        ),
        cost_estimate=pl.CostEstimate(
            flops=70_000_000_000, bytes_accessed=10_000_000, transcendentals=0
        ),
        name="attention_forward",
    )(slots, valid, own, blocks, wq, wk, wv, *tables, key_features, query_features)


def split_bf16(column):
    high = column.astype(BF16).astype(F32)
    return high, column - high


def backward_kernel(
    slot_ref, valid_ref, own_ref, x_ref, wq_ref, wk_ref, wkt_ref, wv_ref, cr_ref, sr_ref, cb_ref,
    sb_ref, ct_ref, st_ref, kf_ref, qf_ref, go_ref, heads_ref, lse_ref, gx_ref, dq_ref, dwk_ref,
    dwv_ref, qb_ref, gm_ref, kb_ref, kt_ref, vb_ref, dqt_ref, dk_ref, dv_ref, gxa_ref, wka_ref,
    wva_ref,
):
    step = pl.program_id(0)
    tokens = own_ref.shape[0]

    @pl.when(step == 0)
    def _():
        cosine, sine = block_angles(0, cr_ref, sr_ref, cb_ref, sb_ref)
        features = qf_ref[...].astype(F32)

        def one_group(g, carry):
            first, second = rotate(nn(own_ref[...], wq_ref[g]), cosine, sine)
            lane = lax.broadcasted_iota(jnp.int32, (tokens, 128), 1)
            wide = lax.broadcasted_iota(jnp.int32, (tokens, 256), 1)
            lanes = pl.ds(pl.multiple_of(g * 256, 256), 256)
            grads = go_ref[:, lanes].astype(F32)
            products = grads * heads_ref[:, lanes]
            for hh in range(GROUP):
                h = g * GROUP + hh
                lse = jnp.sum(jnp.where(lane == h, lse_ref[...], 0.0), axis=1, keepdims=True)
                own = head_lanes((tokens, 256), hh * HEAD_DIM, HEAD_DIM)
                delta = jnp.sum(jnp.where(own, products, 0.0), axis=1, keepdims=True)
                lse_one, rest = split_bf16(lse)
                lse_two, lse_three = split_bf16(rest)
                mask = head_lanes((tokens, 128), hh * HALF, HALF)
                scale = LOG2E * HEAD_DIM**-0.5
                tile = jnp.where(mask, first * scale, features)
                tile = jnp.where(lane == LSE_LANE, -lse_one, tile)
                tile = jnp.where(lane == LSE_LANE + 1, -lse_two, tile)
                tile = jnp.where(lane == LSE_LANE + 2, -lse_three, tile)
                qb_ref[h, :, :128] = tile.astype(BF16)
                qb_ref[h, :, 128:] = jnp.where(mask, second * scale, 0.0).astype(BF16)
                delta_one, delta_two = split_bf16(delta)
                tile = jnp.where(own, grads, 0.0)
                tile = jnp.where(wide == DELTA_LANE, -delta_one, tile)
                tile = jnp.where(wide == DELTA_LANE + 1, -delta_two, tile)
                gm_ref[h] = tile.astype(BF16)
            return carry

        lax.fori_loop(0, GROUPS, one_group, 0)
        dqt_ref[...] = jnp.zeros_like(dqt_ref)
        wka_ref[...] = jnp.zeros_like(wka_ref)
        wva_ref[...] = jnp.zeros_like(wva_ref)

    @pl.when(valid_ref[step] > 0)
    def _():
        cosine, sine = block_angles(step, cr_ref, sr_ref, cb_ref, sb_ref)
        features = kf_ref[0].astype(F32)

        def keys(g, carry):
            first, second = rotate(nn(x_ref[0], wk_ref[g]), cosine, sine)
            kb_ref[g, :, :128] = (first + features).astype(BF16)
            kb_ref[g, :, 128:] = second.astype(BF16)
            values = nn(x_ref[0], wv_ref[g])
            wide = lax.broadcasted_iota(jnp.int32, values.shape, 1)
            ones = (wide == DELTA_LANE) | (wide == DELTA_LANE + 1)
            vb_ref[g] = jnp.where(ones, 1.0, values).astype(BF16)
            turned = nt(wkt_ref[g], x_ref[0])
            for hh in range(GROUP):
                upper = turned[hh * HEAD_DIM : hh * HEAD_DIM + HALF]
                lower = turned[hh * HEAD_DIM + HALF : (hh + 1) * HEAD_DIM]
                c_row, s_row = ct_ref[step], st_ref[step]
                kt_ref[g * GROUP + hh, :HALF] = (upper * c_row - lower * s_row).astype(BF16)
                kt_ref[g * GROUP + hh, HALF:] = (lower * c_row + upper * s_row).astype(BF16)
            return carry

        lax.fori_loop(0, GROUPS, keys, 0)

        def grads(causal):
            def one_group(g, carry):
                for hh in range(GROUP):
                    h = g * GROUP + hh
                    prob = jnp.exp2(nt(kb_ref[g], qb_ref[h]))
                    if causal:
                        key = lax.broadcasted_iota(jnp.int32, prob.shape, 0)
                        query = lax.broadcasted_iota(jnp.int32, prob.shape, 1)
                        prob = jnp.where(key <= query, prob, 0.0)
                    grad = (prob * nt(vb_ref[g], gm_ref[h])).astype(BF16)
                    prob = prob.astype(BF16)
                    value_part = nn(prob, gm_ref[h])
                    key_part = nn(grad, qb_ref[h])
                    if hh == 0:
                        dv_ref[...] = value_part
                        dk_ref[...] = key_part
                    else:
                        dv_ref[...] += value_part
                        dk_ref[...] += key_part
                    dqt_ref[h] += nn(kt_ref[h], grad)
                first, second = rotate(dk_ref[...] * LN2, cosine, -sine)
                pad = head_lanes((tokens, 128), 0, GROUP * HALF)
                key_rows = jnp.concatenate(
                    [jnp.where(pad, first, 0.0), jnp.where(pad, second, 0.0)], axis=1
                ).astype(BF16)
                keep = head_lanes((tokens, 256), 0, GROUP * HEAD_DIM)
                value_rows = jnp.where(keep, dv_ref[...], 0.0).astype(BF16)
                wka_ref[g] += tn(x_ref[0], key_rows)
                wva_ref[g] += tn(x_ref[0], value_rows)
                gxa_ref[...] += nt(key_rows, wk_ref[g]) + nt(value_rows, wv_ref[g])
                return carry

            gxa_ref[...] = jnp.zeros_like(gxa_ref)
            lax.fori_loop(0, GROUPS, one_group, 0)
            gx_ref[0] = gxa_ref[...].astype(BF16)

        @pl.when(step == 0)
        def _():
            grads(True)

        @pl.when(step > 0)
        def _():
            grads(False)

    @pl.when(step == pl.num_programs(0) - 1)
    def _():
        for h in range(HEADS):
            upper = dqt_ref[h, :HALF, :] * HEAD_DIM**-0.5
            lower = dqt_ref[h, HALF:, :] * HEAD_DIM**-0.5
            c_row, s_row = ct_ref[0], st_ref[0]
            dq_ref[h * HEAD_DIM : h * HEAD_DIM + HALF, :] = (
                upper * c_row + lower * s_row
            ).astype(BF16)
            dq_ref[h * HEAD_DIM + HALF : (h + 1) * HEAD_DIM, :] = (
                lower * c_row - upper * s_row
            ).astype(BF16)
        dwk_ref[...] = wka_ref[...].astype(BF16)
        dwv_ref[...] = wva_ref[...].astype(BF16)


def attention_backward(
    own, blocks, slots, valid, weights, tables, turned, features, grad_heads, heads, lse
):
    tokens, width = own.shape
    steps = slots.shape[0]
    key_features, query_features = features
    wq, wk, wkt, wv = weights
    ct, st = turned
    return pl.pallas_call(
        backward_kernel,
        out_shape=(
            jax.ShapeDtypeStruct((SLOTS + 1, tokens, width), BF16),
            jax.ShapeDtypeStruct((width, tokens), BF16),
            jax.ShapeDtypeStruct(wk.shape, BF16),
            jax.ShapeDtypeStruct(wv.shape, BF16),
        ),
        grid_spec=pltpu.PrefetchScalarGridSpec(
            num_scalar_prefetch=2,
            grid=(steps,),
            in_specs=[
                whole(tokens, width),
                pl.BlockSpec((1, tokens, width), lambda t, slot, valid: (slot[t], 0, 0)),
                whole(*wq.shape),
                whole(*wk.shape),
                whole(*wkt.shape),
                whole(*wv.shape),
                whole(tokens, 128),
                whole(tokens, 128),
                whole(*tables[2].shape),
                whole(*tables[3].shape),
                whole(*ct.shape),
                whole(*st.shape),
                pl.BlockSpec((1, tokens, 128), lambda t, slot, valid: (t, 0, 0)),
                whole(tokens, 128),
                whole(tokens, GROUPS * 256),
                whole(tokens, GROUPS * 256),
                whole(tokens, 128),
            ],
            out_specs=[
                pl.BlockSpec((1, tokens, width), lambda t, slot, valid: (slot[t], 0, 0)),
                whole(width, tokens),
                whole(*wk.shape),
                whole(*wv.shape),
            ],
            scratch_shapes=[
                pltpu.VMEM((HEADS, tokens, 256), BF16),
                pltpu.VMEM((HEADS, tokens, 256), BF16),
                pltpu.VMEM((GROUPS, tokens, 256), BF16),
                pltpu.VMEM((HEADS, HEAD_DIM, tokens), BF16),
                pltpu.VMEM((GROUPS, tokens, 256), BF16),
                pltpu.VMEM((HEADS, HEAD_DIM, tokens), F32),
                pltpu.VMEM((tokens, 256), F32),
                pltpu.VMEM((tokens, 256), F32),
                pltpu.VMEM((tokens, width), F32),
                pltpu.VMEM(wk.shape, F32),
                pltpu.VMEM(wv.shape, F32),
            ],
        ),
        compiler_params=pltpu.CompilerParams(
            dimension_semantics=("arbitrary",), vmem_limit_bytes=VMEM_BIG
        ),
        cost_estimate=pl.CostEstimate(
            flops=120_000_000_000, bytes_accessed=20_000_000, transcendentals=0
        ),
        name="attention_backward",
    )(
        slots, valid, own, blocks, wq, wk, wkt, wv, *tables, ct, st, key_features,
        query_features, grad_heads, heads, lse,
    )


def rotary_groups(weight):
    rows = weight.shape[0]
    split = weight.reshape(rows, GROUPS, GROUP, 2, HALF).transpose(1, 0, 3, 2, 4)
    split = split.reshape(GROUPS, rows, 2, GROUP * HALF)
    split = jnp.pad(split, ((0, 0), (0, 0), (0, 0), (0, 128 - GROUP * HALF)))
    return split.reshape(GROUPS, rows, 256)


def from_rotary_groups(grouped):
    rows = grouped.shape[1]
    split = grouped.reshape(GROUPS, rows, 2, 128)[..., : GROUP * HALF]
    split = split.reshape(GROUPS, rows, 2, GROUP, HALF).transpose(1, 0, 3, 2, 4)
    return split.reshape(rows, HEADS * HEAD_DIM)


def value_groups(weight):
    rows = weight.shape[0]
    split = weight.reshape(rows, GROUPS, GROUP * HEAD_DIM).transpose(1, 0, 2)
    return jnp.pad(split, ((0, 0), (0, 0), (0, 256 - GROUP * HEAD_DIM)))


def from_value_groups(grouped):
    rows = grouped.shape[1]
    return grouped[..., : GROUP * HEAD_DIM].transpose(1, 0, 2).reshape(rows, HEADS * HEAD_DIM)


def padded_rows(weight):
    split = weight.reshape(GROUPS, GROUP * HEAD_DIM, weight.shape[1])
    split = jnp.pad(split, ((0, 0), (0, 256 - GROUP * HEAD_DIM), (0, 0)))
    return split.reshape(GROUPS * 256, weight.shape[1])


def from_padded_rows(grouped):
    split = grouped.reshape(GROUPS, 256, grouped.shape[1])[:, : GROUP * HEAD_DIM]
    return split.reshape(HEADS * HEAD_DIM, grouped.shape[1])


def rows_each(rows, seq_count):
    return -(-rows // seq_count)


def lay_rows(grads, seq_count, shard_count):
    laid = []
    for grad in grads:
        width = grad.shape[1]
        own = grad.shape[0] // shard_count
        each = rows_each(own, seq_count)
        block = grad.reshape(shard_count, own, width)
        block = jnp.pad(block, ((0, 0), (0, seq_count * each - own), (0, 0)))
        laid.append(block.reshape(shard_count, seq_count, each, width).transpose(1, 0, 2, 3))
    return laid[0] if len(laid) == 1 else jnp.concatenate(laid, axis=2)


def sum_share(block):
    seq_count, shard_count, rows, width = block.shape
    part = block.reshape(seq_count * shard_count * rows, width)
    part = lax.psum_scatter(part, "seq", scatter_dimension=0, tiled=True)
    part = lax.psum_scatter(part, "shard", scatter_dimension=0, tiled=True)
    whole_part = lax.all_gather(part, "seq", axis=0, tiled=True)
    return whole_part.reshape(seq_count, rows, width)


def take_rows(share, sizes):
    seq_count, _, width = share.shape
    start, taken = 0, []
    for own in sizes:
        each = rows_each(own, seq_count)
        rows = share[:, start : start + each].reshape(seq_count * each, width)[:own]
        taken.append(rows.astype(F32))
        start += each
    return taken


def shards(
    x_embed,
    doc_ids,
    owners,
    row_ids,
    table,
    ngram_weight,
    stream_gain,
    query_weight,
    key_weight,
    value_weight,
    out_weight,
    mixer_gain,
    gate_weight,
    up_weight,
    down_weight,
    feed_gain,
    cotangent,
):
    tokens = x_embed.shape[1]
    seq_count = lax.axis_size("seq")
    shard_count = lax.axis_size("shard")
    owner_count = seq_count * shard_count
    capacity = max(2, 4 * tokens // owner_count)
    score_scale = HEAD_DIM ** (-0.5)
    gathered = (
        lax.all_gather(ngram_weight, "shard", axis=0, tiled=True),
        lax.all_gather(stream_gain, "shard", axis=0, tiled=True),
        lax.all_gather(query_weight, "shard", axis=0, tiled=True),
        lax.all_gather(key_weight, "shard", axis=0, tiled=True),
        lax.all_gather(value_weight, "shard", axis=0, tiled=True),
        lax.all_gather(out_weight, "shard", axis=0, tiled=True),
        lax.all_gather(mixer_gain, "shard", axis=0, tiled=True),
        lax.all_gather(gate_weight, "shard", axis=0, tiled=True),
        lax.all_gather(up_weight, "shard", axis=0, tiled=True),
        lax.all_gather(down_weight, "shard", axis=0, tiled=True),
        lax.all_gather(feed_gain, "shard", axis=0, tiled=True),
    )
    (
        full_ngram,
        full_stream_gain,
        full_query,
        full_key,
        full_value,
        full_out,
        full_mixer_gain,
        full_gate,
        full_up,
        full_down,
        full_feed_gain,
    ) = gathered
    gain_stream = full_stream_gain.astype(jnp.float32)
    gain_mixer = full_mixer_gain.astype(jnp.float32)
    gain_feed = full_feed_gain.astype(jnp.float32)
    flat_owner = owners.reshape(-1)
    flat_row = row_ids.reshape(-1)
    request_count = flat_owner.shape[0]
    one_hot = (flat_owner[:, None] == jnp.arange(owner_count, dtype=jnp.int32)[None, :]).astype(
        jnp.bfloat16
    )
    earlier = (jnp.arange(request_count)[:, None] > jnp.arange(request_count)[None, :]).astype(
        jnp.bfloat16
    )
    before = jnp.dot(earlier, one_hot, preferred_element_type=jnp.float32)
    rank_index = jnp.sum(before * one_hot, axis=1).astype(jnp.int32)
    slot_index = flat_owner * capacity + rank_index
    request = jnp.full((owner_count * capacity,), -1, jnp.int32).at[slot_index].set(flat_row)
    doc_rows = -(-tokens // 128)
    slab = jnp.concatenate(
        [
            jnp.pad(request.reshape(owner_count, 1, capacity), ((0, 0), (0, 0), (0, 128 - capacity))),
            jnp.broadcast_to(doc_ids.reshape(1, doc_rows, 128), (owner_count, doc_rows, 128)),
        ],
        axis=1,
    )
    (slabs,) = exchange((slab,), (False,), 3, "ask")
    asked_rows = slabs[:, 0, :capacity]
    docs_of = slabs[:, 1:].reshape(seq_count, shard_count, tokens)
    all_docs = lax.dynamic_index_in_dim(docs_of, lax.axis_index("shard"), 1, keepdims=False)
    present = asked_rows >= 0
    found_rows = jnp.take(table, jnp.maximum(asked_rows, 0).reshape(-1), axis=0)
    found_rows = jnp.where(present.reshape(-1)[:, None], found_rows, jnp.zeros_like(found_rows))
    (answer,) = exchange((found_rows.reshape(owner_count, capacity, -1),), (False,), 4, "answer")
    picked = jnp.take(answer.reshape(owner_count * capacity, -1), slot_index, axis=0).reshape(
        tokens, -1
    )
    inputs = x_embed[0].astype(jnp.float32)
    embedded = jnp.dot(picked, full_ngram, preferred_element_type=jnp.float32)
    stream = inputs + embedded
    residual, unit_zero, inverse_zero = norm_parts(stream, gain_stream)
    normed_one, unit_one, inverse_one = norm_parts(residual, gain_mixer)
    mixer_in = normed_one.astype(jnp.bfloat16)
    my_index = lax.axis_index("seq")
    reach_count = min((min(DOC_MAX, tokens * seq_count) + tokens - 2) // tokens, seq_count - 1)
    steps = reach_count + 1
    sources = my_index - jnp.arange(steps, dtype=jnp.int32)
    valid = (sources >= 0).astype(jnp.int32)
    levels = my_index // 4 - sources // 4
    slots = jnp.where(sources >= 0, levels * 4 + sources % 4, SLOTS)
    step_docs = jnp.take(all_docs, jnp.maximum(sources, 0), axis=0)
    lane = jnp.arange(128, dtype=jnp.int32)
    doc_lane = (lane >= DOC_LANE) & (lane < DOC_LANE + DOC_FEATURES)
    lse_lane = (lane >= LSE_LANE) & (lane < LSE_LANE + 3)
    same = step_docs[:, :, None] == (lane - DOC_LANE)[None, None, :]
    key_features = ((same & doc_lane) | lse_lane).astype(BF16)
    same_own = doc_ids[0][:, None] == (lane - DOC_LANE)[None, :]
    query_features = jnp.where(doc_lane & ~same_own, -FAR, 0.0).astype(BF16)
    theta, lane_theta, cos_row, sin_row = lane_tables(tokens)
    starts = (sources * tokens).astype(F32)
    block_rows = jnp.pad(starts, (0, 16 - steps))[:, None] * lane_theta[None, :]
    tables = (cos_row, sin_row, jnp.cos(block_rows), jnp.sin(block_rows))
    turned_block = starts[:, None, None] * theta[None, :, None]
    cos_block, sin_block = jnp.cos(turned_block), jnp.sin(turned_block)
    turned_row = theta[:, None] * jnp.arange(tokens, dtype=F32)[None, :]
    cos_turn, sin_turn = jnp.cos(turned_row)[None], jnp.sin(turned_row)[None]
    turned = (
        cos_block * cos_turn - sin_block * sin_turn,
        sin_block * cos_turn + cos_block * sin_turn,
    )
    features = (key_features, query_features)
    query_groups = rotary_groups(full_query)
    key_groups = rotary_groups(full_key)
    value_turned = jnp.pad(
        full_value.T.reshape(HEADS, HEAD_DIM, -1), ((0, 0), (0, VROWS - HEAD_DIM), (0, 0))
    ).reshape(GROUPS, GROUP * VROWS, -1)
    key_turned = full_key.T.reshape(GROUPS, GROUP * HEAD_DIM, -1)
    value_grouped = value_groups(full_value)
    out_rows = padded_rows(full_out)
    blocks = halo_gather(mixer_in, seq_count // 4)
    mixed_full, log_sum = attention_forward(
        mixer_in, blocks, slots, valid, (query_groups, key_groups, value_turned), tables, features
    )
    heads_low = mixed_full.astype(BF16)
    mixer_out = jnp.dot(heads_low, out_rows, preferred_element_type=jnp.float32)
    middle = residual + mixer_out
    normed_two, unit_two, inverse_two = norm_parts(middle, gain_feed)
    feed_in = normed_two.astype(jnp.bfloat16)
    gate_rows = jnp.dot(feed_in, full_gate, preferred_element_type=jnp.float32)
    up_rows = jnp.dot(feed_in, full_up, preferred_element_type=jnp.float32)
    sigmoid = jax.nn.sigmoid(gate_rows)
    hidden = (gate_rows * sigmoid * up_rows).astype(jnp.bfloat16)
    feed_out = jnp.dot(hidden, full_down, preferred_element_type=jnp.float32)
    result = middle + feed_out
    mixed = result.astype(jnp.bfloat16)[None]
    energy = jnp.stack(
        [jnp.sum(stream * stream), jnp.sum(mixer_out * mixer_out), jnp.sum(feed_out * feed_out)]
    )
    energy = jnp.broadcast_to(jnp.pad(energy, (0, 5))[:, None], (8, 128))
    grad_result = cotangent[0].astype(jnp.float32)
    grad_feed = cotangent[0]
    grad_down = jnp.einsum("tf,td->fd", hidden, grad_feed, preferred_element_type=jnp.float32)
    grad_hidden = jnp.einsum("td,fd->tf", grad_feed, full_down, preferred_element_type=jnp.float32)
    grad_gate_rows = (grad_hidden * up_rows * sigmoid * (1.0 + gate_rows * (1.0 - sigmoid))).astype(
        jnp.bfloat16
    )
    grad_up_rows = (grad_hidden * gate_rows * sigmoid).astype(jnp.bfloat16)
    grad_gate = jnp.einsum("td,tf->df", feed_in, grad_gate_rows, preferred_element_type=jnp.float32)
    grad_up = jnp.einsum("td,tf->df", feed_in, grad_up_rows, preferred_element_type=jnp.float32)
    grad_feed_in = jnp.einsum(
        "tf,df->td", grad_gate_rows, full_gate, preferred_element_type=jnp.float32
    ) + jnp.einsum("tf,df->td", grad_up_rows, full_up, preferred_element_type=jnp.float32)
    back_two, grad_feed_gain = norm_back(grad_feed_in, unit_two, inverse_two, gain_feed)
    grad_middle = grad_result + back_two
    grad_mixer = grad_middle.astype(jnp.bfloat16)
    grad_out = from_padded_rows(
        jnp.einsum("te,td->ed", heads_low, grad_mixer, preferred_element_type=jnp.float32)
    )
    grad_heads = jnp.einsum(
        "td,ed->te", grad_mixer, out_rows, preferred_element_type=jnp.float32
    ).astype(jnp.bfloat16)
    early = lay_rows(
        (jnp.concatenate([grad_gate, grad_up], axis=1).astype(BF16),), seq_count, shard_count
    ), lay_rows((grad_down.astype(BF16), grad_out.astype(BF16)), seq_count, shard_count)
    grad_heads, early = lax.optimization_barrier((grad_heads, early))
    early_shares = [sum_share(block) for block in early]
    parts, grad_query_turned, grad_key_groups, grad_value_groups = attention_backward(
        mixer_in,
        blocks,
        slots,
        valid,
        (query_groups, key_groups, key_turned, value_grouped),
        tables,
        turned,
        features,
        grad_heads,
        mixed_full,
        log_sum,
    )
    grad_key = from_rotary_groups(grad_key_groups)
    grad_value = from_value_groups(grad_value_groups)
    grad_mixer_in = halo_reduce(parts, seq_count // 4) + jnp.einsum(
        "et,de->td", grad_query_turned, full_query, preferred_element_type=jnp.float32
    )
    grad_query = jnp.einsum(
        "td,et->de", mixer_in, grad_query_turned, preferred_element_type=jnp.float32
    )
    back_one, grad_mixer_gain = norm_back(grad_mixer_in, unit_one, inverse_one, gain_mixer)
    grad_residual = grad_middle + back_one
    back_zero, grad_stream_gain = norm_back(grad_residual, unit_zero, inverse_zero, gain_stream)
    grad_input = back_zero[None]
    grad_embed = back_zero.astype(jnp.bfloat16)
    grad_ngram = jnp.einsum("ti,to->io", picked, grad_embed, preferred_element_type=jnp.float32)
    grad_picked = (
        jnp.einsum("to,io->ti", grad_embed, full_ngram, preferred_element_type=jnp.float32)
        .astype(jnp.bfloat16)
        .reshape(request_count, -1)
    )
    outgoing = (
        jnp.zeros((owner_count * capacity, grad_picked.shape[1]), jnp.bfloat16)
        .at[slot_index]
        .set(grad_picked)
    )
    incoming, energy_parts = exchange(
        (outgoing.reshape(owner_count, capacity, -1), energy), (False, True), 5, "give_back"
    )
    energies = jnp.sum(energy_parts[:, :, 0], axis=0)
    entry_count = owner_count * tokens * stream.shape[1]
    stream_rms = jnp.sqrt(energies[0] / entry_count)
    mixer_rms = jnp.sqrt(energies[1] / entry_count)
    feed_rms = jnp.sqrt(energies[2] / entry_count)
    incoming = (
        jnp.where(present[..., None], incoming, jnp.zeros_like(incoming))
        .reshape(owner_count * capacity, -1)
        .astype(jnp.float32)
    )
    grad_table = (
        jnp.zeros(table.shape, jnp.float32).at[jnp.maximum(asked_rows, 0).reshape(-1)].add(incoming)
    )
    share_width = stream_gain.shape[0]
    gains = jnp.stack([grad_stream_gain, grad_mixer_gain, grad_feed_gain])
    gains = gains.reshape(3, shard_count, 1, share_width)
    gains = jnp.pad(
        gains, ((0, seq_count - 3), (0, 0), (0, 0), (0, stream.shape[1] - share_width))
    ).astype(BF16)
    late = jnp.concatenate(
        [
            lay_rows(
                (
                    grad_query.astype(BF16),
                    grad_key.astype(BF16),
                    grad_value.astype(BF16),
                    grad_ngram.astype(BF16),
                ),
                seq_count,
                shard_count,
            ),
            gains,
        ],
        axis=2,
    )
    gain_row = late.shape[2] - 1
    late = jnp.pad(late, ((0, 0), (0, 0), (0, -late.shape[2] % 16), (0, 0)))
    late_share = sum_share(late)
    wide = stream.shape[1] // shard_count
    total_gate_up = take_rows(early_shares[0], (wide,))[0]
    total_down, total_out = take_rows(early_shares[1], (down_weight.shape[0], wide))
    total_query, total_key, total_value, total_ngram = take_rows(
        late_share, (wide, wide, wide, ngram_weight.shape[0])
    )
    total_gains = late_share[:3, gain_row, :share_width].astype(F32)
    return (
        mixed,
        grad_input,
        stream_rms,
        mixer_rms,
        feed_rms,
        grad_table,
        total_ngram,
        total_gains[0],
        total_query,
        total_key,
        total_value,
        total_out,
        total_gains[1],
        total_gate_up[:, : gate_weight.shape[1]],
        total_gate_up[:, gate_weight.shape[1] :],
        total_down,
        total_gains[2],
    )


def solution(mesh):
    return jax.shard_map(
        shards,
        mesh=mesh,
        in_specs=(
            P("shard", "seq", None),
            P("shard", "seq"),
            P("shard", "seq", None),
            P("shard", "seq", None),
            P(("seq", "shard"), None),
            P("shard", None),
            P("shard"),
            P("shard", None),
            P("shard", None),
            P("shard", None),
            P("shard", None),
            P("shard"),
            P("shard", None),
            P("shard", None),
            P("shard", None),
            P("shard"),
            P("shard", "seq", None),
        ),
        out_specs=(
            P("shard", "seq", None),
            P("shard", "seq", None),
            P(),
            P(),
            P(),
            P(("seq", "shard"), None),
            P("shard", None),
            P("shard"),
            P("shard", None),
            P("shard", None),
            P("shard", None),
            P("shard", None),
            P("shard"),
            P("shard", None),
            P("shard", None),
            P("shard", None),
            P("shard"),
        ),
        check_vma=False,
    )
```

```python
import functools

import jax
import jax.numpy as jnp
import numpy as np
from jax import lax
from jax.experimental import pallas as pl
from jax.experimental.pallas import tpu as pltpu
from jax.sharding import PartitionSpec as P

HEADS = 12
HEAD_DIM = 64
DOC_MAX = 4096
DOC_FEATURES = 16

EPSILON = 1e-06
ROPE_BASE = 500000.0
LOG2E = 1.4426950408889634
LN2 = 0.6931471805599453
FAR = 1073741824.0

GROUP = 3
GROUPS = HEADS // GROUP
HALF = HEAD_DIM // 2
VROWS = 80
SLOTS = 12
DOC_LANE = 96
LSE_LANE = 112
DELTA_LANE = 192

F32 = jnp.float32
BF16 = jnp.bfloat16
VMEM_BIG = 64000000


def nt(a, b):
    return lax.dot_general(a, b, (((1,), (1,)), ((), ())), preferred_element_type=F32)


def nn(a, b):
    return jnp.dot(a, b, preferred_element_type=F32)


def tn(a, b):
    return lax.dot_general(a, b, (((0,), (0,)), ((), ())), preferred_element_type=F32)


def norm_parts(field, gain_row):
    inverse = lax.rsqrt(jnp.mean(field * field, axis=-1, keepdims=True) + EPSILON)
    unit_rows = field * inverse
    return (unit_rows * gain_row, unit_rows, inverse)


def norm_back(gradient, unit_rows, inverse, gain_row):
    scaled = gradient * gain_row
    back_rows = inverse * (
        scaled - unit_rows * jnp.mean(scaled * unit_rows, axis=-1, keepdims=True)
    )
    return (back_rows, jnp.sum(gradient * unit_rows, axis=0))


def exchange_kernel(seq_count, shard_count, shared, along_seq, *refs):
    count = len(shared)
    srcs, dsts = refs[:count], refs[count : 2 * count]
    send_sem, recv_sem, local_sem = refs[2 * count :]
    total = seq_count if along_seq else seq_count * shard_count
    me = lax.axis_index("seq")
    if not along_seq:
        me = me * shard_count + lax.axis_index("shard")
    barrier = pltpu.get_barrier_semaphore()

    def place(target):
        if along_seq:
            return {"seq": target}
        return {"seq": target // shard_count, "shard": target % shard_count}

    def greet(step, carry):
        pl.semaphore_signal(
            barrier,
            inc=1,
            device_id=place(lax.rem(me + step, total)),
            device_id_type=pl.DeviceIdType.MESH,
        )
        return carry

    lax.fori_loop(1, total, greet, 0)
    local = []
    for p in range(count):
        own = srcs[p] if shared[p] else srcs[p].at[me]
        local.append(pltpu.make_async_copy(own, dsts[p].at[me], local_sem.at[p]))
        local[p].start()
    pl.semaphore_wait(barrier, total - 1)

    def send(step, carry):
        target = lax.rem(me + step, total)
        for p in range(count):
            pltpu.make_async_remote_copy(
                src_ref=srcs[p] if shared[p] else srcs[p].at[target],
                dst_ref=dsts[p].at[me],
                send_sem=send_sem.at[p],
                recv_sem=recv_sem.at[p],
                device_id=place(target),
                device_id_type=pl.DeviceIdType.MESH,
            ).start()
        return carry

    lax.fori_loop(1, total, send, 0)
    for p in range(count):
        local[p].wait()
        others = dsts[p].at[pl.ds(0, total - 1)]
        every = pltpu.make_async_remote_copy(
            src_ref=others,
            dst_ref=others,
            send_sem=send_sem.at[p],
            recv_sem=recv_sem.at[p],
            device_id=place(lax.rem(me + 1, total)),
            device_id_type=pl.DeviceIdType.MESH,
        )
        every.wait_recv()
        every.wait_send()


def exchange(payloads, shared, collective_id, name, along_seq=False):
    seq_count = lax.axis_size("seq")
    shard_count = lax.axis_size("shard")
    total = seq_count if along_seq else seq_count * shard_count
    shapes = [
        jax.ShapeDtypeStruct((total,) + (p.shape if whole_one else p.shape[1:]), p.dtype)
        for p, whole_one in zip(payloads, shared)
    ]
    return pl.pallas_call(
        functools.partial(exchange_kernel, seq_count, shard_count, shared, along_seq),
        out_shape=shapes,
        in_specs=[pl.BlockSpec(memory_space=pltpu.VMEM)] * len(payloads),
        out_specs=[pl.BlockSpec(memory_space=pltpu.VMEM)] * len(payloads),
        scratch_shapes=[pltpu.SemaphoreType.DMA((len(payloads),))] * 3,
        compiler_params=pltpu.CompilerParams(collective_id=collective_id, has_side_effects=True),
        name=name,
    )(*payloads)


CHUNKS = 4


def remote(src, dst, sems, kind, chunk, target):
    return pltpu.make_async_remote_copy(
        src_ref=src,
        dst_ref=dst,
        send_sem=sems[0].at[kind, chunk],
        recv_sem=sems[1].at[kind, chunk],
        device_id={"seq": target},
        device_id_type=pl.DeviceIdType.MESH,
    )


def greet(me, group_count):
    barrier = pltpu.get_barrier_semaphore()
    group = me // 4
    mine = me % 4
    peers = (group * 4 + (mine + 2) % 4, group * 4 + mine + 1 - 2 * (mine % 2))
    for peer in peers:
        pl.semaphore_signal(
            barrier, inc=1, device_id={"seq": peer}, device_id_type=pl.DeviceIdType.MESH
        )
    up = group + 1 < group_count
    down = group > 0

    @pl.when(up)
    def _():
        pl.semaphore_signal(
            barrier, inc=1, device_id={"seq": me + 4}, device_id_type=pl.DeviceIdType.MESH
        )

    @pl.when(down)
    def _():
        pl.semaphore_signal(
            barrier, inc=1, device_id={"seq": me - 4}, device_id_type=pl.DeviceIdType.MESH
        )

    pl.semaphore_wait(barrier, 2 + up.astype(jnp.int32) + down.astype(jnp.int32))


def gather_kernel(group_count, own_ref, out_ref, send_sem, recv_sem, local_sem):
    me = lax.axis_index("seq")
    group = me // 4
    mine = me % 4
    core = mine % 2
    far = mine // 2
    over = (mine + 2) % 4
    partner = mine + 1 - 2 * core
    over_id = group * 4 + over
    partner_id = group * 4 + partner
    rows = own_ref.shape[0] // CHUNKS
    sems = (send_sem, recv_sem)
    has_one = group >= 1
    has_two = group >= 2
    up = group + 1 < group_count
    greet(me, group_count)

    def part(ref, chunk):
        return ref.at[pl.ds(chunk * rows, rows)]

    def slot(level, pos, chunk):
        return out_ref.at[level * 4 + pos, pl.ds(chunk * rows, rows)]

    def own_send(kind, level, target, chunk):
        return remote(part(own_ref, chunk), slot(level, mine, chunk), sems, kind, chunk, target)

    def relay(kind, level, pos, to_level, target, chunk):
        return remote(slot(level, pos, chunk), slot(to_level, pos, chunk), sems, kind, chunk, target)

    moves = {
        "z1": lambda c: own_send(0, 1, me + 4, c),
        "x0": lambda c: own_send(1, 0, over_id, c),
        "c0": lambda c: own_send(2, 0, partner_id, c),
        "c0b": lambda c: relay(3, 0, over, 0, partner_id, c),
        "z2": lambda c: relay(4, 1, mine, 2, me + 4, c),
        "x1": lambda c: relay(5, 1, mine, 1, over_id, c),
        "c1a": lambda c: relay(6, 1, mine, 1, partner_id, c),
        "c1b": lambda c: relay(7, 1, over, 1, partner_id, c),
        "x2": lambda c: relay(8, 2, mine, 2, over_id, c),
        "c2a": lambda c: relay(9, 2, mine, 2, partner_id, c),
        "c2b": lambda c: relay(10, 2, over, 2, partner_id, c),
    }
    sends = {
        "z1": up,
        "x0": far == 0,
        "c0": core == 0,
        "c0b": far == 1,
        "z2": has_one & up,
        "x1": has_one,
        "c1a": has_one,
        "c1b": has_one,
        "x2": has_two & (far == 1),
        "c2a": has_two & (core == 1),
        "c2b": has_two & (far == 0),
    }
    receives = {
        "z1": has_one,
        "x0": far == 1,
        "c0": core == 1,
        "c0b": far == 1,
        "z2": has_two,
        "x1": has_one,
        "c1a": has_one,
        "c1b": has_one,
        "x2": has_two & (far == 0),
        "c2a": has_two & (core == 0),
        "c2b": has_two & (far == 0),
    }

    def start(name, chunk):
        @pl.when(sends[name])
        def _():
            moves[name](chunk).start()

    def take(name, chunk):
        @pl.when(receives[name])
        def _():
            moves[name](chunk).wait_recv()

    def finish(name, chunk):
        @pl.when(sends[name])
        def _():
            moves[name](chunk).wait_send()

    every = range(CHUNKS)
    for chunk in every:
        for name in ("z1", "x0", "c0"):
            start(name, chunk)
    local = pltpu.make_async_copy(own_ref, out_ref.at[mine], local_sem)
    local.start()
    for chunk in every:
        take("z1", chunk)
        for name in ("z2", "x1", "c1a"):
            start(name, chunk)
        take("x0", chunk)
        start("c0b", chunk)
    for chunk in every:
        take("x1", chunk)
        start("c1b", chunk)
        take("z2", chunk)
        start("x2", chunk)
        start("c2a", chunk)
    for chunk in every:
        take("x2", chunk)
        start("c2b", chunk)
    for chunk in every:
        for name in ("c0", "c0b", "c1a", "c1b", "c2a", "c2b"):
            take(name, chunk)
    local.wait()
    for chunk in every:
        for name in moves:
            finish(name, chunk)


def halo_gather(own, group_count):
    tokens, width = own.shape
    return pl.pallas_call(
        functools.partial(gather_kernel, group_count),
        out_shape=jax.ShapeDtypeStruct((SLOTS + 1, tokens, width), own.dtype),
        in_specs=[pl.BlockSpec(memory_space=pltpu.VMEM)],
        out_specs=pl.BlockSpec(memory_space=pl.ANY),
        scratch_shapes=[
            pltpu.SemaphoreType.DMA((11, CHUNKS)),
            pltpu.SemaphoreType.DMA((11, CHUNKS)),
            pltpu.SemaphoreType.DMA,
        ],
        compiler_params=pltpu.CompilerParams(collective_id=1, has_side_effects=True),
        name="halo_gather",
    )(own)


def reduce_kernel(
    group_count, part_ref, out_ref, work_ref, got_ref, send_sem, recv_sem, local_sem
):
    me = lax.axis_index("seq")
    group = me // 4
    mine = me % 4
    core = mine % 2
    far = mine // 2
    over = (mine + 2) % 4
    partner = mine + 1 - 2 * core
    partner_over = (partner + 2) % 4
    over_id = group * 4 + over
    partner_id = group * 4 + partner
    rows = out_ref.shape[0] // CHUNKS
    sems = (send_sem, recv_sem)
    has_one = group >= 1
    has_two = group >= 2
    up = group + 1 < group_count

    def load(level):
        four = pl.ds(level * 4, 4)
        return pltpu.make_async_copy(part_ref.at[four], work_ref.at[four], local_sem.at[level])

    for level in (2, 1, 0):
        load(level).start()
    greet(me, group_count)

    def span(chunk):
        return pl.ds(chunk * rows, rows)

    def send(kind, level, pos, target, chunk):
        return remote(
            work_ref.at[level * 4 + pos, span(chunk)],
            got_ref.at[kind, span(chunk)],
            sems,
            kind,
            chunk,
            target,
        )

    moves = {
        "c2o": lambda c: send(0, 2, partner_over, partner_id, c),
        "c2": lambda c: send(1, 2, partner, partner_id, c),
        "c1o": lambda c: send(2, 1, partner_over, partner_id, c),
        "c1": lambda c: send(3, 1, partner, partner_id, c),
        "c0o": lambda c: send(4, 0, partner_over, partner_id, c),
        "c0": lambda c: send(5, 0, partner, partner_id, c),
        "x2": lambda c: send(6, 2, over, over_id, c),
        "x1": lambda c: send(7, 1, over, over_id, c),
        "x0": lambda c: send(8, 0, over, over_id, c),
        "z2": lambda c: send(9, 2, mine, me - 4, c),
        "z1": lambda c: send(10, 1, mine, me - 4, c),
    }
    kinds = {name: kind for kind, name in enumerate(moves)}
    sends = {
        "c2o": has_two & (far == 0),
        "c2": has_two & (core == 0),
        "c1o": has_one,
        "c1": has_one,
        "c0o": far == 1,
        "c0": core == 1,
        "x2": has_two & (far == 0),
        "x1": has_one,
        "x0": far == 1,
        "z2": has_two,
        "z1": has_one,
    }
    receives = {
        "c2o": has_two & (far == 0),
        "c2": has_two & (core == 1),
        "c1o": has_one,
        "c1": has_one,
        "c0o": far == 1,
        "c0": core == 0,
        "x2": has_two & (far == 1),
        "x1": has_one,
        "x0": far == 0,
        "z2": has_one & up,
        "z1": up,
    }
    lands = {
        "c2o": (2, over),
        "c2": (2, mine),
        "c1o": (1, over),
        "c1": (1, mine),
        "c0o": (0, over),
        "c0": (0, mine),
        "x2": (2, mine),
        "x1": (1, mine),
        "x0": (0, mine),
        "z2": (1, mine),
        "z1": (0, mine),
    }

    def start(name, chunk):
        @pl.when(sends[name])
        def _():
            moves[name](chunk).start()

    def absorb(name, chunk):
        @pl.when(receives[name])
        def _():
            moves[name](chunk).wait_recv()
            level, pos = lands[name]
            at = level * 4 + pos
            total = work_ref[at, span(chunk), :].astype(F32) + got_ref[
                kinds[name], span(chunk), :
            ].astype(F32)
            work_ref[at, span(chunk), :] = total.astype(BF16)

    every = range(CHUNKS)
    for level in (2, 1, 0):
        load(level).wait()
        for name in (f"c{level}o", f"c{level}"):
            for chunk in every:
                start(name, chunk)
    for level in (2, 1, 0):
        for chunk in every:
            absorb(f"c{level}o", chunk)
            start(f"x{level}", chunk)
    for chunk in every:
        absorb("c2", chunk)
        absorb("x2", chunk)
        start("z2", chunk)
    for chunk in every:
        absorb("c1", chunk)
        absorb("x1", chunk)
        absorb("z2", chunk)
        start("z1", chunk)
    for chunk in every:
        absorb("c0", chunk)
        absorb("x0", chunk)
        absorb("z1", chunk)
        out_ref[span(chunk), :] = work_ref[mine, span(chunk), :].astype(F32)
    for name in moves:
        for chunk in every:

            @pl.when(sends[name])
            def _():
                moves[name](chunk).wait_send()


def halo_reduce(parts, group_count):
    slots, tokens, width = parts.shape
    return pl.pallas_call(
        functools.partial(reduce_kernel, group_count),
        out_shape=jax.ShapeDtypeStruct((tokens, width), F32),
        in_specs=[pl.BlockSpec(memory_space=pl.ANY)],
        out_specs=pl.BlockSpec(memory_space=pltpu.VMEM),
        scratch_shapes=[
            pltpu.VMEM((SLOTS, tokens, width), BF16),
            pltpu.VMEM((11, tokens, width), BF16),
            pltpu.SemaphoreType.DMA((11, CHUNKS)),
            pltpu.SemaphoreType.DMA((11, CHUNKS)),
            pltpu.SemaphoreType.DMA((3,)),
        ],
        compiler_params=pltpu.CompilerParams(
            collective_id=2, has_side_effects=True, vmem_limit_bytes=VMEM_BIG
        ),
        name="halo_reduce",
    )(parts)


def lane_tables(tokens):
    theta = ROPE_BASE ** (-2.0 * jnp.arange(HALF, dtype=F32) / HEAD_DIM)
    lanes = jnp.concatenate([theta] * GROUP + [jnp.zeros((128 - GROUP * HALF,), F32)])
    angle = jnp.arange(tokens, dtype=F32)[:, None] * lanes[None, :]
    return theta, lanes, jnp.cos(angle), jnp.sin(angle)


def rotate(pair, cosine, sine):
    first, second = pair[:, :128], pair[:, 128:]
    return first * cosine - second * sine, second * cosine + first * sine


def block_angles(step, cos_row, sin_row, cos_block, sin_block):
    c_row, s_row = cos_row[...], sin_row[...]
    c_blk, s_blk = cos_block[pl.ds(step, 1), :], sin_block[pl.ds(step, 1), :]
    return c_row * c_blk - s_row * s_blk, s_row * c_blk + c_row * s_blk


def head_lanes(shape, start, width):
    lane = lax.broadcasted_iota(jnp.int32, shape, 1)
    return (lane >= start) & (lane < start + width)


def forward_kernel(
    slot_ref, valid_ref, own_ref, x_ref, wq_ref, wk_ref, wv_ref, cr_ref, sr_ref, cb_ref, sb_ref,
    kf_ref, qf_ref, out_ref, lse_ref, qm_ref, kb_ref, vt_ref, acc_ref, top_ref,
):
    step = pl.program_id(0)
    tokens = own_ref.shape[0]

    @pl.when(step == 0)
    def _():
        cosine, sine = block_angles(0, cr_ref, sr_ref, cb_ref, sb_ref)
        features = qf_ref[...].astype(F32)

        def one_group(g, carry):
            first, second = rotate(nn(own_ref[...], wq_ref[g]), cosine, sine)
            for hh in range(GROUP):
                mask = head_lanes((tokens, 128), hh * HALF, HALF)
                scale = LOG2E * HEAD_DIM**-0.5
                qm_ref[g * GROUP + hh, :, :128] = (
                    jnp.where(mask, first * scale, features).astype(BF16)
                )
                qm_ref[g * GROUP + hh, :, 128:] = (
                    jnp.where(mask, second * scale, 0.0).astype(BF16)
                )
            return carry

        lax.fori_loop(0, GROUPS, one_group, 0)
        top_ref[...] = jnp.full_like(top_ref, -FAR * FAR)
        acc_ref[...] = jnp.zeros_like(acc_ref)

    @pl.when(valid_ref[step] > 0)
    def _():
        x = x_ref[0]
        cosine, sine = block_angles(step, cr_ref, sr_ref, cb_ref, sb_ref)
        features = kf_ref[0].astype(F32)

        def keys(g, carry):
            first, second = rotate(nn(x_ref[0], wk_ref[g]), cosine, sine)
            kb_ref[g, :, :128] = (first + features).astype(BF16)
            kb_ref[g, :, 128:] = second.astype(BF16)
            values = nt(wv_ref[g], x_ref[0])
            row = lax.broadcasted_iota(jnp.int32, values.shape, 0) % VROWS
            values = jnp.where(row == HEAD_DIM, 1.0, values).astype(BF16)
            for hh in range(GROUP):
                vt_ref[g * GROUP + hh] = values[hh * VROWS : (hh + 1) * VROWS]
            return carry

        lax.fori_loop(0, GROUPS, keys, 0)

        def attend(causal):
            def one_group(g, carry):
                for hh in range(GROUP):
                    h = g * GROUP + hh
                    scores = nt(kb_ref[g], qm_ref[h])
                    if causal:
                        key = lax.broadcasted_iota(jnp.int32, scores.shape, 0)
                        query = lax.broadcasted_iota(jnp.int32, scores.shape, 1)
                        scores = jnp.where(key <= query, scores, -FAR)
                    old = top_ref[h]
                    new = jnp.maximum(old, jnp.max(scores, axis=0, keepdims=True))
                    prob = jnp.exp2(scores - new).astype(BF16)
                    fade = jnp.exp2(old - new)
                    acc_ref[h] = acc_ref[h] * fade + nn(vt_ref[h], prob)
                    top_ref[h] = new
                return carry

            lax.fori_loop(0, GROUPS, one_group, 0)

        @pl.when(step == 0)
        def _():
            attend(True)

        @pl.when(step > 0)
        def _():
            attend(False)

    @pl.when(step == pl.num_programs(0) - 1)
    def _():
        lses = []
        for g in range(GROUPS):
            parts = []
            for h in range(g * GROUP, (g + 1) * GROUP):
                total = acc_ref[h, HEAD_DIM : HEAD_DIM + 1, :]
                parts.append(acc_ref[h, :HEAD_DIM, :] / total)
                lses.append(top_ref[h] + jnp.log2(total))
            parts.append(jnp.zeros((256 - GROUP * HEAD_DIM, tokens), F32))
            out_ref[:, g * 256 : (g + 1) * 256] = jnp.concatenate(parts, axis=0).T
        lses.append(jnp.zeros((128 - HEADS, tokens), F32))
        lse_ref[...] = jnp.concatenate(lses, axis=0).T


def whole(*shape):
    return pl.BlockSpec(shape, lambda *_: (0,) * len(shape), pipeline_mode=pl.Buffered(1))


def attention_forward(own, blocks, slots, valid, weights, tables, features):
    tokens, width = own.shape
    steps = slots.shape[0]
    key_features, query_features = features
    wq, wk, wv = weights
    return pl.pallas_call(
        forward_kernel,
        out_shape=(
            jax.ShapeDtypeStruct((tokens, GROUPS * 256), F32),
            jax.ShapeDtypeStruct((tokens, 128), F32),
        ),
        grid_spec=pltpu.PrefetchScalarGridSpec(
            num_scalar_prefetch=2,
            grid=(steps,),
            in_specs=[
                whole(tokens, width),
                pl.BlockSpec((1, tokens, width), lambda t, slot, valid: (slot[t], 0, 0)),
                whole(*wq.shape),
                whole(*wk.shape),
                whole(*wv.shape),
                whole(tokens, 128),
                whole(tokens, 128),
                whole(*tables[2].shape),
                whole(*tables[3].shape),
                pl.BlockSpec((1, tokens, 128), lambda t, slot, valid: (t, 0, 0)),
                whole(tokens, 128),
            ],
            out_specs=[whole(tokens, GROUPS * 256), whole(tokens, 128)],
            scratch_shapes=[
                pltpu.VMEM((HEADS, tokens, 256), BF16),
                pltpu.VMEM((GROUPS, tokens, 256), BF16),
                pltpu.VMEM((HEADS, VROWS, tokens), BF16),
                pltpu.VMEM((HEADS, VROWS, tokens), F32),
                pltpu.VMEM((HEADS, 1, tokens), F32),
            ],
        ),
        compiler_params=pltpu.CompilerParams(
            dimension_semantics=("arbitrary",), vmem_limit_bytes=VMEM_BIG
        ),
        cost_estimate=pl.CostEstimate(
            flops=70_000_000_000, bytes_accessed=10_000_000, transcendentals=0
        ),
        name="attention_forward",
    )(slots, valid, own, blocks, wq, wk, wv, *tables, key_features, query_features)


def split_bf16(column):
    high = column.astype(BF16).astype(F32)
    return high, column - high


def backward_kernel(
    slot_ref, valid_ref, own_ref, x_ref, wq_ref, wk_ref, wkt_ref, wv_ref, cr_ref, sr_ref, cb_ref,
    sb_ref, ct_ref, st_ref, kf_ref, qf_ref, go_ref, heads_ref, lse_ref, gx_ref, dq_ref, dwk_ref,
    dwv_ref, qb_ref, gm_ref, kb_ref, kt_ref, vb_ref, dqt_ref, dk_ref, dv_ref, gxa_ref, wka_ref,
    wva_ref,
):
    step = pl.program_id(0)
    tokens = own_ref.shape[0]

    @pl.when(step == 0)
    def _():
        cosine, sine = block_angles(0, cr_ref, sr_ref, cb_ref, sb_ref)
        features = qf_ref[...].astype(F32)

        def one_group(g, carry):
            first, second = rotate(nn(own_ref[...], wq_ref[g]), cosine, sine)
            lane = lax.broadcasted_iota(jnp.int32, (tokens, 128), 1)
            wide = lax.broadcasted_iota(jnp.int32, (tokens, 256), 1)
            lanes = pl.ds(pl.multiple_of(g * 256, 256), 256)
            grads = go_ref[:, lanes].astype(F32)
            products = grads * heads_ref[:, lanes]
            for hh in range(GROUP):
                h = g * GROUP + hh
                lse = jnp.sum(jnp.where(lane == h, lse_ref[...], 0.0), axis=1, keepdims=True)
                own = head_lanes((tokens, 256), hh * HEAD_DIM, HEAD_DIM)
                delta = jnp.sum(jnp.where(own, products, 0.0), axis=1, keepdims=True)
                lse_one, rest = split_bf16(lse)
                lse_two, lse_three = split_bf16(rest)
                mask = head_lanes((tokens, 128), hh * HALF, HALF)
                scale = LOG2E * HEAD_DIM**-0.5
                tile = jnp.where(mask, first * scale, features)
                tile = jnp.where(lane == LSE_LANE, -lse_one, tile)
                tile = jnp.where(lane == LSE_LANE + 1, -lse_two, tile)
                tile = jnp.where(lane == LSE_LANE + 2, -lse_three, tile)
                qb_ref[h, :, :128] = tile.astype(BF16)
                qb_ref[h, :, 128:] = jnp.where(mask, second * scale, 0.0).astype(BF16)
                delta_one, delta_two = split_bf16(delta)
                tile = jnp.where(own, grads, 0.0)
                tile = jnp.where(wide == DELTA_LANE, -delta_one, tile)
                tile = jnp.where(wide == DELTA_LANE + 1, -delta_two, tile)
                gm_ref[h] = tile.astype(BF16)
            return carry

        lax.fori_loop(0, GROUPS, one_group, 0)
        dqt_ref[...] = jnp.zeros_like(dqt_ref)
        wka_ref[...] = jnp.zeros_like(wka_ref)
        wva_ref[...] = jnp.zeros_like(wva_ref)

    @pl.when(valid_ref[step] > 0)
    def _():
        cosine, sine = block_angles(step, cr_ref, sr_ref, cb_ref, sb_ref)
        features = kf_ref[0].astype(F32)

        def keys(g, carry):
            first, second = rotate(nn(x_ref[0], wk_ref[g]), cosine, sine)
            kb_ref[g, :, :128] = (first + features).astype(BF16)
            kb_ref[g, :, 128:] = second.astype(BF16)
            values = nn(x_ref[0], wv_ref[g])
            wide = lax.broadcasted_iota(jnp.int32, values.shape, 1)
            ones = (wide == DELTA_LANE) | (wide == DELTA_LANE + 1)
            vb_ref[g] = jnp.where(ones, 1.0, values).astype(BF16)
            turned = nt(wkt_ref[g], x_ref[0])
            for hh in range(GROUP):
                upper = turned[hh * HEAD_DIM : hh * HEAD_DIM + HALF]
                lower = turned[hh * HEAD_DIM + HALF : (hh + 1) * HEAD_DIM]
                c_row, s_row = ct_ref[step], st_ref[step]
                kt_ref[g * GROUP + hh, :HALF] = (upper * c_row - lower * s_row).astype(BF16)
                kt_ref[g * GROUP + hh, HALF:] = (lower * c_row + upper * s_row).astype(BF16)
            return carry

        lax.fori_loop(0, GROUPS, keys, 0)

        def grads(causal):
            def one_group(g, carry):
                for hh in range(GROUP):
                    h = g * GROUP + hh
                    prob = jnp.exp2(nt(kb_ref[g], qb_ref[h]))
                    if causal:
                        key = lax.broadcasted_iota(jnp.int32, prob.shape, 0)
                        query = lax.broadcasted_iota(jnp.int32, prob.shape, 1)
                        prob = jnp.where(key <= query, prob, 0.0)
                    grad = (prob * nt(vb_ref[g], gm_ref[h])).astype(BF16)
                    prob = prob.astype(BF16)
                    value_part = nn(prob, gm_ref[h])
                    key_part = nn(grad, qb_ref[h])
                    if hh == 0:
                        dv_ref[...] = value_part
                        dk_ref[...] = key_part
                    else:
                        dv_ref[...] += value_part
                        dk_ref[...] += key_part
                    dqt_ref[h] += nn(kt_ref[h], grad)
                first, second = rotate(dk_ref[...] * LN2, cosine, -sine)
                pad = head_lanes((tokens, 128), 0, GROUP * HALF)
                key_rows = jnp.concatenate(
                    [jnp.where(pad, first, 0.0), jnp.where(pad, second, 0.0)], axis=1
                ).astype(BF16)
                keep = head_lanes((tokens, 256), 0, GROUP * HEAD_DIM)
                value_rows = jnp.where(keep, dv_ref[...], 0.0).astype(BF16)
                wka_ref[g] += tn(x_ref[0], key_rows)
                wva_ref[g] += tn(x_ref[0], value_rows)
                gxa_ref[...] += nt(key_rows, wk_ref[g]) + nt(value_rows, wv_ref[g])
                return carry

            gxa_ref[...] = jnp.zeros_like(gxa_ref)
            lax.fori_loop(0, GROUPS, one_group, 0)
            gx_ref[0] = gxa_ref[...].astype(BF16)

        @pl.when(step == 0)
        def _():
            grads(True)

        @pl.when(step > 0)
        def _():
            grads(False)

    @pl.when(step == pl.num_programs(0) - 1)
    def _():
        for h in range(HEADS):
            upper = dqt_ref[h, :HALF, :] * HEAD_DIM**-0.5
            lower = dqt_ref[h, HALF:, :] * HEAD_DIM**-0.5
            c_row, s_row = ct_ref[0], st_ref[0]
            dq_ref[h * HEAD_DIM : h * HEAD_DIM + HALF, :] = (
                upper * c_row + lower * s_row
            ).astype(BF16)
            dq_ref[h * HEAD_DIM + HALF : (h + 1) * HEAD_DIM, :] = (
                lower * c_row - upper * s_row
            ).astype(BF16)
        dwk_ref[...] = wka_ref[...].astype(BF16)
        dwv_ref[...] = wva_ref[...].astype(BF16)


def attention_backward(
    own, blocks, slots, valid, weights, tables, turned, features, grad_heads, heads, lse
):
    tokens, width = own.shape
    steps = slots.shape[0]
    key_features, query_features = features
    wq, wk, wkt, wv = weights
    ct, st = turned
    return pl.pallas_call(
        backward_kernel,
        out_shape=(
            jax.ShapeDtypeStruct((SLOTS + 1, tokens, width), BF16),
            jax.ShapeDtypeStruct((width, tokens), BF16),
            jax.ShapeDtypeStruct(wk.shape, BF16),
            jax.ShapeDtypeStruct(wv.shape, BF16),
        ),
        grid_spec=pltpu.PrefetchScalarGridSpec(
            num_scalar_prefetch=2,
            grid=(steps,),
            in_specs=[
                whole(tokens, width),
                pl.BlockSpec((1, tokens, width), lambda t, slot, valid: (slot[t], 0, 0)),
                whole(*wq.shape),
                whole(*wk.shape),
                whole(*wkt.shape),
                whole(*wv.shape),
                whole(tokens, 128),
                whole(tokens, 128),
                whole(*tables[2].shape),
                whole(*tables[3].shape),
                whole(*ct.shape),
                whole(*st.shape),
                pl.BlockSpec((1, tokens, 128), lambda t, slot, valid: (t, 0, 0)),
                whole(tokens, 128),
                whole(tokens, GROUPS * 256),
                whole(tokens, GROUPS * 256),
                whole(tokens, 128),
            ],
            out_specs=[
                pl.BlockSpec((1, tokens, width), lambda t, slot, valid: (slot[t], 0, 0)),
                whole(width, tokens),
                whole(*wk.shape),
                whole(*wv.shape),
            ],
            scratch_shapes=[
                pltpu.VMEM((HEADS, tokens, 256), BF16),
                pltpu.VMEM((HEADS, tokens, 256), BF16),
                pltpu.VMEM((GROUPS, tokens, 256), BF16),
                pltpu.VMEM((HEADS, HEAD_DIM, tokens), BF16),
                pltpu.VMEM((GROUPS, tokens, 256), BF16),
                pltpu.VMEM((HEADS, HEAD_DIM, tokens), F32),
                pltpu.VMEM((tokens, 256), F32),
                pltpu.VMEM((tokens, 256), F32),
                pltpu.VMEM((tokens, width), F32),
                pltpu.VMEM(wk.shape, F32),
                pltpu.VMEM(wv.shape, F32),
            ],
        ),
        compiler_params=pltpu.CompilerParams(
            dimension_semantics=("arbitrary",), vmem_limit_bytes=VMEM_BIG
        ),
        cost_estimate=pl.CostEstimate(
            flops=120_000_000_000, bytes_accessed=20_000_000, transcendentals=0
        ),
        name="attention_backward",
    )(
        slots, valid, own, blocks, wq, wk, wkt, wv, *tables, ct, st, key_features,
        query_features, grad_heads, heads, lse,
    )


def rotary_groups(weight):
    rows = weight.shape[0]
    split = weight.reshape(rows, GROUPS, GROUP, 2, HALF).transpose(1, 0, 3, 2, 4)
    split = split.reshape(GROUPS, rows, 2, GROUP * HALF)
    split = jnp.pad(split, ((0, 0), (0, 0), (0, 0), (0, 128 - GROUP * HALF)))
    return split.reshape(GROUPS, rows, 256)


def from_rotary_groups(grouped):
    rows = grouped.shape[1]
    split = grouped.reshape(GROUPS, rows, 2, 128)[..., : GROUP * HALF]
    split = split.reshape(GROUPS, rows, 2, GROUP, HALF).transpose(1, 0, 3, 2, 4)
    return split.reshape(rows, HEADS * HEAD_DIM)


def value_groups(weight):
    rows = weight.shape[0]
    split = weight.reshape(rows, GROUPS, GROUP * HEAD_DIM).transpose(1, 0, 2)
    return jnp.pad(split, ((0, 0), (0, 0), (0, 256 - GROUP * HEAD_DIM)))


def from_value_groups(grouped):
    rows = grouped.shape[1]
    return grouped[..., : GROUP * HEAD_DIM].transpose(1, 0, 2).reshape(rows, HEADS * HEAD_DIM)


def padded_rows(weight):
    split = weight.reshape(GROUPS, GROUP * HEAD_DIM, weight.shape[1])
    split = jnp.pad(split, ((0, 0), (0, 256 - GROUP * HEAD_DIM), (0, 0)))
    return split.reshape(GROUPS * 256, weight.shape[1])


def from_padded_rows(grouped):
    split = grouped.reshape(GROUPS, 256, grouped.shape[1])[:, : GROUP * HEAD_DIM]
    return split.reshape(HEADS * HEAD_DIM, grouped.shape[1])


TILE = 256


def rows_each(own, seq_count):
    return -(-own // (8 * seq_count)) * 8


def pieces(grouped, seq_count, shard_count):
    groups, rows, _ = grouped.shape
    own = rows // shard_count
    each = rows_each(own, seq_count)
    block = grouped.astype(BF16).reshape(groups, shard_count, own, TILE)
    block = jnp.pad(block, ((0, 0), (0, 0), (0, seq_count * each - own), (0, 0)))
    block = block.reshape(groups, shard_count, seq_count, each, TILE).transpose(2, 1, 0, 3, 4)
    return block.reshape(seq_count, shard_count, groups * each, TILE)


def columns(grad):
    return grad.reshape(grad.shape[0], -1, TILE).transpose(1, 0, 2)


def from_columns(grouped):
    return grouped.transpose(1, 0, 2).reshape(grouped.shape[1], -1)


def sum_pieces(block):
    seq_count, shard_count, rows, _ = block.shape
    flat = block.reshape(seq_count * shard_count * rows, TILE)
    return lax.psum_scatter(flat, ("seq", "shard"), scatter_dimension=0, tiled=True)


def take_pieces(share, sizes, seq_count):
    share = share.reshape(seq_count, -1, TILE)
    start, taken = 0, []
    for groups, own in sizes:
        each = rows_each(own, seq_count)
        part = share[:, start : start + groups * each].reshape(seq_count, groups, each, TILE)
        part = part.transpose(1, 0, 2, 3).reshape(groups, seq_count * each, TILE)[:, :own]
        taken.append(part.astype(F32))
        start += groups * each
    return taken


def shards(
    x_embed,
    doc_ids,
    owners,
    row_ids,
    table,
    ngram_weight,
    stream_gain,
    query_weight,
    key_weight,
    value_weight,
    out_weight,
    mixer_gain,
    gate_weight,
    up_weight,
    down_weight,
    feed_gain,
    cotangent,
):
    tokens = x_embed.shape[1]
    seq_count = lax.axis_size("seq")
    shard_count = lax.axis_size("shard")
    owner_count = seq_count * shard_count
    capacity = max(2, 4 * tokens // owner_count)
    score_scale = HEAD_DIM ** (-0.5)
    gathered = (
        lax.all_gather(query_weight, "shard", axis=0, tiled=True),
        lax.all_gather(key_weight, "shard", axis=0, tiled=True),
        lax.all_gather(value_weight, "shard", axis=0, tiled=True),
        lax.all_gather(out_weight, "shard", axis=0, tiled=True),
        lax.all_gather(gate_weight, "shard", axis=0, tiled=True),
        lax.all_gather(up_weight, "shard", axis=0, tiled=True),
        lax.all_gather(down_weight, "shard", axis=0, tiled=True),
    )
    (
        full_query,
        full_key,
        full_value,
        full_out,
        full_gate,
        full_up,
        full_down,
    ) = gathered
    ngram_rows, width = ngram_weight.shape
    share_width = stream_gain.shape[0]
    own_gains = jnp.pad(
        jnp.stack([stream_gain, mixer_gain, feed_gain]),
        ((0, -(ngram_rows + 3) % 16 + 0), (0, width - share_width)),
    )
    small = lax.all_gather(
        jnp.concatenate([ngram_weight, own_gains], axis=0), "shard", axis=0, tiled=True
    ).reshape(shard_count, -1, width)
    full_ngram = small[:, :ngram_rows].reshape(shard_count * ngram_rows, width)
    full_gains = small[:, ngram_rows : ngram_rows + 3, :share_width].astype(F32)
    gain_stream, gain_mixer, gain_feed = (
        full_gains[:, which].reshape(shard_count * share_width) for which in range(3)
    )
    flat_owner = owners.reshape(-1)
    flat_row = row_ids.reshape(-1)
    request_count = flat_owner.shape[0]
    one_hot = (flat_owner[:, None] == jnp.arange(owner_count, dtype=jnp.int32)[None, :]).astype(
        jnp.bfloat16
    )
    earlier = (jnp.arange(request_count)[:, None] > jnp.arange(request_count)[None, :]).astype(
        jnp.bfloat16
    )
    before = jnp.dot(earlier, one_hot, preferred_element_type=jnp.float32)
    rank_index = jnp.sum(before * one_hot, axis=1).astype(jnp.int32)
    slot_index = flat_owner * capacity + rank_index
    request = jnp.full((owner_count * capacity,), -1, jnp.int32).at[slot_index].set(flat_row)
    doc_rows = -(-tokens // 128)
    slab = jnp.concatenate(
        [
            jnp.pad(request.reshape(owner_count, 1, capacity), ((0, 0), (0, 0), (0, 128 - capacity))),
            jnp.broadcast_to(doc_ids.reshape(1, doc_rows, 128), (owner_count, doc_rows, 128)),
        ],
        axis=1,
    )
    (slabs,) = exchange((slab,), (False,), 3, "ask")
    asked_rows = slabs[:, 0, :capacity]
    docs_of = slabs[:, 1:].reshape(seq_count, shard_count, tokens)
    all_docs = lax.dynamic_index_in_dim(docs_of, lax.axis_index("shard"), 1, keepdims=False)
    present = asked_rows >= 0
    found_rows = jnp.take(table, jnp.maximum(asked_rows, 0).reshape(-1), axis=0)
    found_rows = jnp.where(present.reshape(-1)[:, None], found_rows, jnp.zeros_like(found_rows))
    (answer,) = exchange((found_rows.reshape(owner_count, capacity, -1),), (False,), 4, "answer")
    picked = jnp.take(answer.reshape(owner_count * capacity, -1), slot_index, axis=0).reshape(
        tokens, -1
    )
    inputs = x_embed[0].astype(jnp.float32)
    embedded = jnp.dot(picked, full_ngram, preferred_element_type=jnp.float32)
    stream = inputs + embedded
    residual, unit_zero, inverse_zero = norm_parts(stream, gain_stream)
    normed_one, unit_one, inverse_one = norm_parts(residual, gain_mixer)
    mixer_in = normed_one.astype(jnp.bfloat16)
    my_index = lax.axis_index("seq")
    reach_count = min((min(DOC_MAX, tokens * seq_count) + tokens - 2) // tokens, seq_count - 1)
    steps = reach_count + 1
    sources = my_index - jnp.arange(steps, dtype=jnp.int32)
    valid = (sources >= 0).astype(jnp.int32)
    levels = my_index // 4 - sources // 4
    slots = jnp.where(sources >= 0, levels * 4 + sources % 4, SLOTS)
    step_docs = jnp.take(all_docs, jnp.maximum(sources, 0), axis=0)
    lane = jnp.arange(128, dtype=jnp.int32)
    doc_lane = (lane >= DOC_LANE) & (lane < DOC_LANE + DOC_FEATURES)
    lse_lane = (lane >= LSE_LANE) & (lane < LSE_LANE + 3)
    same = step_docs[:, :, None] == (lane - DOC_LANE)[None, None, :]
    key_features = ((same & doc_lane) | lse_lane).astype(BF16)
    same_own = doc_ids[0][:, None] == (lane - DOC_LANE)[None, :]
    query_features = jnp.where(doc_lane & ~same_own, -FAR, 0.0).astype(BF16)
    theta, lane_theta, cos_row, sin_row = lane_tables(tokens)
    starts = (sources * tokens).astype(F32)
    block_rows = jnp.pad(starts, (0, 16 - steps))[:, None] * lane_theta[None, :]
    tables = (cos_row, sin_row, jnp.cos(block_rows), jnp.sin(block_rows))
    turned_block = starts[:, None, None] * theta[None, :, None]
    cos_block, sin_block = jnp.cos(turned_block), jnp.sin(turned_block)
    turned_row = theta[:, None] * jnp.arange(tokens, dtype=F32)[None, :]
    cos_turn, sin_turn = jnp.cos(turned_row)[None], jnp.sin(turned_row)[None]
    turned = (
        cos_block * cos_turn - sin_block * sin_turn,
        sin_block * cos_turn + cos_block * sin_turn,
    )
    features = (key_features, query_features)
    query_groups = rotary_groups(full_query)
    key_groups = rotary_groups(full_key)
    value_turned = jnp.pad(
        full_value.T.reshape(HEADS, HEAD_DIM, -1), ((0, 0), (0, VROWS - HEAD_DIM), (0, 0))
    ).reshape(GROUPS, GROUP * VROWS, -1)
    key_turned = full_key.T.reshape(GROUPS, GROUP * HEAD_DIM, -1)
    value_grouped = value_groups(full_value)
    out_rows = padded_rows(full_out)
    blocks = halo_gather(mixer_in, seq_count // 4)
    mixed_full, log_sum = attention_forward(
        mixer_in, blocks, slots, valid, (query_groups, key_groups, value_turned), tables, features
    )
    heads_low = mixed_full.astype(BF16)
    mixer_out = jnp.dot(heads_low, out_rows, preferred_element_type=jnp.float32)
    middle = residual + mixer_out
    normed_two, unit_two, inverse_two = norm_parts(middle, gain_feed)
    feed_in = normed_two.astype(jnp.bfloat16)
    gate_rows = jnp.dot(feed_in, full_gate, preferred_element_type=jnp.float32)
    up_rows = jnp.dot(feed_in, full_up, preferred_element_type=jnp.float32)
    sigmoid = jax.nn.sigmoid(gate_rows)
    hidden = (gate_rows * sigmoid * up_rows).astype(jnp.bfloat16)
    feed_out = jnp.dot(hidden, full_down, preferred_element_type=jnp.float32)
    result = middle + feed_out
    mixed = result.astype(jnp.bfloat16)[None]
    energy = jnp.stack(
        [jnp.sum(stream * stream), jnp.sum(mixer_out * mixer_out), jnp.sum(feed_out * feed_out)]
    )
    energy = jnp.broadcast_to(jnp.pad(energy, (0, 5))[:, None], (8, 128))
    grad_result = cotangent[0].astype(jnp.float32)
    grad_feed = cotangent[0]
    grad_down = jnp.einsum("tf,td->fd", hidden, grad_feed, preferred_element_type=jnp.float32)
    grad_hidden = jnp.einsum("td,fd->tf", grad_feed, full_down, preferred_element_type=jnp.float32)
    grad_gate_rows = (grad_hidden * up_rows * sigmoid * (1.0 + gate_rows * (1.0 - sigmoid))).astype(
        jnp.bfloat16
    )
    grad_up_rows = (grad_hidden * gate_rows * sigmoid).astype(jnp.bfloat16)
    grad_gate = jnp.einsum("td,tf->df", feed_in, grad_gate_rows, preferred_element_type=jnp.float32)
    grad_up = jnp.einsum("td,tf->df", feed_in, grad_up_rows, preferred_element_type=jnp.float32)
    grad_feed_in = jnp.einsum(
        "tf,df->td", grad_gate_rows, full_gate, preferred_element_type=jnp.float32
    ) + jnp.einsum("tf,df->td", grad_up_rows, full_up, preferred_element_type=jnp.float32)
    back_two, grad_feed_gain = norm_back(grad_feed_in, unit_two, inverse_two, gain_feed)
    grad_middle = grad_result + back_two
    grad_mixer = grad_middle.astype(jnp.bfloat16)
    grad_out = from_padded_rows(
        jnp.einsum("te,td->ed", heads_low, grad_mixer, preferred_element_type=jnp.float32)
    )
    grad_heads = jnp.einsum(
        "td,ed->te", grad_mixer, out_rows, preferred_element_type=jnp.float32
    ).astype(jnp.bfloat16)
    early = jnp.concatenate(
        [
            pieces(columns(grad.astype(BF16)), seq_count, shard_count)
            for grad in (grad_gate, grad_up, grad_down, grad_out)
        ],
        axis=2,
    )
    grad_heads, early = lax.optimization_barrier((grad_heads, early))
    early_part = sum_pieces(early)
    parts, grad_query_turned, grad_key_groups, grad_value_groups = attention_backward(
        mixer_in,
        blocks,
        slots,
        valid,
        (query_groups, key_groups, key_turned, value_grouped),
        tables,
        turned,
        features,
        grad_heads,
        mixed_full,
        log_sum,
    )
    grad_query = jnp.einsum(
        "td,et->de", mixer_in, grad_query_turned, preferred_element_type=jnp.float32
    )
    late = jnp.concatenate(
        [
            pieces(grouped, seq_count, shard_count)
            for grouped in (columns(grad_query.astype(BF16)), grad_key_groups, grad_value_groups)
        ],
        axis=2,
    )
    parts, late, early_part = lax.optimization_barrier((parts, late, early_part))
    late_part = sum_pieces(late)
    reduced, early_part = lax.optimization_barrier((halo_reduce(parts, seq_count // 4), early_part))
    early_share = lax.all_gather(early_part, "seq", axis=0, tiled=True)
    grad_mixer_in = reduced + jnp.einsum(
        "et,de->td", grad_query_turned, full_query, preferred_element_type=jnp.float32
    )
    back_one, grad_mixer_gain = norm_back(grad_mixer_in, unit_one, inverse_one, gain_mixer)
    grad_residual = grad_middle + back_one
    back_zero, grad_stream_gain = norm_back(grad_residual, unit_zero, inverse_zero, gain_stream)
    grad_input = back_zero[None]
    grad_embed = back_zero.astype(jnp.bfloat16)
    grad_ngram = jnp.einsum("ti,to->io", picked, grad_embed, preferred_element_type=jnp.float32)
    grad_picked = (
        jnp.einsum("to,io->ti", grad_embed, full_ngram, preferred_element_type=jnp.float32)
        .astype(jnp.bfloat16)
        .reshape(request_count, -1)
    )
    outgoing = (
        jnp.zeros((owner_count * capacity, grad_picked.shape[1]), jnp.bfloat16)
        .at[slot_index]
        .set(grad_picked)
    )
    each = -(-ngram_rows // seq_count)
    ngram_pieces = jnp.pad(
        grad_ngram.reshape(shard_count, ngram_rows, width),
        ((0, 0), (0, seq_count * each - ngram_rows), (0, 0)),
    )
    ngram_pieces = ngram_pieces.reshape(shard_count, seq_count, each, width)
    gain_rows = jnp.stack([grad_stream_gain, grad_mixer_gain, grad_feed_gain])
    gain_rows = gain_rows.reshape(3, shard_count, share_width).transpose(1, 0, 2)
    gain_rows = jnp.pad(gain_rows, ((0, 0), (0, -(each + 3) % 16), (0, width - share_width)))
    gain_rows = jnp.broadcast_to(
        gain_rows[:, None], (shard_count, seq_count) + gain_rows.shape[1:]
    )
    small_rows = jnp.concatenate([ngram_pieces, gain_rows], axis=2).astype(BF16)
    small_rows = small_rows.transpose(1, 0, 2, 3).reshape(owner_count, -1, width)
    incoming, small_parts, energy_parts = exchange(
        (outgoing.reshape(owner_count, capacity, -1), small_rows, energy),
        (False, False, True),
        5,
        "give_back",
    )
    incoming, small_parts, energy_parts, late_part = lax.optimization_barrier(
        (incoming, small_parts, energy_parts, late_part)
    )
    late_share = lax.all_gather(late_part, "seq", axis=0, tiled=True)
    small_sum = jnp.sum(small_parts.astype(F32), axis=0)
    total_gains = small_sum[each : each + 3, :share_width]
    (ngram_share,) = exchange((small_sum.astype(BF16),), (True,), 6, "spread", along_seq=True)
    total_ngram = ngram_share[:, :each].reshape(seq_count * each, width)[:ngram_rows].astype(F32)
    energies = jnp.sum(energy_parts[:, :, 0], axis=0)
    entry_count = owner_count * tokens * stream.shape[1]
    stream_rms = jnp.sqrt(energies[0] / entry_count)
    mixer_rms = jnp.sqrt(energies[1] / entry_count)
    feed_rms = jnp.sqrt(energies[2] / entry_count)
    incoming = (
        jnp.where(present[..., None], incoming, jnp.zeros_like(incoming))
        .reshape(owner_count * capacity, -1)
        .astype(jnp.float32)
    )
    grad_table = (
        jnp.zeros(table.shape, jnp.float32).at[jnp.maximum(asked_rows, 0).reshape(-1)].add(incoming)
    )
    wide = share_width
    total_gate, total_up, total_down, total_out = (
        from_columns(total)
        for total in take_pieces(
            early_share,
            (
                (gate_weight.shape[1] // TILE, wide),
                (up_weight.shape[1] // TILE, wide),
                (width // TILE, down_weight.shape[0]),
                (width // TILE, wide),
            ),
            seq_count,
        )
    )
    total_query, total_key, total_value = take_pieces(
        late_share, ((width // TILE, wide), (GROUPS, wide), (GROUPS, wide)), seq_count
    )
    return (
        mixed,
        grad_input,
        stream_rms,
        mixer_rms,
        feed_rms,
        grad_table,
        total_ngram,
        total_gains[0],
        from_columns(total_query),
        from_rotary_groups(total_key),
        from_value_groups(total_value),
        total_out,
        total_gains[1],
        total_gate,
        total_up,
        total_down,
        total_gains[2],
    )


def solution(mesh):
    return jax.shard_map(
        shards,
        mesh=mesh,
        in_specs=(
            P("shard", "seq", None),
            P("shard", "seq"),
            P("shard", "seq", None),
            P("shard", "seq", None),
            P(("seq", "shard"), None),
            P("shard", None),
            P("shard"),
            P("shard", None),
            P("shard", None),
            P("shard", None),
            P("shard", None),
            P("shard"),
            P("shard", None),
            P("shard", None),
            P("shard", None),
            P("shard"),
            P("shard", "seq", None),
        ),
        out_specs=(
            P("shard", "seq", None),
            P("shard", "seq", None),
            P(),
            P(),
            P(),
            P(("seq", "shard"), None),
            P("shard", None),
            P("shard"),
            P("shard", None),
            P("shard", None),
            P("shard", None),
            P("shard", None),
            P("shard"),
            P("shard", None),
            P("shard", None),
            P("shard", None),
            P("shard"),
        ),
        check_vma=False,
    )
```

```python
import functools

import jax
import jax.numpy as jnp
import numpy as np
from jax import lax
from jax.experimental import pallas as pl
from jax.experimental.pallas import tpu as pltpu
from jax.sharding import PartitionSpec as P

HEADS = 12
HEAD_DIM = 64
DOC_MAX = 4096
DOC_FEATURES = 16

EPSILON = 1e-06
ROPE_BASE = 500000.0
LOG2E = 1.4426950408889634
LN2 = 0.6931471805599453
FAR = 1073741824.0

GROUP = 3
GROUPS = HEADS // GROUP
HALF = HEAD_DIM // 2
VROWS = 80
SLOTS = 12
DOC_LANE = 96
LSE_LANE = 112
DELTA_LANE = 192

F32 = jnp.float32
BF16 = jnp.bfloat16
VMEM_BIG = 64000000


def nt(a, b):
    return lax.dot_general(a, b, (((1,), (1,)), ((), ())), preferred_element_type=F32)


def nn(a, b):
    return jnp.dot(a, b, preferred_element_type=F32)


def tn(a, b):
    return lax.dot_general(a, b, (((0,), (0,)), ((), ())), preferred_element_type=F32)


def norm_parts(field, gain_row):
    inverse = lax.rsqrt(jnp.mean(field * field, axis=-1, keepdims=True) + EPSILON)
    unit_rows = field * inverse
    return (unit_rows * gain_row, unit_rows, inverse)


def norm_back(gradient, unit_rows, inverse, gain_row):
    scaled = gradient * gain_row
    back_rows = inverse * (
        scaled - unit_rows * jnp.mean(scaled * unit_rows, axis=-1, keepdims=True)
    )
    return (back_rows, jnp.sum(gradient * unit_rows, axis=0))


def exchange_kernel(seq_count, shard_count, shared, along_seq, *refs):
    count = len(shared)
    srcs, dsts = refs[:count], refs[count : 2 * count]
    send_sem, recv_sem, local_sem = refs[2 * count :]
    total = seq_count if along_seq else seq_count * shard_count
    me = lax.axis_index("seq")
    if not along_seq:
        me = me * shard_count + lax.axis_index("shard")
    barrier = pltpu.get_barrier_semaphore()

    def place(target):
        if along_seq:
            return {"seq": target}
        return {"seq": target // shard_count, "shard": target % shard_count}

    def greet(step, carry):
        pl.semaphore_signal(
            barrier,
            inc=1,
            device_id=place(lax.rem(me + step, total)),
            device_id_type=pl.DeviceIdType.MESH,
        )
        return carry

    lax.fori_loop(1, total, greet, 0)
    local = []
    for p in range(count):
        own = srcs[p] if shared[p] else srcs[p].at[me]
        local.append(pltpu.make_async_copy(own, dsts[p].at[me], local_sem.at[p]))
        local[p].start()
    pl.semaphore_wait(barrier, total - 1)

    def send(step, carry):
        target = lax.rem(me + step, total)
        for p in range(count):
            pltpu.make_async_remote_copy(
                src_ref=srcs[p] if shared[p] else srcs[p].at[target],
                dst_ref=dsts[p].at[me],
                send_sem=send_sem.at[p],
                recv_sem=recv_sem.at[p],
                device_id=place(target),
                device_id_type=pl.DeviceIdType.MESH,
            ).start()
        return carry

    lax.fori_loop(1, total, send, 0)
    for p in range(count):
        local[p].wait()
        others = dsts[p].at[pl.ds(0, total - 1)]
        every = pltpu.make_async_remote_copy(
            src_ref=others,
            dst_ref=others,
            send_sem=send_sem.at[p],
            recv_sem=recv_sem.at[p],
            device_id=place(lax.rem(me + 1, total)),
            device_id_type=pl.DeviceIdType.MESH,
        )
        every.wait_recv()
        every.wait_send()


def exchange(payloads, shared, collective_id, name, along_seq=False):
    seq_count = lax.axis_size("seq")
    shard_count = lax.axis_size("shard")
    total = seq_count if along_seq else seq_count * shard_count
    shapes = [
        jax.ShapeDtypeStruct((total,) + (p.shape if whole_one else p.shape[1:]), p.dtype)
        for p, whole_one in zip(payloads, shared)
    ]
    return pl.pallas_call(
        functools.partial(exchange_kernel, seq_count, shard_count, shared, along_seq),
        out_shape=shapes,
        in_specs=[pl.BlockSpec(memory_space=pltpu.VMEM)] * len(payloads),
        out_specs=[pl.BlockSpec(memory_space=pltpu.VMEM)] * len(payloads),
        scratch_shapes=[pltpu.SemaphoreType.DMA((len(payloads),))] * 3,
        compiler_params=pltpu.CompilerParams(collective_id=collective_id, has_side_effects=True),
        name=name,
    )(*payloads)


CHUNKS = 4


def remote(src, dst, sems, kind, chunk, target):
    return pltpu.make_async_remote_copy(
        src_ref=src,
        dst_ref=dst,
        send_sem=sems[0].at[kind, chunk],
        recv_sem=sems[1].at[kind, chunk],
        device_id={"seq": target},
        device_id_type=pl.DeviceIdType.MESH,
    )


def greet(me, group_count):
    barrier = pltpu.get_barrier_semaphore()
    group = me // 4
    mine = me % 4
    peers = (group * 4 + (mine + 2) % 4, group * 4 + mine + 1 - 2 * (mine % 2))
    for peer in peers:
        pl.semaphore_signal(
            barrier, inc=1, device_id={"seq": peer}, device_id_type=pl.DeviceIdType.MESH
        )
    up = group + 1 < group_count
    down = group > 0

    @pl.when(up)
    def _():
        pl.semaphore_signal(
            barrier, inc=1, device_id={"seq": me + 4}, device_id_type=pl.DeviceIdType.MESH
        )

    @pl.when(down)
    def _():
        pl.semaphore_signal(
            barrier, inc=1, device_id={"seq": me - 4}, device_id_type=pl.DeviceIdType.MESH
        )

    pl.semaphore_wait(barrier, 2 + up.astype(jnp.int32) + down.astype(jnp.int32))


def gather_kernel(group_count, own_ref, out_ref, send_sem, recv_sem, local_sem):
    me = lax.axis_index("seq")
    group = me // 4
    mine = me % 4
    core = mine % 2
    far = mine // 2
    over = (mine + 2) % 4
    partner = mine + 1 - 2 * core
    over_id = group * 4 + over
    partner_id = group * 4 + partner
    rows = own_ref.shape[0] // CHUNKS
    sems = (send_sem, recv_sem)
    has_one = group >= 1
    has_two = group >= 2
    up = group + 1 < group_count
    greet(me, group_count)

    def part(ref, chunk):
        return ref.at[pl.ds(chunk * rows, rows)]

    def slot(level, pos, chunk):
        return out_ref.at[level * 4 + pos, pl.ds(chunk * rows, rows)]

    def own_send(kind, level, target, chunk):
        return remote(part(own_ref, chunk), slot(level, mine, chunk), sems, kind, chunk, target)

    def relay(kind, level, pos, to_level, target, chunk):
        return remote(slot(level, pos, chunk), slot(to_level, pos, chunk), sems, kind, chunk, target)

    moves = {
        "z1": lambda c: own_send(0, 1, me + 4, c),
        "x0": lambda c: own_send(1, 0, over_id, c),
        "c0": lambda c: own_send(2, 0, partner_id, c),
        "c0b": lambda c: relay(3, 0, over, 0, partner_id, c),
        "z2": lambda c: relay(4, 1, mine, 2, me + 4, c),
        "x1": lambda c: relay(5, 1, mine, 1, over_id, c),
        "c1a": lambda c: relay(6, 1, mine, 1, partner_id, c),
        "c1b": lambda c: relay(7, 1, over, 1, partner_id, c),
        "x2": lambda c: relay(8, 2, mine, 2, over_id, c),
        "c2a": lambda c: relay(9, 2, mine, 2, partner_id, c),
        "c2b": lambda c: relay(10, 2, over, 2, partner_id, c),
    }
    sends = {
        "z1": up,
        "x0": far == 0,
        "c0": core == 0,
        "c0b": far == 1,
        "z2": has_one & up,
        "x1": has_one,
        "c1a": has_one,
        "c1b": has_one,
        "x2": has_two & (far == 1),
        "c2a": has_two & (core == 1),
        "c2b": has_two & (far == 0),
    }
    receives = {
        "z1": has_one,
        "x0": far == 1,
        "c0": core == 1,
        "c0b": far == 1,
        "z2": has_two,
        "x1": has_one,
        "c1a": has_one,
        "c1b": has_one,
        "x2": has_two & (far == 0),
        "c2a": has_two & (core == 0),
        "c2b": has_two & (far == 0),
    }

    def start(name, chunk):
        @pl.when(sends[name])
        def _():
            moves[name](chunk).start()

    def take(name, chunk):
        @pl.when(receives[name])
        def _():
            moves[name](chunk).wait_recv()

    def finish(name, chunk):
        @pl.when(sends[name])
        def _():
            moves[name](chunk).wait_send()

    every = range(CHUNKS)
    for chunk in every:
        for name in ("z1", "x0", "c0"):
            start(name, chunk)
    local = pltpu.make_async_copy(own_ref, out_ref.at[mine], local_sem)
    local.start()
    for chunk in every:
        take("z1", chunk)
        for name in ("z2", "x1", "c1a"):
            start(name, chunk)
        take("x0", chunk)
        start("c0b", chunk)
    for chunk in every:
        take("x1", chunk)
        start("c1b", chunk)
        take("z2", chunk)
        start("x2", chunk)
        start("c2a", chunk)
    for chunk in every:
        take("x2", chunk)
        start("c2b", chunk)
    for chunk in every:
        for name in ("c0", "c0b", "c1a", "c1b", "c2a", "c2b"):
            take(name, chunk)
    local.wait()
    for chunk in every:
        for name in moves:
            finish(name, chunk)


def halo_gather(own, group_count):
    tokens, width = own.shape
    return pl.pallas_call(
        functools.partial(gather_kernel, group_count),
        out_shape=jax.ShapeDtypeStruct((SLOTS + 1, tokens, width), own.dtype),
        in_specs=[pl.BlockSpec(memory_space=pltpu.VMEM)],
        out_specs=pl.BlockSpec(memory_space=pl.ANY),
        scratch_shapes=[
            pltpu.SemaphoreType.DMA((11, CHUNKS)),
            pltpu.SemaphoreType.DMA((11, CHUNKS)),
            pltpu.SemaphoreType.DMA,
        ],
        compiler_params=pltpu.CompilerParams(collective_id=1, has_side_effects=True),
        name="halo_gather",
    )(own)


def reduce_kernel(
    group_count, part_ref, out_ref, work_ref, got_ref, send_sem, recv_sem, local_sem
):
    me = lax.axis_index("seq")
    group = me // 4
    mine = me % 4
    core = mine % 2
    far = mine // 2
    over = (mine + 2) % 4
    partner = mine + 1 - 2 * core
    partner_over = (partner + 2) % 4
    over_id = group * 4 + over
    partner_id = group * 4 + partner
    rows = out_ref.shape[0] // CHUNKS
    sems = (send_sem, recv_sem)
    has_one = group >= 1
    has_two = group >= 2
    up = group + 1 < group_count

    def load(level):
        four = pl.ds(level * 4, 4)
        return pltpu.make_async_copy(part_ref.at[four], work_ref.at[four], local_sem.at[level])

    for level in (2, 1, 0):
        load(level).start()
    greet(me, group_count)

    def span(chunk):
        return pl.ds(chunk * rows, rows)

    def send(kind, level, pos, target, chunk):
        return remote(
            work_ref.at[level * 4 + pos, span(chunk)],
            got_ref.at[kind, span(chunk)],
            sems,
            kind,
            chunk,
            target,
        )

    moves = {
        "c2o": lambda c: send(0, 2, partner_over, partner_id, c),
        "c2": lambda c: send(1, 2, partner, partner_id, c),
        "c1o": lambda c: send(2, 1, partner_over, partner_id, c),
        "c1": lambda c: send(3, 1, partner, partner_id, c),
        "c0o": lambda c: send(4, 0, partner_over, partner_id, c),
        "c0": lambda c: send(5, 0, partner, partner_id, c),
        "x2": lambda c: send(6, 2, over, over_id, c),
        "x1": lambda c: send(7, 1, over, over_id, c),
        "x0": lambda c: send(8, 0, over, over_id, c),
        "z2": lambda c: send(9, 2, mine, me - 4, c),
        "z1": lambda c: send(10, 1, mine, me - 4, c),
    }
    kinds = {name: kind for kind, name in enumerate(moves)}
    sends = {
        "c2o": has_two & (far == 0),
        "c2": has_two & (core == 0),
        "c1o": has_one,
        "c1": has_one,
        "c0o": far == 1,
        "c0": core == 1,
        "x2": has_two & (far == 0),
        "x1": has_one,
        "x0": far == 1,
        "z2": has_two,
        "z1": has_one,
    }
    receives = {
        "c2o": has_two & (far == 0),
        "c2": has_two & (core == 1),
        "c1o": has_one,
        "c1": has_one,
        "c0o": far == 1,
        "c0": core == 0,
        "x2": has_two & (far == 1),
        "x1": has_one,
        "x0": far == 0,
        "z2": has_one & up,
        "z1": up,
    }
    lands = {
        "c2o": (2, over),
        "c2": (2, mine),
        "c1o": (1, over),
        "c1": (1, mine),
        "c0o": (0, over),
        "c0": (0, mine),
        "x2": (2, mine),
        "x1": (1, mine),
        "x0": (0, mine),
        "z2": (1, mine),
        "z1": (0, mine),
    }

    def start(name, chunk):
        @pl.when(sends[name])
        def _():
            moves[name](chunk).start()

    def absorb(name, chunk):
        @pl.when(receives[name])
        def _():
            moves[name](chunk).wait_recv()
            level, pos = lands[name]
            at = level * 4 + pos
            total = work_ref[at, span(chunk), :].astype(F32) + got_ref[
                kinds[name], span(chunk), :
            ].astype(F32)
            work_ref[at, span(chunk), :] = total.astype(BF16)

    every = range(CHUNKS)
    for level in (2, 1, 0):
        load(level).wait()
        for name in (f"c{level}o", f"c{level}"):
            for chunk in every:
                start(name, chunk)
    for level in (2, 1, 0):
        for chunk in every:
            absorb(f"c{level}o", chunk)
            start(f"x{level}", chunk)
    for chunk in every:
        absorb("c2", chunk)
        absorb("x2", chunk)
        start("z2", chunk)
    for chunk in every:
        absorb("c1", chunk)
        absorb("x1", chunk)
        absorb("z2", chunk)
        start("z1", chunk)
    for chunk in every:
        absorb("c0", chunk)
        absorb("x0", chunk)
        absorb("z1", chunk)
        out_ref[span(chunk), :] = work_ref[mine, span(chunk), :].astype(F32)
    for name in moves:
        for chunk in every:

            @pl.when(sends[name])
            def _():
                moves[name](chunk).wait_send()


def halo_reduce(parts, group_count):
    slots, tokens, width = parts.shape
    return pl.pallas_call(
        functools.partial(reduce_kernel, group_count),
        out_shape=jax.ShapeDtypeStruct((tokens, width), F32),
        in_specs=[pl.BlockSpec(memory_space=pl.ANY)],
        out_specs=pl.BlockSpec(memory_space=pltpu.VMEM),
        scratch_shapes=[
            pltpu.VMEM((SLOTS, tokens, width), BF16),
            pltpu.VMEM((11, tokens, width), BF16),
            pltpu.SemaphoreType.DMA((11, CHUNKS)),
            pltpu.SemaphoreType.DMA((11, CHUNKS)),
            pltpu.SemaphoreType.DMA((3,)),
        ],
        compiler_params=pltpu.CompilerParams(
            collective_id=2, has_side_effects=True, vmem_limit_bytes=VMEM_BIG
        ),
        name="halo_reduce",
    )(parts)


def lane_tables(tokens):
    theta = ROPE_BASE ** (-2.0 * jnp.arange(HALF, dtype=F32) / HEAD_DIM)
    lanes = jnp.concatenate([theta] * GROUP + [jnp.zeros((128 - GROUP * HALF,), F32)])
    angle = jnp.arange(tokens, dtype=F32)[:, None] * lanes[None, :]
    return theta, lanes, jnp.cos(angle), jnp.sin(angle)


def rotate(pair, cosine, sine):
    first, second = pair[:, :128], pair[:, 128:]
    return first * cosine - second * sine, second * cosine + first * sine


def block_angles(step, cos_row, sin_row, cos_block, sin_block):
    c_row, s_row = cos_row[...], sin_row[...]
    c_blk, s_blk = cos_block[pl.ds(step, 1), :], sin_block[pl.ds(step, 1), :]
    return c_row * c_blk - s_row * s_blk, s_row * c_blk + c_row * s_blk


def head_lanes(shape, start, width):
    lane = lax.broadcasted_iota(jnp.int32, shape, 1)
    return (lane >= start) & (lane < start + width)


def forward_kernel(
    slot_ref, valid_ref, own_ref, x_ref, wq_ref, wk_ref, wv_ref, cr_ref, sr_ref, cb_ref, sb_ref,
    kf_ref, qf_ref, out_ref, lse_ref, kb_ref, qm_ref, vt_ref, acc_ref, top_ref,
):
    step = pl.program_id(0)
    tokens = own_ref.shape[0]

    @pl.when(step == 0)
    def _():
        cosine, sine = block_angles(0, cr_ref, sr_ref, cb_ref, sb_ref)
        features = qf_ref[...].astype(F32)

        def one_group(g, carry):
            first, second = rotate(nn(own_ref[...], wq_ref[g]), cosine, sine)
            for hh in range(GROUP):
                mask = head_lanes((tokens, 128), hh * HALF, HALF)
                scale = LOG2E * HEAD_DIM**-0.5
                qm_ref[g * GROUP + hh, :, :128] = (
                    jnp.where(mask, first * scale, features).astype(BF16)
                )
                qm_ref[g * GROUP + hh, :, 128:] = (
                    jnp.where(mask, second * scale, 0.0).astype(BF16)
                )
            return carry

        lax.fori_loop(0, GROUPS, one_group, 0)
        top_ref[...] = jnp.full_like(top_ref, -FAR * FAR)
        acc_ref[...] = jnp.zeros_like(acc_ref)

    @pl.when(valid_ref[step] > 0)
    def _():
        x = x_ref[0]
        cosine, sine = block_angles(step, cr_ref, sr_ref, cb_ref, sb_ref)
        features = kf_ref[0].astype(F32)

        def keys(g, carry):
            first, second = rotate(nn(x_ref[0], wk_ref[g]), cosine, sine)
            kb_ref[0, g, :, :128] = (first + features).astype(BF16)
            kb_ref[0, g, :, 128:] = second.astype(BF16)
            values = nt(wv_ref[g], x_ref[0])
            row = lax.broadcasted_iota(jnp.int32, values.shape, 0) % VROWS
            values = jnp.where(row == HEAD_DIM, 1.0, values).astype(BF16)
            for hh in range(GROUP):
                vt_ref[g * GROUP + hh] = values[hh * VROWS : (hh + 1) * VROWS]
            return carry

        lax.fori_loop(0, GROUPS, keys, 0)

        def attend(causal):
            def one_group(g, carry):
                for hh in range(GROUP):
                    h = g * GROUP + hh
                    scores = nt(kb_ref[0, g], qm_ref[h])
                    if causal:
                        key = lax.broadcasted_iota(jnp.int32, scores.shape, 0)
                        query = lax.broadcasted_iota(jnp.int32, scores.shape, 1)
                        scores = jnp.where(key <= query, scores, -FAR)
                    old = top_ref[h]
                    new = jnp.maximum(old, jnp.max(scores, axis=0, keepdims=True))
                    prob = jnp.exp2(scores - new).astype(BF16)
                    fade = jnp.exp2(old - new)
                    acc_ref[h] = acc_ref[h] * fade + nn(vt_ref[h], prob)
                    top_ref[h] = new
                return carry

            lax.fori_loop(0, GROUPS, one_group, 0)

        @pl.when(step == 0)
        def _():
            attend(True)

        @pl.when(step > 0)
        def _():
            attend(False)

    @pl.when(step == pl.num_programs(0) - 1)
    def _():
        lses = []
        for g in range(GROUPS):
            parts = []
            for h in range(g * GROUP, (g + 1) * GROUP):
                total = acc_ref[h, HEAD_DIM : HEAD_DIM + 1, :]
                parts.append(acc_ref[h, :HEAD_DIM, :] / total)
                lses.append(top_ref[h] + jnp.log2(total))
            parts.append(jnp.zeros((256 - GROUP * HEAD_DIM, tokens), F32))
            out_ref[:, g * 256 : (g + 1) * 256] = jnp.concatenate(parts, axis=0).T
        lses.append(jnp.zeros((128 - HEADS, tokens), F32))
        lse_ref[...] = jnp.concatenate(lses, axis=0).T


def whole(*shape):
    return pl.BlockSpec(shape, lambda *_: (0,) * len(shape), pipeline_mode=pl.Buffered(1))


def attention_forward(own, blocks, slots, valid, weights, tables, features):
    tokens, width = own.shape
    steps = slots.shape[0]
    key_features, query_features = features
    wq, wk, wv = weights
    return pl.pallas_call(
        forward_kernel,
        out_shape=(
            jax.ShapeDtypeStruct((tokens, GROUPS * 256), F32),
            jax.ShapeDtypeStruct((tokens, 128), F32),
            jax.ShapeDtypeStruct((steps, GROUPS, tokens, 256), BF16),
        ),
        grid_spec=pltpu.PrefetchScalarGridSpec(
            num_scalar_prefetch=2,
            grid=(steps,),
            in_specs=[
                whole(tokens, width),
                pl.BlockSpec((1, tokens, width), lambda t, slot, valid: (slot[t], 0, 0)),
                whole(*wq.shape),
                whole(*wk.shape),
                whole(*wv.shape),
                whole(tokens, 128),
                whole(tokens, 128),
                whole(*tables[2].shape),
                whole(*tables[3].shape),
                pl.BlockSpec((1, tokens, 128), lambda t, slot, valid: (t, 0, 0)),
                whole(tokens, 128),
            ],
            out_specs=[
                whole(tokens, GROUPS * 256),
                whole(tokens, 128),
                pl.BlockSpec((1, GROUPS, tokens, 256), lambda t, slot, valid: (t, 0, 0, 0)),
            ],
            scratch_shapes=[
                pltpu.VMEM((HEADS, tokens, 256), BF16),
                pltpu.VMEM((HEADS, VROWS, tokens), BF16),
                pltpu.VMEM((HEADS, VROWS, tokens), F32),
                pltpu.VMEM((HEADS, 1, tokens), F32),
            ],
        ),
        compiler_params=pltpu.CompilerParams(
            dimension_semantics=("arbitrary",), vmem_limit_bytes=VMEM_BIG
        ),
        cost_estimate=pl.CostEstimate(
            flops=70_000_000_000, bytes_accessed=10_000_000, transcendentals=0
        ),
        name="attention_forward",
    )(slots, valid, own, blocks, wq, wk, wv, *tables, key_features, query_features)


def split_bf16(column):
    high = column.astype(BF16).astype(F32)
    return high, column - high


def backward_kernel(
    slot_ref, valid_ref, own_ref, x_ref, wq_ref, wk_ref, wkt_ref, wv_ref, cr_ref, sr_ref, cb_ref,
    sb_ref, ct_ref, st_ref, kb_ref, qf_ref, go_ref, heads_ref, lse_ref, gx_ref, dq_ref, dwk_ref,
    dwv_ref, qb_ref, gm_ref, kt_ref, vb_ref, dqt_ref, dk_ref, dv_ref, gxa_ref, wka_ref,
    wva_ref,
):
    step = pl.program_id(0)
    tokens = own_ref.shape[0]

    @pl.when(step == 0)
    def _():
        cosine, sine = block_angles(0, cr_ref, sr_ref, cb_ref, sb_ref)
        features = qf_ref[...].astype(F32)

        def one_group(g, carry):
            first, second = rotate(nn(own_ref[...], wq_ref[g]), cosine, sine)
            lane = lax.broadcasted_iota(jnp.int32, (tokens, 128), 1)
            wide = lax.broadcasted_iota(jnp.int32, (tokens, 256), 1)
            lanes = pl.ds(pl.multiple_of(g * 256, 256), 256)
            grads = go_ref[:, lanes].astype(F32)
            products = grads * heads_ref[:, lanes]
            for hh in range(GROUP):
                h = g * GROUP + hh
                lse = jnp.sum(jnp.where(lane == h, lse_ref[...], 0.0), axis=1, keepdims=True)
                own = head_lanes((tokens, 256), hh * HEAD_DIM, HEAD_DIM)
                delta = jnp.sum(jnp.where(own, products, 0.0), axis=1, keepdims=True)
                lse_one, rest = split_bf16(lse)
                lse_two, lse_three = split_bf16(rest)
                mask = head_lanes((tokens, 128), hh * HALF, HALF)
                scale = LOG2E * HEAD_DIM**-0.5
                tile = jnp.where(mask, first * scale, features)
                tile = jnp.where(lane == LSE_LANE, -lse_one, tile)
                tile = jnp.where(lane == LSE_LANE + 1, -lse_two, tile)
                tile = jnp.where(lane == LSE_LANE + 2, -lse_three, tile)
                qb_ref[h, :, :128] = tile.astype(BF16)
                qb_ref[h, :, 128:] = jnp.where(mask, second * scale, 0.0).astype(BF16)
                delta_one, delta_two = split_bf16(delta)
                tile = jnp.where(own, grads, 0.0)
                tile = jnp.where(wide == DELTA_LANE, -delta_one, tile)
                tile = jnp.where(wide == DELTA_LANE + 1, -delta_two, tile)
                gm_ref[h] = tile.astype(BF16)
            return carry

        lax.fori_loop(0, GROUPS, one_group, 0)
        dqt_ref[...] = jnp.zeros_like(dqt_ref)
        wka_ref[...] = jnp.zeros_like(wka_ref)
        wva_ref[...] = jnp.zeros_like(wva_ref)

    @pl.when(valid_ref[step] > 0)
    def _():
        cosine, sine = block_angles(step, cr_ref, sr_ref, cb_ref, sb_ref)

        def keys(g, carry):
            values = nn(x_ref[0], wv_ref[g])
            wide = lax.broadcasted_iota(jnp.int32, values.shape, 1)
            ones = (wide == DELTA_LANE) | (wide == DELTA_LANE + 1)
            vb_ref[g] = jnp.where(ones, 1.0, values).astype(BF16)
            turned = nt(wkt_ref[g], x_ref[0])
            for hh in range(GROUP):
                upper = turned[hh * HEAD_DIM : hh * HEAD_DIM + HALF]
                lower = turned[hh * HEAD_DIM + HALF : (hh + 1) * HEAD_DIM]
                c_row, s_row = ct_ref[step], st_ref[step]
                kt_ref[g * GROUP + hh, :HALF] = (upper * c_row - lower * s_row).astype(BF16)
                kt_ref[g * GROUP + hh, HALF:] = (lower * c_row + upper * s_row).astype(BF16)
            return carry

        lax.fori_loop(0, GROUPS, keys, 0)

        def grads(causal):
            def one_group(g, carry):
                for hh in range(GROUP):
                    h = g * GROUP + hh
                    prob = jnp.exp2(nt(kb_ref[0, g], qb_ref[h]))
                    if causal:
                        key = lax.broadcasted_iota(jnp.int32, prob.shape, 0)
                        query = lax.broadcasted_iota(jnp.int32, prob.shape, 1)
                        prob = jnp.where(key <= query, prob, 0.0)
                    grad = (prob * nt(vb_ref[g], gm_ref[h])).astype(BF16)
                    prob = prob.astype(BF16)
                    value_part = nn(prob, gm_ref[h])
                    key_part = nn(grad, qb_ref[h])
                    if hh == 0:
                        dv_ref[...] = value_part
                        dk_ref[...] = key_part
                    else:
                        dv_ref[...] += value_part
                        dk_ref[...] += key_part
                    dqt_ref[h] += nn(kt_ref[h], grad)
                first, second = rotate(dk_ref[...] * LN2, cosine, -sine)
                pad = head_lanes((tokens, 128), 0, GROUP * HALF)
                key_rows = jnp.concatenate(
                    [jnp.where(pad, first, 0.0), jnp.where(pad, second, 0.0)], axis=1
                ).astype(BF16)
                keep = head_lanes((tokens, 256), 0, GROUP * HEAD_DIM)
                value_rows = jnp.where(keep, dv_ref[...], 0.0).astype(BF16)
                wka_ref[g] += tn(x_ref[0], key_rows)
                wva_ref[g] += tn(x_ref[0], value_rows)
                gxa_ref[...] += nt(key_rows, wk_ref[g]) + nt(value_rows, wv_ref[g])
                return carry

            gxa_ref[...] = jnp.zeros_like(gxa_ref)
            lax.fori_loop(0, GROUPS, one_group, 0)
            gx_ref[0] = gxa_ref[...].astype(BF16)

        @pl.when(step == 0)
        def _():
            grads(True)

        @pl.when(step > 0)
        def _():
            grads(False)

    @pl.when(step == pl.num_programs(0) - 1)
    def _():
        for h in range(HEADS):
            upper = dqt_ref[h, :HALF, :] * HEAD_DIM**-0.5
            lower = dqt_ref[h, HALF:, :] * HEAD_DIM**-0.5
            c_row, s_row = ct_ref[0], st_ref[0]
            dq_ref[h * HEAD_DIM : h * HEAD_DIM + HALF, :] = (
                upper * c_row + lower * s_row
            ).astype(BF16)
            dq_ref[h * HEAD_DIM + HALF : (h + 1) * HEAD_DIM, :] = (
                lower * c_row - upper * s_row
            ).astype(BF16)
        dwk_ref[...] = wka_ref[...].astype(BF16)
        dwv_ref[...] = wva_ref[...].astype(BF16)


def attention_backward(
    own, blocks, slots, valid, weights, tables, turned, keys, query_features, grad_heads, heads, lse
):
    tokens, width = own.shape
    steps = slots.shape[0]
    wq, wk, wkt, wv = weights
    ct, st = turned
    return pl.pallas_call(
        backward_kernel,
        out_shape=(
            jax.ShapeDtypeStruct((SLOTS + 1, tokens, width), BF16),
            jax.ShapeDtypeStruct((width, tokens), BF16),
            jax.ShapeDtypeStruct(wk.shape, BF16),
            jax.ShapeDtypeStruct(wv.shape, BF16),
        ),
        grid_spec=pltpu.PrefetchScalarGridSpec(
            num_scalar_prefetch=2,
            grid=(steps,),
            in_specs=[
                whole(tokens, width),
                pl.BlockSpec((1, tokens, width), lambda t, slot, valid: (slot[t], 0, 0)),
                whole(*wq.shape),
                whole(*wk.shape),
                whole(*wkt.shape),
                whole(*wv.shape),
                whole(tokens, 128),
                whole(tokens, 128),
                whole(*tables[2].shape),
                whole(*tables[3].shape),
                whole(*ct.shape),
                whole(*st.shape),
                pl.BlockSpec((1, GROUPS, tokens, 256), lambda t, slot, valid: (t, 0, 0, 0)),
                whole(tokens, 128),
                whole(tokens, GROUPS * 256),
                whole(tokens, GROUPS * 256),
                whole(tokens, 128),
            ],
            out_specs=[
                pl.BlockSpec((1, tokens, width), lambda t, slot, valid: (slot[t], 0, 0)),
                whole(width, tokens),
                whole(*wk.shape),
                whole(*wv.shape),
            ],
            scratch_shapes=[
                pltpu.VMEM((HEADS, tokens, 256), BF16),
                pltpu.VMEM((HEADS, tokens, 256), BF16),
                pltpu.VMEM((HEADS, HEAD_DIM, tokens), BF16),
                pltpu.VMEM((GROUPS, tokens, 256), BF16),
                pltpu.VMEM((HEADS, HEAD_DIM, tokens), F32),
                pltpu.VMEM((tokens, 256), F32),
                pltpu.VMEM((tokens, 256), F32),
                pltpu.VMEM((tokens, width), F32),
                pltpu.VMEM(wk.shape, F32),
                pltpu.VMEM(wv.shape, F32),
            ],
        ),
        compiler_params=pltpu.CompilerParams(
            dimension_semantics=("arbitrary",), vmem_limit_bytes=VMEM_BIG
        ),
        cost_estimate=pl.CostEstimate(
            flops=120_000_000_000, bytes_accessed=20_000_000, transcendentals=0
        ),
        name="attention_backward",
    )(
        slots, valid, own, blocks, wq, wk, wkt, wv, *tables, ct, st, keys,
        query_features, grad_heads, heads, lse,
    )


def rotary_groups(weight):
    rows = weight.shape[0]
    split = weight.reshape(rows, GROUPS, GROUP, 2, HALF).transpose(1, 0, 3, 2, 4)
    split = split.reshape(GROUPS, rows, 2, GROUP * HALF)
    split = jnp.pad(split, ((0, 0), (0, 0), (0, 0), (0, 128 - GROUP * HALF)))
    return split.reshape(GROUPS, rows, 256)


def from_rotary_groups(grouped):
    rows = grouped.shape[1]
    split = grouped.reshape(GROUPS, rows, 2, 128)[..., : GROUP * HALF]
    split = split.reshape(GROUPS, rows, 2, GROUP, HALF).transpose(1, 0, 3, 2, 4)
    return split.reshape(rows, HEADS * HEAD_DIM)


def value_groups(weight):
    rows = weight.shape[0]
    split = weight.reshape(rows, GROUPS, GROUP * HEAD_DIM).transpose(1, 0, 2)
    return jnp.pad(split, ((0, 0), (0, 0), (0, 256 - GROUP * HEAD_DIM)))


def from_value_groups(grouped):
    rows = grouped.shape[1]
    return grouped[..., : GROUP * HEAD_DIM].transpose(1, 0, 2).reshape(rows, HEADS * HEAD_DIM)


def padded_rows(weight):
    split = weight.reshape(GROUPS, GROUP * HEAD_DIM, weight.shape[1])
    split = jnp.pad(split, ((0, 0), (0, 256 - GROUP * HEAD_DIM), (0, 0)))
    return split.reshape(GROUPS * 256, weight.shape[1])


def from_padded_rows(grouped):
    split = grouped.reshape(GROUPS, 256, grouped.shape[1])[:, : GROUP * HEAD_DIM]
    return split.reshape(HEADS * HEAD_DIM, grouped.shape[1])


TILE = 256


def rows_each(own, seq_count):
    return -(-own // (8 * seq_count)) * 8


def pieces(grouped, seq_count, shard_count):
    groups, rows, _ = grouped.shape
    own = rows // shard_count
    each = rows_each(own, seq_count)
    block = grouped.astype(BF16).reshape(groups, shard_count, own, TILE)
    block = jnp.pad(block, ((0, 0), (0, 0), (0, seq_count * each - own), (0, 0)))
    block = block.reshape(groups, shard_count, seq_count, each, TILE).transpose(2, 1, 0, 3, 4)
    return block.reshape(seq_count, shard_count, groups * each, TILE)


def columns(grad):
    return grad.reshape(grad.shape[0], -1, TILE).transpose(1, 0, 2)


def from_columns(grouped):
    return grouped.transpose(1, 0, 2).reshape(grouped.shape[1], -1)


def sum_pieces(block):
    seq_count, shard_count, rows, _ = block.shape
    flat = block.reshape(seq_count * shard_count * rows, TILE)
    return lax.psum_scatter(flat, ("seq", "shard"), scatter_dimension=0, tiled=True)


def take_pieces(share, sizes, seq_count):
    share = share.reshape(seq_count, -1, TILE)
    start, taken = 0, []
    for groups, own in sizes:
        each = rows_each(own, seq_count)
        part = share[:, start : start + groups * each].reshape(seq_count, groups, each, TILE)
        part = part.transpose(1, 0, 2, 3).reshape(groups, seq_count * each, TILE)[:, :own]
        taken.append(part.astype(F32))
        start += groups * each
    return taken


def shards(
    x_embed,
    doc_ids,
    owners,
    row_ids,
    table,
    ngram_weight,
    stream_gain,
    query_weight,
    key_weight,
    value_weight,
    out_weight,
    mixer_gain,
    gate_weight,
    up_weight,
    down_weight,
    feed_gain,
    cotangent,
):
    tokens = x_embed.shape[1]
    seq_count = lax.axis_size("seq")
    shard_count = lax.axis_size("shard")
    owner_count = seq_count * shard_count
    capacity = max(2, 4 * tokens // owner_count)
    score_scale = HEAD_DIM ** (-0.5)
    gathered = (
        lax.all_gather(query_weight, "shard", axis=0, tiled=True),
        lax.all_gather(key_weight, "shard", axis=0, tiled=True),
        lax.all_gather(value_weight, "shard", axis=0, tiled=True),
        lax.all_gather(out_weight, "shard", axis=0, tiled=True),
        lax.all_gather(gate_weight, "shard", axis=0, tiled=True),
        lax.all_gather(up_weight, "shard", axis=0, tiled=True),
        lax.all_gather(down_weight, "shard", axis=0, tiled=True),
    )
    (
        full_query,
        full_key,
        full_value,
        full_out,
        full_gate,
        full_up,
        full_down,
    ) = gathered
    ngram_rows, width = ngram_weight.shape
    share_width = stream_gain.shape[0]
    own_gains = jnp.pad(
        jnp.stack([stream_gain, mixer_gain, feed_gain]),
        ((0, -(ngram_rows + 3) % 16 + 0), (0, width - share_width)),
    )
    small = lax.all_gather(
        jnp.concatenate([ngram_weight, own_gains], axis=0), "shard", axis=0, tiled=True
    ).reshape(shard_count, -1, width)
    full_ngram = small[:, :ngram_rows].reshape(shard_count * ngram_rows, width)
    full_gains = small[:, ngram_rows : ngram_rows + 3, :share_width].astype(F32)
    gain_stream, gain_mixer, gain_feed = (
        full_gains[:, which].reshape(shard_count * share_width) for which in range(3)
    )
    flat_owner = owners.reshape(-1)
    flat_row = row_ids.reshape(-1)
    request_count = flat_owner.shape[0]
    one_hot = (flat_owner[:, None] == jnp.arange(owner_count, dtype=jnp.int32)[None, :]).astype(
        jnp.bfloat16
    )
    earlier = (jnp.arange(request_count)[:, None] > jnp.arange(request_count)[None, :]).astype(
        jnp.bfloat16
    )
    before = jnp.dot(earlier, one_hot, preferred_element_type=jnp.float32)
    rank_index = jnp.sum(before * one_hot, axis=1).astype(jnp.int32)
    slot_index = flat_owner * capacity + rank_index
    request = jnp.full((owner_count * capacity,), -1, jnp.int32).at[slot_index].set(flat_row)
    doc_rows = -(-tokens // 128)
    slab = jnp.concatenate(
        [
            jnp.pad(request.reshape(owner_count, 1, capacity), ((0, 0), (0, 0), (0, 128 - capacity))),
            jnp.broadcast_to(doc_ids.reshape(1, doc_rows, 128), (owner_count, doc_rows, 128)),
        ],
        axis=1,
    )
    (slabs,) = exchange((slab,), (False,), 3, "ask")
    asked_rows = slabs[:, 0, :capacity]
    docs_of = slabs[:, 1:].reshape(seq_count, shard_count, tokens)
    all_docs = lax.dynamic_index_in_dim(docs_of, lax.axis_index("shard"), 1, keepdims=False)
    present = asked_rows >= 0
    found_rows = jnp.take(table, jnp.maximum(asked_rows, 0).reshape(-1), axis=0)
    found_rows = jnp.where(present.reshape(-1)[:, None], found_rows, jnp.zeros_like(found_rows))
    (answer,) = exchange((found_rows.reshape(owner_count, capacity, -1),), (False,), 4, "answer")
    picked = jnp.take(answer.reshape(owner_count * capacity, -1), slot_index, axis=0).reshape(
        tokens, -1
    )
    inputs = x_embed[0].astype(jnp.float32)
    embedded = jnp.dot(picked, full_ngram, preferred_element_type=jnp.float32)
    stream = inputs + embedded
    residual, unit_zero, inverse_zero = norm_parts(stream, gain_stream)
    normed_one, unit_one, inverse_one = norm_parts(residual, gain_mixer)
    mixer_in = normed_one.astype(jnp.bfloat16)
    my_index = lax.axis_index("seq")
    reach_count = min((min(DOC_MAX, tokens * seq_count) + tokens - 2) // tokens, seq_count - 1)
    steps = reach_count + 1
    sources = my_index - jnp.arange(steps, dtype=jnp.int32)
    valid = (sources >= 0).astype(jnp.int32)
    levels = my_index // 4 - sources // 4
    slots = jnp.where(sources >= 0, levels * 4 + sources % 4, SLOTS)
    step_docs = jnp.take(all_docs, jnp.maximum(sources, 0), axis=0)
    lane = jnp.arange(128, dtype=jnp.int32)
    doc_lane = (lane >= DOC_LANE) & (lane < DOC_LANE + DOC_FEATURES)
    lse_lane = (lane >= LSE_LANE) & (lane < LSE_LANE + 3)
    same = step_docs[:, :, None] == (lane - DOC_LANE)[None, None, :]
    key_features = ((same & doc_lane) | lse_lane).astype(BF16)
    same_own = doc_ids[0][:, None] == (lane - DOC_LANE)[None, :]
    query_features = jnp.where(doc_lane & ~same_own, -FAR, 0.0).astype(BF16)
    theta, lane_theta, cos_row, sin_row = lane_tables(tokens)
    starts = (sources * tokens).astype(F32)
    block_rows = jnp.pad(starts, (0, 16 - steps))[:, None] * lane_theta[None, :]
    tables = (cos_row, sin_row, jnp.cos(block_rows), jnp.sin(block_rows))
    turned_block = starts[:, None, None] * theta[None, :, None]
    cos_block, sin_block = jnp.cos(turned_block), jnp.sin(turned_block)
    turned_row = theta[:, None] * jnp.arange(tokens, dtype=F32)[None, :]
    cos_turn, sin_turn = jnp.cos(turned_row)[None], jnp.sin(turned_row)[None]
    turned = (
        cos_block * cos_turn - sin_block * sin_turn,
        sin_block * cos_turn + cos_block * sin_turn,
    )
    features = (key_features, query_features)
    query_groups = rotary_groups(full_query)
    key_groups = rotary_groups(full_key)
    value_turned = jnp.pad(
        full_value.T.reshape(HEADS, HEAD_DIM, -1), ((0, 0), (0, VROWS - HEAD_DIM), (0, 0))
    ).reshape(GROUPS, GROUP * VROWS, -1)
    key_turned = full_key.T.reshape(GROUPS, GROUP * HEAD_DIM, -1)
    value_grouped = value_groups(full_value)
    out_rows = padded_rows(full_out)
    blocks = halo_gather(mixer_in, seq_count // 4)
    mixed_full, log_sum, keys = attention_forward(
        mixer_in, blocks, slots, valid, (query_groups, key_groups, value_turned), tables, features
    )
    heads_low = mixed_full.astype(BF16)
    mixer_out = jnp.dot(heads_low, out_rows, preferred_element_type=jnp.float32)
    middle = residual + mixer_out
    normed_two, unit_two, inverse_two = norm_parts(middle, gain_feed)
    feed_in = normed_two.astype(jnp.bfloat16)
    gate_rows = jnp.dot(feed_in, full_gate, preferred_element_type=jnp.float32)
    up_rows = jnp.dot(feed_in, full_up, preferred_element_type=jnp.float32)
    sigmoid = jax.nn.sigmoid(gate_rows)
    hidden = (gate_rows * sigmoid * up_rows).astype(jnp.bfloat16)
    feed_out = jnp.dot(hidden, full_down, preferred_element_type=jnp.float32)
    result = middle + feed_out
    mixed = result.astype(jnp.bfloat16)[None]
    energy = jnp.stack(
        [jnp.sum(stream * stream), jnp.sum(mixer_out * mixer_out), jnp.sum(feed_out * feed_out)]
    )
    energy = jnp.broadcast_to(jnp.pad(energy, (0, 5))[:, None], (8, 128))
    grad_result = cotangent[0].astype(jnp.float32)
    grad_feed = cotangent[0]
    grad_down = jnp.einsum("tf,td->fd", hidden, grad_feed, preferred_element_type=jnp.float32)
    grad_hidden = jnp.einsum("td,fd->tf", grad_feed, full_down, preferred_element_type=jnp.float32)
    grad_gate_rows = (grad_hidden * up_rows * sigmoid * (1.0 + gate_rows * (1.0 - sigmoid))).astype(
        jnp.bfloat16
    )
    grad_up_rows = (grad_hidden * gate_rows * sigmoid).astype(jnp.bfloat16)
    grad_gate = jnp.einsum("td,tf->df", feed_in, grad_gate_rows, preferred_element_type=jnp.float32)
    grad_up = jnp.einsum("td,tf->df", feed_in, grad_up_rows, preferred_element_type=jnp.float32)
    grad_feed_in = jnp.einsum(
        "tf,df->td", grad_gate_rows, full_gate, preferred_element_type=jnp.float32
    ) + jnp.einsum("tf,df->td", grad_up_rows, full_up, preferred_element_type=jnp.float32)
    back_two, grad_feed_gain = norm_back(grad_feed_in, unit_two, inverse_two, gain_feed)
    grad_middle = grad_result + back_two
    grad_mixer = grad_middle.astype(jnp.bfloat16)
    grad_out = from_padded_rows(
        jnp.einsum("te,td->ed", heads_low, grad_mixer, preferred_element_type=jnp.float32)
    )
    grad_heads = jnp.einsum(
        "td,ed->te", grad_mixer, out_rows, preferred_element_type=jnp.float32
    ).astype(jnp.bfloat16)
    early = jnp.concatenate(
        [
            pieces(columns(grad.astype(BF16)), seq_count, shard_count)
            for grad in (grad_gate, grad_up, grad_down, grad_out)
        ],
        axis=2,
    )
    grad_heads, early = lax.optimization_barrier((grad_heads, early))
    early_part = sum_pieces(early)
    parts, grad_query_turned, grad_key_groups, grad_value_groups = attention_backward(
        mixer_in,
        blocks,
        slots,
        valid,
        (query_groups, key_groups, key_turned, value_grouped),
        tables,
        turned,
        keys,
        query_features,
        grad_heads,
        mixed_full,
        log_sum,
    )
    grad_query = jnp.einsum(
        "td,et->de", mixer_in, grad_query_turned, preferred_element_type=jnp.float32
    )
    late = jnp.concatenate(
        [
            pieces(grouped, seq_count, shard_count)
            for grouped in (columns(grad_query.astype(BF16)), grad_key_groups, grad_value_groups)
        ],
        axis=2,
    )
    parts, late, early_part = lax.optimization_barrier((parts, late, early_part))
    early_share = lax.all_gather(early_part, "seq", axis=0, tiled=True)
    reduced = halo_reduce(parts, seq_count // 4)
    grad_mixer_in = reduced + jnp.einsum(
        "et,de->td", grad_query_turned, full_query, preferred_element_type=jnp.float32
    )
    back_one, grad_mixer_gain = norm_back(grad_mixer_in, unit_one, inverse_one, gain_mixer)
    grad_residual = grad_middle + back_one
    back_zero, grad_stream_gain = norm_back(grad_residual, unit_zero, inverse_zero, gain_stream)
    grad_input = back_zero[None]
    grad_embed = back_zero.astype(jnp.bfloat16)
    grad_ngram = jnp.einsum("ti,to->io", picked, grad_embed, preferred_element_type=jnp.float32)
    grad_picked = (
        jnp.einsum("to,io->ti", grad_embed, full_ngram, preferred_element_type=jnp.float32)
        .astype(jnp.bfloat16)
        .reshape(request_count, -1)
    )
    outgoing = (
        jnp.zeros((owner_count * capacity, grad_picked.shape[1]), jnp.bfloat16)
        .at[slot_index]
        .set(grad_picked)
    )
    each = -(-ngram_rows // seq_count)
    ngram_pieces = jnp.pad(
        grad_ngram.reshape(shard_count, ngram_rows, width),
        ((0, 0), (0, seq_count * each - ngram_rows), (0, 0)),
    )
    ngram_pieces = ngram_pieces.reshape(shard_count, seq_count, each, width)
    gain_rows = jnp.stack([grad_stream_gain, grad_mixer_gain, grad_feed_gain])
    gain_rows = gain_rows.reshape(3, shard_count, share_width).transpose(1, 0, 2)
    gain_rows = jnp.pad(gain_rows, ((0, 0), (0, -(each + 3) % 16), (0, width - share_width)))
    gain_rows = jnp.broadcast_to(
        gain_rows[:, None], (shard_count, seq_count) + gain_rows.shape[1:]
    )
    small_rows = jnp.concatenate([ngram_pieces, gain_rows], axis=2).astype(BF16)
    small_rows = small_rows.transpose(1, 0, 2, 3).reshape(owner_count, -1, width)
    outgoing, late, early_share = lax.optimization_barrier((outgoing, late, early_share))
    late_part = sum_pieces(late)
    incoming, small_parts, energy_parts = exchange(
        (outgoing.reshape(owner_count, capacity, -1), small_rows, energy),
        (False, False, True),
        5,
        "give_back",
    )
    small_sum = jnp.sum(small_parts.astype(F32), axis=0)
    total_gains = small_sum[each : each + 3, :share_width]
    (ngram_share,) = exchange((small_sum.astype(BF16),), (True,), 6, "spread", along_seq=True)
    energies = jnp.sum(energy_parts[:, :, 0], axis=0)
    entry_count = owner_count * tokens * stream.shape[1]
    stream_rms = jnp.sqrt(energies[0] / entry_count)
    mixer_rms = jnp.sqrt(energies[1] / entry_count)
    feed_rms = jnp.sqrt(energies[2] / entry_count)
    incoming = (
        jnp.where(present[..., None], incoming, jnp.zeros_like(incoming))
        .reshape(owner_count * capacity, -1)
        .astype(jnp.float32)
    )
    grad_table = (
        jnp.zeros(table.shape, jnp.float32).at[jnp.maximum(asked_rows, 0).reshape(-1)].add(incoming)
    )
    grad_table, ngram_share, late_part = lax.optimization_barrier(
        (grad_table, ngram_share, late_part)
    )
    late_share = lax.all_gather(late_part, "seq", axis=0, tiled=True)
    total_ngram = ngram_share[:, :each].reshape(seq_count * each, width)[:ngram_rows].astype(F32)
    wide = share_width
    total_gate, total_up, total_down, total_out = (
        from_columns(total)
        for total in take_pieces(
            early_share,
            (
                (gate_weight.shape[1] // TILE, wide),
                (up_weight.shape[1] // TILE, wide),
                (width // TILE, down_weight.shape[0]),
                (width // TILE, wide),
            ),
            seq_count,
        )
    )
    total_query, total_key, total_value = take_pieces(
        late_share, ((width // TILE, wide), (GROUPS, wide), (GROUPS, wide)), seq_count
    )
    return (
        mixed,
        grad_input,
        stream_rms,
        mixer_rms,
        feed_rms,
        grad_table,
        total_ngram,
        total_gains[0],
        from_columns(total_query),
        from_rotary_groups(total_key),
        from_value_groups(total_value),
        total_out,
        total_gains[1],
        total_gate,
        total_up,
        total_down,
        total_gains[2],
    )


def solution(mesh):
    return jax.shard_map(
        shards,
        mesh=mesh,
        in_specs=(
            P("shard", "seq", None),
            P("shard", "seq"),
            P("shard", "seq", None),
            P("shard", "seq", None),
            P(("seq", "shard"), None),
            P("shard", None),
            P("shard"),
            P("shard", None),
            P("shard", None),
            P("shard", None),
            P("shard", None),
            P("shard"),
            P("shard", None),
            P("shard", None),
            P("shard", None),
            P("shard"),
            P("shard", "seq", None),
        ),
        out_specs=(
            P("shard", "seq", None),
            P("shard", "seq", None),
            P(),
            P(),
            P(),
            P(("seq", "shard"), None),
            P("shard", None),
            P("shard"),
            P("shard", None),
            P("shard", None),
            P("shard", None),
            P("shard", None),
            P("shard"),
            P("shard", None),
            P("shard", None),
            P("shard", None),
            P("shard"),
        ),
        check_vma=False,
    )
```
